128 devices in a mesh: grid: 32 (over x, y, core), sub: 4 (over z).
Axes of the slice: x: 4, y: 4, z: 4, core: 2. Of those that a mesh axis runs over, the one named last changes fastest.
Arguments:
- grid_x: bfloat16 [262144, 512], P(('grid', 'sub')), may hold values from -6 to 6
- mesh_h: bfloat16 [8192, 512], P(('grid', 'sub')), may hold values from -6 to 6
- gain_grid: float32 [512], replicated, may hold values from 0.1 to 1.9
- gain_mesh: float32 [512], replicated, may hold values from 0.1 to 1.9
- w_query: bfloat16 [512, 512], replicated, may hold values from -0.25 to 0.25
- w_key: bfloat16 [512, 512], replicated, may hold values from -0.25 to 0.25
- w_value: bfloat16 [512, 512], replicated, may hold values from -0.25 to 0.25
- w_out: bfloat16 [512, 512], replicated, may hold values from -0.25 to 0.25
- edge_bias: float32 [8192, 384], P(('grid', 'sub')), may hold values from -9 to 300
- neighbours: int32 [8192, 96], P(('grid', 'sub')), may hold values from 0 to 767, as said below
- valid: int32 [8192, 96], P(('grid', 'sub')), may hold values from 0 to 1, as said below
- send_rows: int32 [128, 3, 4, 64], P(('grid', 'sub')), may hold values from 0 to 2047, as said below
- out_grad: bfloat16 [8192, 512], P(('grid', 'sub')), may hold values from -24 to 24
Outputs:
- mesh_out: bfloat16 [8192, 512], P(('grid', 'sub'))
- mesh_grad: bfloat16 [8192, 512], P(('grid', 'sub'))
- grid_grad: bfloat16 [262144, 512], P(('grid', 'sub'))
- weight_grads: float32 [4, 512, 512], replicated
The draws below stay inside these ranges and needn't reach their ends.
Inputs may be any that keep to these rules, and one draw needn't show every extreme that they name: `send_rows`: for each source device, slab offset and destination sub index the 64 local rows are distinct; rows sent to the slab below (o = 0) lie in the lower half of the device's 2048 rows, rows sent to the slab above (o = 2) in the upper half. `neighbours`: a slot (o * 4 + s) * 64 + t names row t of what device s of slab g - o + 1 sends to the node's device; slots of slabs outside the grid are never named; the 96 entries of a node are distinct; some slots are named by no node. The first two edges of every node are valid.
All inputs are finite; a program needn't handle non-finite values.
Results may differ from the reference program's by a relative error of at most 0.009.
Values may be sent and summed in bfloat16 or wider, within the bound.
No kernel may reach another device: no remote copies, remote signals or barrier semaphores. Data moves between devices by JAX's collectives and lax.ppermute only.
A program may use at most 128 MiB of HBM per device.

```python
import jax
import jax.numpy as jnp
from jax import lax

FEATURE_WIDTH = 512
HEADS = 4
GRID_NEIGHBOURS = 96
G_DEV = 2048
MESH_PER_SHARD = 64
RANKS = 128
CAP = 64
SLOTS = 768
HEAD_DIM = 128
GRID = 262144
MESH = 8192
N_GRID = 32
N_SUB = 4


def pair_counts(key):
    count_key = jax.random.fold_in(key, 11)
    lowest = max(2, CAP // 2)
    counts = jax.random.randint(count_key, (RANKS, 3, N_SUB), lowest, CAP + 1)
    rank_ids = jnp.arange(RANKS)[:, None, None]
    offsets = jnp.arange(3)[None, :, None]
    subs = jnp.arange(N_SUB)[None, None, :]
    slab = rank_ids // N_SUB
    own_sub = rank_ids % N_SUB
    counts = jnp.where((offsets == 1) & (subs == own_sub), CAP, counts)
    source_slab = slab - offsets + 1
    inside = (source_slab >= 0) & (source_slab < N_GRID)
    return jnp.where(inside, counts, 0)


def draw_send_rows(key, part):
    subkeys = jax.random.split(jax.random.fold_in(key, 23), RANKS * 3 * N_SUB)
    half_rows = jax.vmap(lambda subkey: jax.random.permutation(subkey, G_DEV // 2)[:CAP])(subkeys)
    full_rows = jax.vmap(lambda subkey: jax.random.permutation(jax.random.fold_in(subkey, 5), G_DEV)[:CAP])(subkeys)
    half_rows = half_rows.reshape(RANKS, 3, N_SUB, CAP)
    full_rows = full_rows.reshape(RANKS, 3, N_SUB, CAP)
    offsets = jnp.arange(3)[None, :, None, None]
    picked = jnp.where(offsets == 0, half_rows, jnp.where(offsets == 2, half_rows + G_DEV // 2, full_rows))
    return picked.astype(jnp.int32)


def draw_neighbours(key, part):
    counts = pair_counts(key)
    slot_iota = jnp.arange(SLOTS)
    offset_of = slot_iota // (N_SUB * CAP)
    sub_of = slot_iota // CAP % N_SUB
    within = slot_iota % CAP
    owner = jnp.arange(MESH) // MESH_PER_SHARD
    limit = counts[owner[:, None], offset_of[None, :], sub_of[None, :]]
    used = within[None, :] < limit
    top_value = (1 << 30) // SLOTS
    noise = jax.random.randint(jax.random.fold_in(key, 37), (MESH, SLOTS), 0, top_value)
    ranked = jnp.where(used, noise * SLOTS + slot_iota[None, :], -1)
    chosen = lax.top_k(ranked, GRID_NEIGHBOURS)[1]
    return chosen.astype(jnp.int32)


def draw_valid(key, part):
    levels = jax.random.randint(jax.random.fold_in(key, 41), (MESH, GRID_NEIGHBOURS), 0, 5)
    column = jnp.arange(GRID_NEIGHBOURS)[None, :]
    return jnp.where((levels > 0) | (column < 2), 1, 0).astype(jnp.int32)


def draw_edge_bias(key, part):
    normal_key = jax.random.fold_in(jax.random.fold_in(key, 53), 0)
    base = jax.random.normal(normal_key, (MESH, HEADS, GRID_NEIGHBOURS), jnp.float32)
    base = jnp.clip(base, -4.0, 4.0)
    return base.reshape(MESH, HEADS * GRID_NEIGHBOURS).astype(jnp.float32)


def steps_of(rng, dims, cuts, least, high):
    loudness = 1.0
    for axis_at, shards_of in cuts:
        draws = jax.random.uniform(jax.random.fold_in(jax.random.fold_in(rng, 6), axis_at), (shards_of,), jnp.float32, least / len(cuts), high / len(cuts))
        loudness = loudness * jnp.repeat(jnp.exp(draws), dims[axis_at] // shards_of).reshape((-1,) + (1,) * (len(dims) - 1 - axis_at))
    return loudness


def scatter_about(stream_key, extent, deviation, bound, cuts=(), kind=jnp.bfloat16):
    values = deviation * jax.random.normal(stream_key, extent, jnp.float32)
    if cuts:
        values = values * steps_of(stream_key, extent, cuts, -0.22, 0.18)
    return jnp.clip(values, -bound, bound).astype(kind)


def setup_inputs(seed: int = 0) -> dict:
    streams_of = jax.random.split(jax.random.key(seed), 14)
    return {
        "grid_x": scatter_about(streams_of[0], (GRID, FEATURE_WIDTH), 1.0, 6.0, ((0, 128),)),
        "mesh_h": scatter_about(streams_of[1], (MESH, FEATURE_WIDTH), 1.0, 6.0, ((0, 128),)),
        "gain_grid": jnp.clip(1.0 + 0.18 * jax.random.normal(streams_of[2], (FEATURE_WIDTH,), jnp.float32), 0.1, 1.9),
        "gain_mesh": jnp.clip(1.0 + 0.18 * jax.random.normal(streams_of[3], (FEATURE_WIDTH,), jnp.float32), 0.1, 1.9),
        "w_query": scatter_about(streams_of[4], (FEATURE_WIDTH, FEATURE_WIDTH), FEATURE_WIDTH ** -0.5, 0.25),
        "w_key": scatter_about(streams_of[5], (FEATURE_WIDTH, FEATURE_WIDTH), FEATURE_WIDTH ** -0.5, 0.25),
        "w_value": scatter_about(streams_of[6], (FEATURE_WIDTH, FEATURE_WIDTH), FEATURE_WIDTH ** -0.5, 0.25),
        "w_out": scatter_about(streams_of[7], (FEATURE_WIDTH, FEATURE_WIDTH), FEATURE_WIDTH ** -0.5, 0.25),
        "edge_bias": draw_edge_bias(jax.random.fold_in(streams_of[13], 71), 0),
        "neighbours": draw_neighbours(jax.random.fold_in(streams_of[13], 71), 0),
        "valid": draw_valid(jax.random.fold_in(streams_of[13], 71), 0),
        "send_rows": draw_send_rows(jax.random.fold_in(streams_of[13], 71), 0),
        "out_grad": scatter_about(streams_of[12], (MESH, FEATURE_WIDTH), 4.0, 24.0, ((0, 128),)),
    }


EPSILON = 1e-06
NEG_FILL = -1e+30

def normalize(values_in, gain_row):
    widened = values_in.astype(jnp.float32)
    factor = lax.rsqrt(lax.optimization_barrier(jnp.mean(widened * widened, axis=-1, keepdims=True)) + EPSILON)
    return (widened, factor, (widened * factor * gain_row).astype(jnp.bfloat16))

def normalize_back(widened, factor, gain_row, upstream):
    scaled = gain_row * upstream
    inner_mean = lax.optimization_barrier(jnp.mean(widened * scaled, axis=-1, keepdims=True))
    return factor * scaled - widened * factor ** 3 * inner_mean

def reference(grid_x, mesh_h, gain_grid, gain_mesh, w_query, w_key, w_value, w_out, edge_bias, neighbours, valid, send_rows, out_grad):
    logit_scale = HEAD_DIM ** (-0.5)
    grid_wide, grid_factor, grid_normed = normalize(grid_x, gain_grid)
    keys = jnp.dot(grid_normed, w_key, preferred_element_type=jnp.float32).astype(jnp.bfloat16)
    values = jnp.dot(grid_normed, w_value, preferred_element_type=jnp.float32).astype(jnp.bfloat16)
    mesh_wide, mesh_factor, mesh_normed = normalize(mesh_h, gain_mesh)
    queries = (jnp.dot(mesh_normed, w_query, preferred_element_type=jnp.float32) * logit_scale).astype(jnp.bfloat16)
    offsets = jnp.arange(3, dtype=jnp.int32)[:, None]
    subs = jnp.arange(N_SUB, dtype=jnp.int32)[None, :]

    def per_device(state_pair, rank_id):
        grid_acc, grad_acc = state_pair
        slab = (rank_id // N_SUB).astype(jnp.int32)
        own_sub = (rank_id % N_SUB).astype(jnp.int32)
        src_slab = jnp.clip(slab - offsets + 1, 0, N_GRID - 1).astype(jnp.int32)
        src_rank = (src_slab * N_SUB + subs).astype(jnp.int32)
        rows = send_rows[src_rank, jnp.broadcast_to(offsets, (3, N_SUB)), own_sub]
        point_ids = (src_rank[:, :, None] * G_DEV + rows).reshape(SLOTS).astype(jnp.int32)
        row_start = (rank_id * MESH_PER_SHARD).astype(jnp.int32)
        node_q = lax.dynamic_slice_in_dim(queries, row_start, MESH_PER_SHARD, 0)
        node_wide = lax.dynamic_slice_in_dim(mesh_wide, row_start, MESH_PER_SHARD, 0)
        node_factor = lax.dynamic_slice_in_dim(mesh_factor, row_start, MESH_PER_SHARD, 0)
        node_normed = lax.dynamic_slice_in_dim(mesh_normed, row_start, MESH_PER_SHARD, 0)
        node_grad = lax.dynamic_slice_in_dim(out_grad, row_start, MESH_PER_SHARD, 0)
        mesh_node_bias = lax.dynamic_slice_in_dim(edge_bias, row_start, MESH_PER_SHARD, 0).reshape(MESH_PER_SHARD, HEADS, GRID_NEIGHBOURS)
        node_nbr = lax.dynamic_slice_in_dim(neighbours, row_start, MESH_PER_SHARD, 0)
        node_valid = lax.dynamic_slice_in_dim(valid, row_start, MESH_PER_SHARD, 0)
        edge_points = point_ids[node_nbr]
        edge_key_rows = keys[edge_points].astype(jnp.float32).reshape(MESH_PER_SHARD, GRID_NEIGHBOURS, HEADS, HEAD_DIM)
        edge_value_rows = values[edge_points].astype(jnp.float32).reshape(MESH_PER_SHARD, GRID_NEIGHBOURS, HEADS, HEAD_DIM)
        query_head_rows = node_q.astype(jnp.float32).reshape(MESH_PER_SHARD, HEADS, HEAD_DIM)
        score_matrix = jnp.einsum('fog,flog->fol', query_head_rows, edge_key_rows) + mesh_node_bias
        live_mask = (node_valid == 1)[:, None, :]
        row_peak = lax.optimization_barrier(jnp.max(jnp.where(live_mask, score_matrix, NEG_FILL), axis=2, keepdims=True))
        exp_terms = jnp.exp(jnp.where(live_mask, score_matrix - row_peak, NEG_FILL))
        attn_probs = exp_terms / lax.optimization_barrier(jnp.sum(exp_terms, axis=2, keepdims=True))
        probabilities_batch = attn_probs.astype(jnp.bfloat16)
        attended_rows = jnp.einsum('bao,boai->bai', probabilities_batch.astype(jnp.float32), edge_value_rows).reshape(MESH_PER_SHARD, FEATURE_WIDTH).astype(jnp.bfloat16)
        out_rows = (node_wide + jnp.dot(attended_rows, w_out, preferred_element_type=jnp.float32)).astype(jnp.bfloat16)
        grad_wo = jnp.dot(attended_rows.T, node_grad, preferred_element_type=jnp.float32)
        att_grad = jnp.dot(node_grad, w_out.T, preferred_element_type=jnp.float32).astype(jnp.bfloat16)
        head_gradient = att_grad.astype(jnp.float32).reshape(MESH_PER_SHARD, HEADS, HEAD_DIM)
        probability_gradient = jnp.einsum('fog,flog->fol', head_gradient, edge_value_rows)
        score_gradient = (attn_probs * (probability_gradient - lax.optimization_barrier(jnp.sum(attn_probs * probability_gradient, axis=2, keepdims=True)))).astype(jnp.bfloat16)
        query_gradient = (jnp.einsum('bao,boai->bai', score_gradient.astype(jnp.float32), edge_key_rows) * logit_scale).reshape(MESH_PER_SHARD, FEATURE_WIDTH).astype(jnp.bfloat16)
        key_per_edge = jnp.einsum('iuw,iuy->iwuy', score_gradient.astype(jnp.float32), query_head_rows).reshape(MESH_PER_SHARD * GRID_NEIGHBOURS, FEATURE_WIDTH)
        value_per_edge = jnp.einsum('iuw,iuy->iwuy', probabilities_batch.astype(jnp.float32), head_gradient).reshape(MESH_PER_SHARD * GRID_NEIGHBOURS, FEATURE_WIDTH)
        slot_ids = node_nbr.reshape(MESH_PER_SHARD * GRID_NEIGHBOURS)
        key_part = jax.ops.segment_sum(key_per_edge, slot_ids, num_segments=SLOTS).astype(jnp.bfloat16)
        value_part = jax.ops.segment_sum(value_per_edge, slot_ids, num_segments=SLOTS).astype(jnp.bfloat16)
        sent_normed = grid_normed[point_ids]
        grad_wk = jnp.dot(sent_normed.T, key_part, preferred_element_type=jnp.float32)
        grad_wv = jnp.dot(sent_normed.T, value_part, preferred_element_type=jnp.float32)
        slot_back = jnp.dot(key_part, w_key.T, preferred_element_type=jnp.float32) + jnp.dot(value_part, w_value.T, preferred_element_type=jnp.float32)
        grid_acc = grid_acc.at[point_ids].add(slot_back)
        grad_wq = jnp.dot(node_normed.T, query_gradient, preferred_element_type=jnp.float32)
        normed_grad = jnp.dot(query_gradient, w_query.T, preferred_element_type=jnp.float32)
        grad_rows = (node_grad.astype(jnp.float32) + normalize_back(node_wide, node_factor, gain_mesh, normed_grad)).astype(jnp.bfloat16)
        grad_acc = grad_acc + jnp.stack([grad_wq, grad_wk, grad_wv, grad_wo])
        return ((grid_acc, grad_acc), (out_rows, grad_rows))
    initial = (jnp.zeros((GRID, FEATURE_WIDTH), jnp.float32), jnp.zeros((4, FEATURE_WIDTH, FEATURE_WIDTH), jnp.float32))
    (grid_acc, grad_acc), (out_rows, grad_rows) = lax.scan(per_device, initial, jnp.arange(RANKS, dtype=jnp.int32))
    grid_grad = normalize_back(grid_wide, grid_factor, gain_grid, grid_acc).astype(jnp.bfloat16)
    return (out_rows.reshape(MESH, FEATURE_WIDTH), grad_rows.reshape(MESH, FEATURE_WIDTH), grid_grad, grad_acc)
```

```python
import functools

import jax
import jax.numpy as jnp
from jax import lax
from jax.experimental import pallas as pl
from jax.experimental.pallas import tpu as pltpu
from jax.sharding import Mesh
from jax.sharding import PartitionSpec as P

SLAB = ("gx", "gy", "gc")
CHIPS = ("gx", "gy", "z")
ALL = ("gx", "gy", "gc", "z")

EPSILON = 1e-06
ABSENT = -1e30
F32 = jnp.float32
BF16 = jnp.bfloat16

VM = pl.BlockSpec(memory_space=pltpu.VMEM)
SM = pl.BlockSpec(memory_space=pltpu.SMEM)
ANY = pl.BlockSpec(memory_space=pl.ANY)


def nn(a, b):
    return lax.dot_general(a, b, (((1,), (0,)), ((), ())), preferred_element_type=F32)


def nt(a, b):
    return lax.dot_general(a, b, (((1,), (1,)), ((), ())), preferred_element_type=F32)


def tn(a, b):
    return lax.dot_general(a, b, (((0,), (0,)), ((), ())), preferred_element_type=F32)


def inv_rms(wide):
    return lax.rsqrt(jnp.mean(wide * wide, axis=-1, keepdims=True) + EPSILON)


def norm_back(wide, factor, gain_row, upstream):
    scaled = gain_row * upstream
    inner = jnp.mean(wide * scaled, axis=-1, keepdims=True)
    return factor * scaled - wide * (factor * factor * factor * inner)


def call(body, outs, in_specs, args, flops, nbytes, name, scratch=(), vmem=None):
    return pl.pallas_call(
        body,
        out_shape=outs,
        in_specs=in_specs,
        out_specs=[VM] * len(outs),
        scratch_shapes=list(scratch),
        compiler_params=pltpu.CompilerParams(vmem_limit_bytes=vmem or (40 << 20)),
        cost_estimate=pl.CostEstimate(flops=flops, bytes_accessed=nbytes, transcendentals=0),
        name=name,
    )(*args)


def gather_body(sub_ref, rows_ref, x_hbm, gain_ref, o0, o1, o2, o3, x_ref, sems):
    half = x_ref.shape[0] // 2
    cap = rows_ref.shape[3]
    outs = (o0, o1, o2, o3)
    copies = []
    for i in range(2):
        part = pl.ds(i * half, half)
        cp = pltpu.make_async_copy(x_hbm.at[part], x_ref.at[part], sems.at[i])
        cp.start()
        copies.append(cp)
    me = sub_ref[0]
    eye = lax.broadcasted_iota(jnp.int32, (cap, cap), 0) == lax.broadcasted_iota(
        jnp.int32, (cap, cap), 1
    )
    gain = gain_ref[...]
    for step, (o, first, count) in enumerate(((0, 0, half), (2, half, half), (1, 0, 2 * half))):
        cols = []
        for k in range(4):
            s = lax.rem(me + k, 4)
            row = rows_ref[0, o, pl.ds(s, 1), :].astype(F32)
            cols.append(jnp.sum(jnp.where(eye, row, 0.0), axis=1, keepdims=True))
        col = jnp.concatenate(cols, axis=0).astype(jnp.int32) - first
        lanes = lax.broadcasted_iota(jnp.int32, (4 * cap, count), 1)
        onehot = jnp.where(lanes == col, 1.0, 0.0).astype(BF16)
        if step < 2:
            copies[step].wait()
        wide = nn(onehot, x_ref[first : first + count, :])
        normed = (wide * inv_rms(wide) * gain).astype(BF16)
        for k in range(4):
            outs[k][o] = normed[k * cap : (k + 1) * cap]


def prep_body(mesh_ref, gain_ref, wq_ref, wo_ref, og_ref, nbr_ref, bias_ref,
              normed_ref, q_ref, ag_ref, dense_ref, inv_ref):
    heads, nodes, slots = dense_ref.shape
    wide = mesh_ref[...].astype(F32)
    normed = (wide * inv_rms(wide) * gain_ref[...]).astype(BF16)
    normed_ref[...] = normed
    q_ref[...] = (nn(normed, wq_ref[...]) * (128 ** -0.5)).astype(BF16)
    ag_ref[...] = nt(og_ref[...], wo_ref[...]).astype(BF16)
    groups, fan, per = nbr_ref.shape
    lanes = lax.broadcasted_iota(jnp.int32, (fan, slots), 1)
    edge = lax.broadcasted_iota(jnp.int32, (fan, slots), 0) + 1

    def group(g, carry):
        block = nbr_ref[g]
        found = []
        for i in range(per):
            hit = jnp.where(block[:, i : i + 1] == lanes, edge, 0)
            found.append(jnp.sum(hit, axis=0, keepdims=True))
        inv_ref[pl.ds(pl.multiple_of(g * per, per), per), :] = jnp.concatenate(found, axis=0)
        return carry

    lax.fori_loop(0, groups, group, 0)
    for b in range(slots // 128):
        at = inv_ref[:, b * 128 : (b + 1) * 128] - 1
        here = at >= 0
        at = jnp.maximum(at, 0)
        for h in range(heads):
            got = jnp.take_along_axis(bias_ref[h], at, axis=1, mode="promise_in_bounds")
            dense_ref[h, :, b * 128 : (b + 1) * 128] = jnp.where(here, got, ABSENT)


def middle_body(core_ref, a0, a2, b0, b1, b2, b3, wk_ref, wv_ref, q_ref, ag_ref, mn_ref, og_ref,
                bias_ref, keep_ref, send_ref, kp_ref, vp_ref, att_ref, qg_ref, rows, keys, vals):
    heads = bias_ref.shape[0]
    block = a0.shape[0]
    cap = b0.shape[1]
    rows[0:block] = a0[...]
    for k, piece in enumerate((b0, b1, b2, b3)):
        rows[block + k * cap : block + (k + 1) * cap] = piece[1]
    rows[2 * block : 3 * block] = a2[...]
    keys[...] = nn(rows[...], wk_ref[...]).astype(BF16)
    vals[...] = nn(rows[...], wv_ref[...]).astype(BF16)
    for h in range(heads):
        at = slice(h * 128, (h + 1) * 128)
        q, ag = q_ref[:, at], ag_ref[:, at]
        kh, vh = keys[:, at], vals[:, at]
        scores = nt(q, kh) + bias_ref[h]
        peak = jnp.max(scores, axis=1, keepdims=True)
        terms = jnp.exp(scores - peak)
        probs = terms / jnp.sum(terms, axis=1, keepdims=True)
        probs_b = probs.astype(BF16)
        att_ref[:, at] = nn(probs_b, vh).astype(BF16)
        pg = nt(ag, vh)
        sg = (probs * (pg - jnp.sum(probs * pg, axis=1, keepdims=True))).astype(BF16)
        qg_ref[:, at] = (nn(sg, kh) * (128 ** -0.5)).astype(BF16)
        kp_ref[:, at] = tn(sg, q).astype(BF16)
        vp_ref[:, at] = tn(probs_b, ag).astype(BF16)
    core = core_ref[0]
    width = wk_ref.shape[0]

    def place(half, row, value):
        @pl.when(core == half)
        def _():
            keep_ref[row : row + width, :] = value

        @pl.when(core != half)
        def _():
            send_ref[row : row + width, :] = value

    place(0, 0, tn(mn_ref[...], qg_ref[...]).astype(BF16))
    place(0, width, tn(rows[...], kp_ref[...]).astype(BF16))
    place(1, 0, tn(rows[...], vp_ref[...]).astype(BF16))
    place(1, width, tn(att_ref[...], og_ref[...]).astype(BF16))


def tail_body(kp_ref, vp_ref, wk_ref, wv_ref, att_ref, wo_ref, mesh_ref, qg_ref, wq_ref, gain_ref,
              og_ref, out_ref, grad_ref, s0, s1, s2, s3):
    cap = s0.shape[1]
    back = (nt(kp_ref[...], wk_ref[...]) + nt(vp_ref[...], wv_ref[...])).astype(BF16)
    for o in range(3):
        for k, piece in enumerate((s0, s1, s2, s3)):
            first = (o * 4 + k) * cap
            piece[o] = back[first : first + cap]
    wide = mesh_ref[...].astype(F32)
    out_ref[...] = (wide + nn(att_ref[...], wo_ref[...])).astype(BF16)
    upstream = nt(qg_ref[...], wq_ref[...])
    back = norm_back(wide, inv_rms(wide), gain_ref[...], upstream)
    grad_ref[...] = (og_ref[...].astype(F32) + back).astype(BF16)


def grid_body(sub_ref, rows_ref, x_ref, gain_ref, r0, r2, s0, s1, s2, s3, out_ref, got):
    points = x_ref.shape[0]
    half = points // 2
    cap = rows_ref.shape[3]
    block = 4 * cap
    me = sub_ref[0]
    gain = gain_ref[...]
    got[0:block] = r0[...]
    for k, piece in enumerate((s0, s1, s2, s3)):
        got[block + k * cap : block + (k + 1) * cap] = piece[1]
    got[2 * block : 3 * block] = r2[...]
    idx = []
    for o in range(3):
        for k in range(4):
            idx.append(rows_ref[0, o, pl.ds(lax.rem(me + k, 4), 1), :])
    idx = jnp.concatenate(idx, axis=1)
    tile = 256
    for t in range(points // tile):
        first = t * tile
        low = 0 if first < half else block
        ids = lax.broadcasted_iota(jnp.int32, (tile, 2 * block), 0) + first
        onehot = jnp.where(ids == idx[:, low : low + 2 * block], 1.0, 0.0).astype(BF16)
        upstream = nn(onehot, got[low : low + 2 * block, :])
        wide = x_ref[first : first + tile, :].astype(F32)
        out_ref[first : first + tile, :] = norm_back(
            wide, inv_rms(wide), gain, upstream
        ).astype(BF16)


def shifted(block, axis, k):
    n = lax.axis_size(axis)
    return lax.ppermute(block, axis, [(i, (i + k) % n) for i in range(n)])


def to_slab(block, d):
    n = lax.axis_size(SLAB)
    return lax.ppermute(block, SLAB, [(i, i + d) for i in range(n) if 0 <= i + d < n])


def sds(shape, dtype=BF16):
    return jax.ShapeDtypeStruct(shape, dtype)


def shards(grid_x, mesh_h, gain_grid, gain_mesh, w_query, w_key, w_value, w_out, edge_bias,
           neighbours, valid, send_rows, out_grad):
    points, width = grid_x.shape
    nodes, fan = neighbours.shape
    cap = send_rows.shape[3]
    block = 4 * cap
    slots = 3 * block
    heads = edge_bias.shape[1] // fan
    sub = lax.axis_index("z").astype(jnp.int32)
    core = lax.axis_index("gc").astype(jnp.int32)
    sub1, core1 = sub.reshape(1), core.reshape(1)
    gain_g, gain_m = gain_grid.reshape(1, width), gain_mesh.reshape(1, width)
    piece = sds((3, cap, width))

    b0, b1, b2, b3 = call(
        gather_body, [piece] * 4, [SM, VM, ANY, VM], (sub1, send_rows, grid_x, gain_g),
        1 << 30, 4 << 20, "gather_rows",
        [pltpu.VMEM((points, width), BF16), pltpu.SemaphoreType.DMA((2,))],
    )
    c1 = shifted(b1, "z", 1)
    c2 = shifted(b2, "z", 2)
    c3 = shifted(b3, "z", 3)

    source = (neighbours >> 6) & 3
    slot = (neighbours & ~192) | (((sub - source) & 3) << 6)
    nbr = slot.reshape(nodes // 8, 8, fan).transpose(0, 2, 1)
    bias = jnp.where((valid == 1)[:, None, :], edge_bias.reshape(nodes, heads, fan), ABSENT)
    bias = jnp.pad(bias.transpose(1, 0, 2), ((0, 0), (0, 0), (0, 128 - fan)))
    mesh_normed, queries, att_grad, dense = call(
        prep_body,
        [sds((nodes, width))] * 3 + [sds((heads, nodes, slots), F32)],
        [VM] * 7, (mesh_h, gain_m, w_query, w_out, out_grad, nbr, bias),
        1 << 26, 4 << 20, "prep", [pltpu.VMEM((nodes, slots), jnp.int32)],
    )

    def of(o):
        return jnp.concatenate([b0[o], c1[o], c2[o], c3[o]], axis=0)

    a0 = to_slab(of(0), -1)
    a2 = to_slab(of(2), 1)
    keep, send, key_part, value_part, attended, query_grad = call(
        middle_body,
        [sds((2 * width, width))] * 2 + [sds((slots, width))] * 2 + [sds((nodes, width))] * 2,
        [SM] + [VM] * 13,
        (core1, a0, a2, b0, c1, c2, c3, w_key, w_value, queries, att_grad, mesh_normed, out_grad,
         dense),
        3 << 30, 8 << 20, "middle", [pltpu.VMEM((slots, width), BF16)] * 3,
    )
    other = shifted(send, "gc", 1)
    mesh_out, mesh_grad, s0, s1, s2, s3 = call(
        tail_body, [sds((nodes, width))] * 2 + [piece] * 4, [VM] * 11,
        (key_part, value_part, w_key, w_value, attended, w_out, mesh_h, query_grad, w_query, gain_m,
         out_grad),
        1 << 30, 5 << 20, "tail",
    )
    chips = lax.axis_size(CHIPS)
    own = (keep.astype(F32) + other.astype(F32)).astype(BF16)
    own = own.reshape(chips, 2 * width // chips, width)
    parts = lax.all_to_all(own, CHIPS, 0, 0, tiled=True)

    t1 = shifted(s1, "z", -1)
    t2 = shifted(s2, "z", -2)
    t3 = shifted(s3, "z", -3)

    def back_of(o):
        return jnp.concatenate([s0[o], t1[o], t2[o], t3[o]], axis=0)

    r0 = to_slab(back_of(0), 1)
    r2 = to_slab(back_of(2), -1)
    (grid_grad,) = call(
        grid_body, [sds((points, width))], [SM] + [VM] * 9,
        (sub1, send_rows, grid_x, gain_g, r0, r2, s0, t1, t2, t3),
        1 << 30, 5 << 20, "grid_grad", [pltpu.VMEM((slots, width), BF16)],
    )

    total = jnp.sum(parts.astype(F32), axis=0).astype(BF16)
    mine = lax.all_to_all(
        jnp.broadcast_to(total[None], (chips, *total.shape)), CHIPS, 0, 0, tiled=True
    ).reshape(2 * width, width)
    theirs = shifted(mine, "gc", 1)
    first = jnp.where(core == 0, mine, theirs)
    second = jnp.where(core == 0, theirs, mine)
    weight_grads = jnp.concatenate([first, second], axis=0).astype(F32).reshape(4, width, width)
    return mesh_out, mesh_grad, grid_grad, weight_grads


def solution(mesh):
    split = Mesh(mesh.devices.reshape(4, 4, 2, mesh.shape["sub"]), ALL)
    rows = P(ALL, None)
    return jax.shard_map(
        shards,
        mesh=split,
        in_specs=(rows, rows, P(), P(), P(), P(), P(), P(), rows, rows, rows,
                  P(ALL, None, None, None), rows),
        out_specs=(rows, rows, rows, P()),
        check_vma=False,
    )
```

```python
import functools

import jax
import jax.numpy as jnp
from jax import lax
from jax.experimental import pallas as pl
from jax.experimental.pallas import tpu as pltpu
from jax.sharding import Mesh
from jax.sharding import PartitionSpec as P

SLAB = ("gx", "gy", "gc")
CHIPS = ("gx", "gy", "z")
ALL = ("gx", "gy", "gc", "z")

EPSILON = 1e-06
ABSENT = -1e30
F32 = jnp.float32
BF16 = jnp.bfloat16

VM = pl.BlockSpec(memory_space=pltpu.VMEM)
SM = pl.BlockSpec(memory_space=pltpu.SMEM)
HB = pl.BlockSpec(memory_space=pltpu.HBM)


def nn(a, b):
    return lax.dot_general(a, b, (((1,), (0,)), ((), ())), preferred_element_type=F32)


def nt(a, b):
    return lax.dot_general(a, b, (((1,), (1,)), ((), ())), preferred_element_type=F32)


def tn(a, b):
    return lax.dot_general(a, b, (((0,), (0,)), ((), ())), preferred_element_type=F32)


def inv_rms(wide):
    return lax.rsqrt(jnp.mean(wide * wide, axis=-1, keepdims=True) + EPSILON)


def norm_back(wide, factor, gain_row, upstream):
    scaled = gain_row * upstream
    inner = jnp.mean(wide * scaled, axis=-1, keepdims=True)
    return factor * scaled - wide * (factor * factor * factor * inner)


def call(body, outs, in_specs, args, flops, nbytes, name, scratch=(), out_specs=None, aliases=None):
    return pl.pallas_call(
        body,
        out_shape=outs,
        in_specs=in_specs,
        out_specs=out_specs or [VM] * len(outs),
        scratch_shapes=list(scratch),
        input_output_aliases=aliases or {},
        compiler_params=pltpu.CompilerParams(vmem_limit_bytes=24 << 20),
        cost_estimate=pl.CostEstimate(flops=flops, bytes_accessed=nbytes, transcendentals=0),
        name=name,
    )(*args)


def fetch(sources, targets, sems):
    copies = []
    for i, (source, target) in enumerate(zip(sources, targets)):
        copies.append(pltpu.make_async_copy(source, target, sems.at[i]))
        copies[-1].start()
    return copies


def held(*args):
    return [pltpu.VMEM(a.shape, a.dtype) for a in args] + [pltpu.SemaphoreType.DMA((len(args),))]


def gather_body(sub_ref, rows_hbm, gain_hbm, x_hbm, o0, o1, o2, o3, rows_ref, gain_ref, x_ref, sems):
    half = x_ref.shape[0] // 2
    cap = rows_ref.shape[3]
    outs = (o0, o1, o2, o3)
    parts = [pl.ds(i * half, half) for i in range(2)]
    copies = fetch(
        [rows_hbm, gain_hbm] + [x_hbm.at[p] for p in parts],
        [rows_ref, gain_ref] + [x_ref.at[p] for p in parts],
        sems,
    )
    copies[0].wait()
    copies[1].wait()
    me = sub_ref[0]
    eye = lax.broadcasted_iota(jnp.int32, (cap, cap), 0) == lax.broadcasted_iota(
        jnp.int32, (cap, cap), 1
    )
    gain = gain_ref[...]
    for step, (o, first, count) in enumerate(((0, 0, half), (2, half, half), (1, 0, 2 * half))):
        cols = []
        for k in range(4):
            s = lax.rem(me + k, 4)
            row = rows_ref[0, o, pl.ds(s, 1), :].astype(F32)
            cols.append(jnp.sum(jnp.where(eye, row, 0.0), axis=1, keepdims=True))
        col = jnp.concatenate(cols, axis=0).astype(jnp.int32) - first
        lanes = lax.broadcasted_iota(jnp.int32, (4 * cap, count), 1)
        onehot = jnp.where(lanes == col, 1.0, 0.0).astype(BF16)
        if step < 2:
            copies[2 + step].wait()
        wide = nn(onehot, x_ref[first : first + count, :])
        normed = (wide * inv_rms(wide) * gain).astype(BF16)
        for k in range(4):
            outs[k][o] = normed[k * cap : (k + 1) * cap]


def prep_body(nbr_ref, bias_ref, mesh_hbm, gain_hbm, wq_hbm, wo_hbm, og_hbm,
              normed_ref, q_ref, ag_ref, dense_ref, inv_ref,
              mesh_ref, gain_ref, wq_ref, wo_ref, og_ref, sems):
    copies = fetch(
        (mesh_hbm, gain_hbm, wq_hbm, wo_hbm, og_hbm), (mesh_ref, gain_ref, wq_ref, wo_ref, og_ref), sems
    )
    heads, nodes, slots = dense_ref.shape
    groups, fan, per = nbr_ref.shape
    lanes = lax.broadcasted_iota(jnp.int32, (fan, slots), 1)
    edge = lax.broadcasted_iota(jnp.int32, (fan, slots), 0) + 1

    def group(g, carry):
        block = nbr_ref[g]
        found = []
        for i in range(per):
            hit = jnp.where(block[:, i : i + 1] == lanes, edge, 0)
            found.append(jnp.sum(hit, axis=0, keepdims=True))
        inv_ref[pl.ds(pl.multiple_of(g * per, per), per), :] = jnp.concatenate(found, axis=0)
        return carry

    lax.fori_loop(0, groups, group, 0)
    for b in range(slots // 128):
        at = inv_ref[:, b * 128 : (b + 1) * 128] - 1
        here = at >= 0
        at = jnp.maximum(at, 0)
        for h in range(heads):
            got = jnp.take_along_axis(bias_ref[h], at, axis=1, mode="promise_in_bounds")
            dense_ref[h, :, b * 128 : (b + 1) * 128] = jnp.where(here, got, ABSENT)
    for copy in copies:
        copy.wait()
    wide = mesh_ref[...].astype(F32)
    normed = (wide * inv_rms(wide) * gain_ref[...]).astype(BF16)
    normed_ref[...] = normed
    q_ref[...] = (nn(normed, wq_ref[...]) * (128 ** -0.5)).astype(BF16)
    ag_ref[...] = nt(og_ref[...], wo_ref[...]).astype(BF16)


def middle_body(core_ref, a0, a2, b0, b1, b2, b3, q_ref, ag_ref, mn_ref, bias_ref,
                wk_hbm, wv_hbm, og_hbm, keep_ref, send_ref, kp_ref, vp_ref, att_ref, qg_ref,
                rows, keys, vals, wk_ref, wv_ref, og_ref, sems):
    copies = fetch((wk_hbm, wv_hbm, og_hbm), (wk_ref, wv_ref, og_ref), sems)
    heads = bias_ref.shape[0]
    block = a0.shape[0]
    cap = b0.shape[1]
    rows[0:block] = a0[...]
    for k, piece in enumerate((b0, b1, b2, b3)):
        rows[block + k * cap : block + (k + 1) * cap] = piece[1]
    rows[2 * block : 3 * block] = a2[...]
    copies[0].wait()
    keys[...] = nn(rows[...], wk_ref[...]).astype(BF16)
    copies[1].wait()
    copies[2].wait()
    vals[...] = nn(rows[...], wv_ref[...]).astype(BF16)
    for h in range(heads):
        at = slice(h * 128, (h + 1) * 128)
        q, ag = q_ref[:, at], ag_ref[:, at]
        kh, vh = keys[:, at], vals[:, at]
        scores = nt(q, kh) + bias_ref[h]
        peak = jnp.max(scores, axis=1, keepdims=True)
        terms = jnp.exp(scores - peak)
        probs = terms / jnp.sum(terms, axis=1, keepdims=True)
        probs_b = probs.astype(BF16)
        att_ref[:, at] = nn(probs_b, vh).astype(BF16)
        pg = nt(ag, vh)
        sg = (probs * (pg - jnp.sum(probs * pg, axis=1, keepdims=True))).astype(BF16)
        qg_ref[:, at] = (nn(sg, kh) * (128 ** -0.5)).astype(BF16)
        kp_ref[:, at] = tn(sg, q).astype(BF16)
        vp_ref[:, at] = tn(probs_b, ag).astype(BF16)
    core = core_ref[0]
    width = wk_ref.shape[0]

    def place(half, row, value):
        @pl.when(core == half)
        def _():
            keep_ref[row : row + width, :] = value

        @pl.when(core != half)
        def _():
            send_ref[row : row + width, :] = value

    place(0, 0, tn(mn_ref[...], qg_ref[...]).astype(BF16))
    place(0, width, tn(rows[...], kp_ref[...]).astype(BF16))
    place(1, 0, tn(rows[...], vp_ref[...]).astype(BF16))
    place(1, width, tn(att_ref[...], og_ref[...]).astype(BF16))


def tail_body(kp_ref, vp_ref, att_ref, qg_ref, wk_hbm, wv_hbm, wo_hbm, wq_hbm, mesh_hbm, gain_hbm,
              og_hbm, out_ref, grad_ref, s0, s1, s2, s3,
              wk_ref, wv_ref, wo_ref, wq_ref, mesh_ref, gain_ref, og_ref, sems):
    copies = fetch(
        (wk_hbm, wv_hbm, wo_hbm, wq_hbm, mesh_hbm, gain_hbm, og_hbm),
        (wk_ref, wv_ref, wo_ref, wq_ref, mesh_ref, gain_ref, og_ref),
        sems,
    )
    cap = s0.shape[1]
    copies[0].wait()
    copies[1].wait()
    back = (nt(kp_ref[...], wk_ref[...]) + nt(vp_ref[...], wv_ref[...])).astype(BF16)
    for o in range(3):
        for k, piece in enumerate((s0, s1, s2, s3)):
            first = (o * 4 + k) * cap
            piece[o] = back[first : first + cap]
    for copy in copies[2:]:
        copy.wait()
    wide = mesh_ref[...].astype(F32)
    out_ref[...] = (wide + nn(att_ref[...], wo_ref[...])).astype(BF16)
    upstream = nt(qg_ref[...], wq_ref[...])
    back = norm_back(wide, inv_rms(wide), gain_ref[...], upstream)
    grad_ref[...] = (og_ref[...].astype(F32) + back).astype(BF16)


def pack_body(p0, p1, p2, p3, low_ref, high_ref):
    cap = p0.shape[1]
    for k, piece in enumerate((p0, p1, p2, p3)):
        low_ref[k * cap : (k + 1) * cap, :] = piece[0]
        high_ref[k * cap : (k + 1) * cap, :] = piece[2]


def grid_body(sub_ref, r0, r2, s0, s1, s2, s3, rows_hbm, gain_hbm, x_hbm, out_hbm,
              got, done_ref, done_sems, rows_ref, gain_ref, x_ref, sems):
    copies = fetch((rows_hbm, gain_hbm, x_hbm), (rows_ref, gain_ref, x_ref), sems)
    points = x_ref.shape[0]
    half = points // 2
    cap = rows_ref.shape[3]
    block = 4 * cap
    me = sub_ref[0]
    got[0:block] = r0[...]
    for k, piece in enumerate((s0, s1, s2, s3)):
        got[block + k * cap : block + (k + 1) * cap] = piece[1]
    got[2 * block : 3 * block] = r2[...]
    for copy in copies:
        copy.wait()
    gain = gain_ref[...]
    idx = []
    for o in range(3):
        for k in range(4):
            idx.append(rows_ref[0, o, pl.ds(lax.rem(me + k, 4), 1), :])
    idx = jnp.concatenate(idx, axis=1)
    tile = 256
    stores = []
    for t in range(points // tile):
        first = t * tile
        low = 0 if first < half else block
        ids = lax.broadcasted_iota(jnp.int32, (tile, 2 * block), 0) + first
        onehot = jnp.where(ids == idx[:, low : low + 2 * block], 1.0, 0.0).astype(BF16)
        upstream = nn(onehot, got[low : low + 2 * block, :])
        wide = x_ref[first : first + tile, :].astype(F32)
        part = slice(first, first + tile)
        done_ref[part, :] = norm_back(wide, inv_rms(wide), gain, upstream).astype(BF16)
        stores.append(
            pltpu.make_async_copy(done_ref.at[part], out_hbm.at[part], done_sems.at[t])
        )
        stores[-1].start()
    for store in stores:
        store.wait()


def widen_body(turn, core_ref, half_ref, *refs):
    out_hbm, wide, sems = refs[-3:]
    count, width, _ = wide.shape
    first = (core_ref[0] ^ turn) * count
    part = width // 2
    copies = []
    for i in range(2 * count):
        m, rows = i // 2, pl.ds((i % 2) * part, part)
        wide[m, rows, :] = half_ref[i * part : (i + 1) * part, :].astype(F32)
        copies.append(
            pltpu.make_async_copy(wide.at[m, rows], out_hbm.at[first + m, rows], sems.at[i])
        )
        copies[-1].start()
    for copy in copies:
        copy.wait()


def shifted(block, axis, k):
    n = lax.axis_size(axis)
    return lax.ppermute(block, axis, [(i, (i + k) % n) for i in range(n)])


def to_slab(block, d):
    n = lax.axis_size(SLAB)
    return lax.ppermute(block, SLAB, [(i, i + d) for i in range(n) if 0 <= i + d < n])


def sds(shape, dtype=BF16):
    return jax.ShapeDtypeStruct(shape, dtype)


def shards(grid_x, mesh_h, gain_grid, gain_mesh, w_query, w_key, w_value, w_out, edge_bias,
           neighbours, valid, send_rows, out_grad):
    points, width = grid_x.shape
    nodes, fan = neighbours.shape
    cap = send_rows.shape[3]
    block = 4 * cap
    slots = 3 * block
    heads = edge_bias.shape[1] // fan
    sub = lax.axis_index("z").astype(jnp.int32)
    core = lax.axis_index("gc").astype(jnp.int32)
    sub1, core1 = sub.reshape(1), core.reshape(1)
    gain_g, gain_m = gain_grid.reshape(1, width), gain_mesh.reshape(1, width)
    piece = sds((3, cap, width))
    grid_x, mesh_h, out_grad, send_rows, w_key, w_value, w_query, w_out, gain_g, gain_m = (
        pltpu.with_memory_space_constraint(a, pltpu.HBM)
        for a in (grid_x, mesh_h, out_grad, send_rows, w_key, w_value, w_query, w_out, gain_g, gain_m)
    )

    b0, b1, b2, b3 = call(
        gather_body, [piece] * 4, [SM, HB, HB, HB], (sub1, send_rows, gain_g, grid_x),
        1 << 30, 4 << 20, "gather_rows",
        held(send_rows, gain_g, grid_x)[:-1] + [pltpu.SemaphoreType.DMA((4,))],
    )
    c1 = shifted(b1, "z", 1)
    c2 = shifted(b2, "z", 2)
    c3 = shifted(b3, "z", 3)

    neighbours, b0 = lax.optimization_barrier((neighbours, b0))
    source = (neighbours >> 6) & 3
    slot = (neighbours & ~192) | (((sub - source) & 3) << 6)
    nbr = slot.reshape(nodes // 8, 8, fan).transpose(0, 2, 1)
    bias = jnp.where((valid == 1)[:, None, :], edge_bias.reshape(nodes, heads, fan), ABSENT)
    bias = jnp.pad(bias.transpose(1, 0, 2), ((0, 0), (0, 0), (0, 128 - fan)))
    mesh_normed, queries, att_grad, dense = call(
        prep_body,
        [sds((nodes, width))] * 3 + [sds((heads, nodes, slots), F32)],
        [VM] * 2 + [HB] * 5, (nbr, bias, mesh_h, gain_m, w_query, w_out, out_grad),
        1 << 30, 8 << 20, "prep",
        [pltpu.VMEM((nodes, slots), jnp.int32)] + held(mesh_h, gain_m, w_query, w_out, out_grad),
    )
    c1, c2, c3, dense = lax.optimization_barrier((c1, c2, c3, dense))

    def packed(*pieces):
        return call(pack_body, [sds((block, width))] * 2, [VM] * 4, pieces, 0, 1 << 20, "pack")

    low, high = packed(b0, c1, c2, c3)
    a0 = to_slab(low, -1)
    a2 = to_slab(high, 1)
    keep, send, key_part, value_part, attended, query_grad = call(
        middle_body,
        [sds((2 * width, width))] * 2 + [sds((slots, width))] * 2 + [sds((nodes, width))] * 2,
        [SM] + [VM] * 10 + [HB] * 3,
        (core1, a0, a2, b0, c1, c2, c3, queries, att_grad, mesh_normed, dense, w_key, w_value,
         out_grad),
        3 << 30, 8 << 20, "middle",
        [pltpu.VMEM((slots, width), BF16)] * 3 + held(w_key, w_value, out_grad),
    )
    other = shifted(send, "gc", 1)
    mesh_out, mesh_grad, s0, s1, s2, s3 = call(
        tail_body, [sds((nodes, width))] * 2 + [piece] * 4, [VM] * 4 + [HB] * 7,
        (key_part, value_part, attended, query_grad, w_key, w_value, w_out, w_query, mesh_h, gain_m,
         out_grad),
        1 << 30, 5 << 20, "tail", held(w_key, w_value, w_out, w_query, mesh_h, gain_m, out_grad),
    )
    other, s1 = lax.optimization_barrier((other, s1))
    chips = lax.axis_size(CHIPS)
    own = (keep.astype(F32) + other.astype(F32)).astype(BF16)
    own = own.reshape(chips, 2 * width // chips, width)
    parts = lax.all_to_all(own, CHIPS, 0, 0, tiled=True)

    t1 = shifted(s1, "z", -1)
    t2 = shifted(s2, "z", -2)
    t3 = shifted(s3, "z", -3)
    parts, t1, t2, t3 = lax.optimization_barrier((parts, t1, t2, t3))

    low, high = packed(s0, t1, t2, t3)
    r0 = to_slab(low, 1)
    r2 = to_slab(high, -1)
    (grid_grad,) = call(
        grid_body, [sds((points, width))], [SM] + [VM] * 6 + [HB] * 3,
        (sub1, r0, r2, s0, t1, t2, t3, send_rows, gain_g, grid_x),
        1 << 30, 5 << 20, "grid_grad",
        [pltpu.VMEM((slots, width), BF16), pltpu.VMEM((points, width), BF16),
         pltpu.SemaphoreType.DMA((points // 256,))] + held(send_rows, gain_g, grid_x),
        [HB],
    )

    total = jnp.sum(parts.astype(F32), axis=0).astype(BF16)
    mine = lax.all_to_all(
        jnp.broadcast_to(total[None], (chips, *total.shape)), CHIPS, 0, 0, tiled=True
    ).reshape(2 * width, width)
    mine, grid_grad = lax.optimization_barrier((mine, grid_grad))
    theirs = shifted(mine, "gc", 1)
    whole = sds((4, width, width), F32)
    wide = [pltpu.VMEM((2, width, width), F32), pltpu.SemaphoreType.DMA((4,))]
    (weight_grads,) = call(
        functools.partial(widen_body, 0), [whole], [SM, VM], (core1, mine), 1 << 20, 3 << 20, "widen_own",
        wide, [HB],
    )
    (weight_grads,) = call(
        functools.partial(widen_body, 1), [whole], [SM, VM, HB], (core1, theirs, weight_grads),
        1 << 20, 3 << 20, "widen_other", wide, [HB], {2: 0},
    )
    return mesh_out, mesh_grad, grid_grad, weight_grads


def solution(mesh):
    split = Mesh(mesh.devices.reshape(4, 4, 2, mesh.shape["sub"]), ALL)
    rows = P(ALL, None)
    return jax.shard_map(
        shards,
        mesh=split,
        in_specs=(rows, rows, P(), P(), P(), P(), P(), P(), rows, rows, rows,
                  P(ALL, None, None, None), rows),
        out_specs=(rows, rows, rows, P()),
        check_vma=False,
    )
```

```python
import functools

import jax
import jax.numpy as jnp
from jax import lax
from jax.experimental import pallas as pl
from jax.experimental.pallas import tpu as pltpu
from jax.sharding import Mesh
from jax.sharding import PartitionSpec as P

SLAB = ("gx", "gy", "gc")
PLANE = ("gx", "gy")
ALL = ("gx", "gy", "gc", "z")

EPSILON = 1e-06
ABSENT = -1e30
F32 = jnp.float32
BF16 = jnp.bfloat16

VM = pl.BlockSpec(memory_space=pltpu.VMEM)
SM = pl.BlockSpec(memory_space=pltpu.SMEM)
HB = pl.BlockSpec(memory_space=pltpu.HBM)


def nn(a, b):
    return lax.dot_general(a, b, (((1,), (0,)), ((), ())), preferred_element_type=F32)


def nt(a, b):
    return lax.dot_general(a, b, (((1,), (1,)), ((), ())), preferred_element_type=F32)


def tn(a, b):
    return lax.dot_general(a, b, (((0,), (0,)), ((), ())), preferred_element_type=F32)


def inv_rms(wide):
    return lax.rsqrt(jnp.mean(wide * wide, axis=-1, keepdims=True) + EPSILON)


def norm_back(wide, factor, gain_row, upstream):
    scaled = gain_row * upstream
    inner = jnp.mean(wide * scaled, axis=-1, keepdims=True)
    return factor * scaled - wide * (factor * factor * factor * inner)


def call(body, outs, in_specs, args, flops, nbytes, name, scratch=(), out_specs=None, aliases=None):
    return pl.pallas_call(
        body,
        out_shape=outs,
        in_specs=in_specs,
        out_specs=out_specs or [VM] * len(outs),
        scratch_shapes=list(scratch),
        input_output_aliases=aliases or {},
        compiler_params=pltpu.CompilerParams(vmem_limit_bytes=24 << 20),
        cost_estimate=pl.CostEstimate(flops=flops, bytes_accessed=nbytes, transcendentals=0),
        name=name,
    )(*args)


def fetch(sources, targets, sems):
    copies = []
    for i, (source, target) in enumerate(zip(sources, targets)):
        copies.append(pltpu.make_async_copy(source, target, sems.at[i]))
        copies[-1].start()
    return copies


def held(*args):
    return [pltpu.VMEM(a.shape, a.dtype) for a in args] + [pltpu.SemaphoreType.DMA((len(args),))]


def gather_body(sub_ref, rows_hbm, gain_hbm, x_hbm, n0, n1, n2, n3, w0, w1, w2, w3,
                rows_ref, gain_ref, x_ref, sems):
    half = x_ref.shape[0] // 2
    cap = rows_ref.shape[3]
    parts = [pl.ds(i * half, half) for i in range(2)]
    copies = fetch(
        [rows_hbm, gain_hbm] + [x_hbm.at[p] for p in parts],
        [rows_ref, gain_ref] + [x_ref.at[p] for p in parts],
        sems,
    )
    copies[0].wait()
    copies[1].wait()
    me = sub_ref[0]
    eye = lax.broadcasted_iota(jnp.int32, (cap, cap), 0) == lax.broadcasted_iota(
        jnp.int32, (cap, cap), 1
    )
    gain = gain_ref[...]
    for step, (o, first, count) in enumerate(((0, 0, half), (2, half, half), (1, 0, 2 * half))):
        cols = []
        for k in range(4):
            s = lax.rem(me + k, 4)
            row = rows_ref[0, o, pl.ds(s, 1), :].astype(F32)
            cols.append(jnp.sum(jnp.where(eye, row, 0.0), axis=1, keepdims=True))
        col = jnp.concatenate(cols, axis=0).astype(jnp.int32) - first
        lanes = lax.broadcasted_iota(jnp.int32, (4 * cap, count), 1)
        onehot = jnp.where(lanes == col, 1.0, 0.0).astype(BF16)
        if step < 2:
            copies[2 + step].wait()
        wide = nn(onehot, x_ref[first : first + count, :])
        normed = (wide * inv_rms(wide) * gain).astype(BF16)
        for k in range(4):
            piece = normed[k * cap : (k + 1) * cap]
            if step < 2:
                (n0, n1, n2, n3)[k][step] = piece
            else:
                (w0, w1, w2, w3)[k][...] = piece


def prep_body(sub_ref, mesh_hbm, gain_hbm, wq_hbm, wo_hbm, og_hbm, nbr_hbm, valid_hbm, bias_hbm,
              normed_ref, q_ref, ag_ref, dense_ref, inv_ref, edge_ref,
              nbr_ref, valid_ref, bias_ref, mesh_ref, gain_ref, wq_ref, wo_ref, og_ref, sems):
    copies = fetch(
        (nbr_hbm, valid_hbm, bias_hbm, mesh_hbm, gain_hbm, wq_hbm, wo_hbm, og_hbm),
        (nbr_ref, valid_ref, bias_ref, mesh_ref, gain_ref, wq_ref, wo_ref, og_ref),
        sems,
    )
    heads, nodes, slots = dense_ref.shape
    fan = nbr_ref.shape[1]
    for copy in copies[:3]:
        copy.wait()
    slot = nbr_ref[...]
    slot = (slot & ~192) | (((sub_ref[0] - (slot >> 6)) & 3) << 6)
    high, low = slot >> 7, slot & 127
    blocks = lax.broadcasted_iota(jnp.int32, (8, fan), 0)
    lanes = lax.broadcasted_iota(jnp.int32, (128, fan), 0)
    edge = lax.broadcasted_iota(jnp.int32, (8, fan), 1).astype(F32) + 1.0
    for m in range(nodes):
        named = jnp.where(high[m : m + 1, :] == blocks, edge, 0.0).astype(BF16)
        places = jnp.where(low[m : m + 1, :] == lanes, 1.0, 0.0).astype(BF16)
        inv_ref[m * 8 : (m + 1) * 8, :] = nt(named, places)
    live = valid_ref[...] == 1
    for h in range(heads):
        edge_ref[h, :, 0:fan] = jnp.where(live, bias_ref[:, h * fan : (h + 1) * fan], ABSENT)
    for b in range(slots // 128):
        at = inv_ref[pl.ds(b, nodes, stride=8), :].astype(jnp.int32) - 1
        here = at >= 0
        at = jnp.maximum(at, 0)
        for h in range(heads):
            got = jnp.take_along_axis(edge_ref[h], at, axis=1, mode="promise_in_bounds")
            dense_ref[h, :, b * 128 : (b + 1) * 128] = jnp.where(here, got, ABSENT)
    for copy in copies[3:]:
        copy.wait()
    wide = mesh_ref[...].astype(F32)
    normed = (wide * inv_rms(wide) * gain_ref[...]).astype(BF16)
    normed_ref[...] = normed
    q_ref[...] = (nn(normed, wq_ref[...]) * (128 ** -0.5)).astype(BF16)
    ag_ref[...] = nt(og_ref[...], wo_ref[...]).astype(BF16)


def middle_body(core_ref, a0, a2, b0, b1, b2, b3, q_ref, ag_ref, mn_ref, bias_ref,
                wk_hbm, wv_hbm, og_hbm, keep_ref, send_ref, kp_ref, vp_ref, att_ref, qg_ref,
                wk_ref, wv_ref, og_ref, rows, keys, vals, sems):
    copies = fetch((wk_hbm, wv_hbm, og_hbm), (wk_ref, wv_ref, og_ref), sems)
    heads = bias_ref.shape[0]
    block = a0.shape[0]
    cap = b0.shape[0]
    rows[0:block] = a0[...]
    for k, piece in enumerate((b0, b1, b2, b3)):
        rows[block + k * cap : block + (k + 1) * cap] = piece[...]
    rows[2 * block : 3 * block] = a2[...]
    copies[0].wait()
    keys[...] = nn(rows[...], wk_ref[...]).astype(BF16)
    copies[1].wait()
    copies[2].wait()
    vals[...] = nn(rows[...], wv_ref[...]).astype(BF16)
    for h in range(heads):
        at = slice(h * 128, (h + 1) * 128)
        q, ag = q_ref[:, at], ag_ref[:, at]
        kh, vh = keys[:, at], vals[:, at]
        scores = nt(q, kh) + bias_ref[h]
        peak = jnp.max(scores, axis=1, keepdims=True)
        terms = jnp.exp(scores - peak)
        probs = terms / jnp.sum(terms, axis=1, keepdims=True)
        probs_b = probs.astype(BF16)
        att_ref[:, at] = nn(probs_b, vh).astype(BF16)
        pg = nt(ag, vh)
        sg = (probs * (pg - jnp.sum(probs * pg, axis=1, keepdims=True))).astype(BF16)
        qg_ref[:, at] = (nn(sg, kh) * (128 ** -0.5)).astype(BF16)
        kp_ref[:, at] = tn(sg, q).astype(BF16)
        vp_ref[:, at] = tn(probs_b, ag).astype(BF16)
    core = core_ref[0]
    width = wk_ref.shape[0]

    def place(half, row, value):
        @pl.when(core == half)
        def _():
            keep_ref[row : row + width, :] = value

        @pl.when(core != half)
        def _():
            send_ref[row : row + width, :] = value

    place(0, 0, tn(mn_ref[...], qg_ref[...]).astype(BF16))
    place(0, width, tn(rows[...], kp_ref[...]).astype(BF16))
    place(1, 0, tn(rows[...], vp_ref[...]).astype(BF16))
    place(1, width, tn(att_ref[...], og_ref[...]).astype(BF16))


def tail_body(kp_ref, vp_ref, att_ref, qg_ref, wk_ref, wv_ref, og_ref, wo_hbm, wq_hbm, mesh_hbm,
              gain_hbm, out_ref, grad_ref, s0, s1, s2, s3,
              wo_ref, wq_ref, mesh_ref, gain_ref, sems):
    copies = fetch(
        (wo_hbm, wq_hbm, mesh_hbm, gain_hbm), (wo_ref, wq_ref, mesh_ref, gain_ref), sems
    )
    cap = s0.shape[1]
    back = (nt(kp_ref[...], wk_ref[...]) + nt(vp_ref[...], wv_ref[...])).astype(BF16)
    for o in range(3):
        for k, piece in enumerate((s0, s1, s2, s3)):
            first = (o * 4 + k) * cap
            piece[o] = back[first : first + cap]
    for copy in copies:
        copy.wait()
    wide = mesh_ref[...].astype(F32)
    out_ref[...] = (wide + nn(att_ref[...], wo_ref[...])).astype(BF16)
    upstream = nt(qg_ref[...], wq_ref[...])
    back = norm_back(wide, inv_rms(wide), gain_ref[...], upstream)
    grad_ref[...] = (og_ref[...].astype(F32) + back).astype(BF16)


def pack_body(p0, p1, p2, p3, low_ref, high_ref):
    cap = p0.shape[1]
    for k, piece in enumerate((p0, p1, p2, p3)):
        low_ref[k * cap : (k + 1) * cap, :] = piece[0]
        high_ref[k * cap : (k + 1) * cap, :] = piece[piece.shape[0] - 1]


def grid_body(sub_ref, r0, r2, s0, s1, s2, s3, rows_hbm, gain_hbm, x_hbm, out_hbm,
              got, done_ref, done_sems, rows_ref, gain_ref, x_ref, sems):
    copies = fetch((rows_hbm, gain_hbm, x_hbm), (rows_ref, gain_ref, x_ref), sems)
    points = x_ref.shape[0]
    half = points // 2
    cap = rows_ref.shape[3]
    block = 4 * cap
    me = sub_ref[0]
    got[0:block] = r0[...]
    for k, piece in enumerate((s0, s1, s2, s3)):
        got[block + k * cap : block + (k + 1) * cap] = piece[1]
    got[2 * block : 3 * block] = r2[...]
    for copy in copies:
        copy.wait()
    gain = gain_ref[...]
    idx = []
    for o in range(3):
        for k in range(4):
            idx.append(rows_ref[0, o, pl.ds(lax.rem(me + k, 4), 1), :])
    idx = jnp.concatenate(idx, axis=1)
    tile = 256
    stores = []
    for t in range(points // tile):
        first = t * tile
        low = 0 if first < half else block
        ids = lax.broadcasted_iota(jnp.int32, (tile, 2 * block), 0) + first
        onehot = jnp.where(ids == idx[:, low : low + 2 * block], 1.0, 0.0).astype(BF16)
        upstream = nn(onehot, got[low : low + 2 * block, :])
        wide = x_ref[first : first + tile, :].astype(F32)
        part = slice(first, first + tile)
        done_ref[part, :] = norm_back(wide, inv_rms(wide), gain, upstream).astype(BF16)
        stores.append(
            pltpu.make_async_copy(done_ref.at[part], out_hbm.at[part], done_sems.at[t])
        )
        stores[-1].start()
    for store in stores:
        store.wait()


def widen_body(turn, core_ref, half_ref, *refs):
    out_hbm, wide, sems = refs[-3:]
    count, width, _ = wide.shape
    first = (core_ref[0] ^ turn) * count
    part = width // 2
    copies = []
    for i in range(2 * count):
        m, rows = i // 2, pl.ds((i % 2) * part, part)
        wide[m, rows, :] = half_ref[i * part : (i + 1) * part, :].astype(F32)
        copies.append(
            pltpu.make_async_copy(wide.at[m, rows], out_hbm.at[first + m, rows], sems.at[i])
        )
        copies[-1].start()
    for copy in copies:
        copy.wait()


def pair_body(keep_ref, other_ref, out_hbm, sums, sems):
    part = sums.shape[0] // 4
    copies = []
    for i in range(4):
        at = slice(i * part, (i + 1) * part)
        sums[at, :] = (keep_ref[at, :].astype(F32) + other_ref[at, :].astype(F32)).astype(BF16)
        copies.append(pltpu.make_async_copy(sums.at[at], out_hbm.at[at], sems.at[i]))
        copies[-1].start()
    for copy in copies:
        copy.wait()


def spread_body(p0, p1, p2, p3, out_hbm, total, sems):
    even = p0[...].astype(F32) + p2[...].astype(F32)
    odd = p1[...].astype(F32) + p3[...].astype(F32)
    total[...] = (even + odd).astype(BF16)
    copies = []
    for i in range(out_hbm.shape[0]):
        copies.append(pltpu.make_async_copy(total, out_hbm.at[i], sems.at[i]))
        copies[-1].start()
    for copy in copies:
        copy.wait()


def shifted(block, axis, k):
    n = lax.axis_size(axis)
    return lax.ppermute(block, axis, [(i, (i + k) % n) for i in range(n)])


def to_slab(block, d):
    n = lax.axis_size(SLAB)
    return lax.ppermute(block, SLAB, [(i, i + d) for i in range(n) if 0 <= i + d < n])


def sds(shape, dtype=BF16):
    return jax.ShapeDtypeStruct(shape, dtype)


def shards(grid_x, mesh_h, gain_grid, gain_mesh, w_query, w_key, w_value, w_out, edge_bias,
           neighbours, valid, send_rows, out_grad):
    points, width = grid_x.shape
    nodes, fan = neighbours.shape
    cap = send_rows.shape[3]
    block = 4 * cap
    slots = 3 * block
    heads = edge_bias.shape[1] // fan
    sub1 = lax.axis_index("z").astype(jnp.int32).reshape(1)
    core1 = lax.axis_index("gc").astype(jnp.int32).reshape(1)
    gain_g, gain_m = gain_grid.reshape(1, width), gain_mesh.reshape(1, width)
    (grid_x, mesh_h, out_grad, send_rows, w_key, w_value, w_query, w_out, gain_g, gain_m, edge_bias,
     neighbours, valid) = (
        pltpu.with_memory_space_constraint(a, pltpu.HBM)
        for a in (grid_x, mesh_h, out_grad, send_rows, w_key, w_value, w_query, w_out, gain_g, gain_m,
                  edge_bias, neighbours, valid)
    )

    n0, n1, n2, n3, w0, w1, w2, w3 = call(
        gather_body, [sds((2, cap, width))] * 4 + [sds((cap, width))] * 4, [SM, HB, HB, HB],
        (sub1, send_rows, gain_g, grid_x), 1 << 30, 4 << 20, "gather_rows",
        held(send_rows, gain_g, grid_x)[:-1] + [pltpu.SemaphoreType.DMA((4,))],
    )
    n1, n2, n3 = (shifted(n, "z", k) for k, n in ((1, n1), (2, n2), (3, n3)))
    w1, w2, w3 = (shifted(w, "z", k) for k, w in ((1, w1), (2, w2), (3, w3)))

    def packed(*pieces):
        return call(pack_body, [sds((block, width))] * 2, [VM] * 4, pieces, 0, 1 << 20, "pack")

    low, high = packed(n0, n1, n2, n3)
    sub2, low = lax.optimization_barrier((sub1, low))
    a0 = to_slab(low, -1)
    a2 = to_slab(high, 1)
    prep_args = (mesh_h, gain_m, w_query, w_out, out_grad, neighbours, valid, edge_bias)
    mesh_normed, queries, att_grad, dense = call(
        prep_body,
        [sds((nodes, width))] * 3 + [sds((heads, nodes, slots), F32)],
        [SM] + [HB] * 8, (sub2, *prep_args), 1 << 30, 8 << 20, "prep",
        [pltpu.VMEM((nodes * 8, 128), F32), pltpu.VMEM((heads, nodes, 128), F32)]
        + held(neighbours, valid, edge_bias, mesh_h, gain_m, w_query, w_out, out_grad),
    )
    keep, send, key_part, value_part, attended, query_grad, wk_near, wv_near, og_near = call(
        middle_body,
        [sds((2 * width, width))] * 2 + [sds((slots, width))] * 2 + [sds((nodes, width))] * 2
        + [sds((width, width))] * 2 + [sds((nodes, width))],
        [SM] + [VM] * 10 + [HB] * 3,
        (core1, a0, a2, w0, w1, w2, w3, queries, att_grad, mesh_normed, dense, w_key, w_value,
         out_grad),
        3 << 30, 8 << 20, "middle",
        [pltpu.VMEM((slots, width), BF16)] * 3 + [pltpu.SemaphoreType.DMA((3,))],
    )

    other = shifted(send, "gc", 1)
    piece = sds((3, cap, width))
    mesh_out, mesh_grad, s0, s1, s2, s3 = call(
        tail_body, [sds((nodes, width))] * 2 + [piece] * 4, [VM] * 7 + [HB] * 4,
        (key_part, value_part, attended, query_grad, wk_near, wv_near, og_near, w_out, w_query, mesh_h,
         gain_m),
        1 << 30, 5 << 20, "tail", held(w_out, w_query, mesh_h, gain_m),
    )
    other, s1 = lax.optimization_barrier((other, s1))
    (own,) = call(
        pair_body, [sds((2 * width, width))], [VM] * 2, (keep, other), 1 << 20, 3 << 20, "pair",
        [pltpu.VMEM((2 * width, width), BF16), pltpu.SemaphoreType.DMA((4,))], [HB],
    )
    plane = lax.axis_size(PLANE)
    share = 2 * width // plane
    parts = lax.all_to_all(own.reshape(plane, share, width), PLANE, 0, 0, tiled=True)

    t1, t2, t3 = (shifted(s, "z", -k) for k, s in ((1, s1), (2, s2), (3, s3)))
    low, high = packed(s0, t1, t2, t3)
    parts, low, high = lax.optimization_barrier((parts, low, high))
    r0 = to_slab(low, 1)
    r2 = to_slab(high, -1)
    part = jnp.sum(parts.astype(F32), axis=0).astype(BF16)
    p1, p2, p3 = (shifted(part, "z", k) for k in (1, 2, 3))
    (spread,) = call(
        spread_body, [sds((plane, share, width))], [VM] * 4, (part, p1, p2, p3), 1 << 18, 1 << 20,
        "spread", [pltpu.VMEM((share, width), BF16), pltpu.SemaphoreType.DMA((plane,))], [HB],
    )
    mine = lax.all_to_all(spread, PLANE, 0, 0, tiled=True).reshape(2 * width, width)
    (grid_grad,) = call(
        grid_body, [sds((points, width))], [SM] + [VM] * 6 + [HB] * 3,
        (sub1, r0, r2, s0, t1, t2, t3, send_rows, gain_g, grid_x),
        1 << 30, 5 << 20, "grid_grad",
        [pltpu.VMEM((slots, width), BF16), pltpu.VMEM((points, width), BF16),
         pltpu.SemaphoreType.DMA((points // 256,))] + held(send_rows, gain_g, grid_x),
        [HB],
    )
    mine, grid_grad = lax.optimization_barrier((mine, grid_grad))
    theirs = shifted(mine, "gc", 1)
    whole = sds((4, width, width), F32)
    wide = [pltpu.VMEM((2, width, width), F32), pltpu.SemaphoreType.DMA((4,))]
    (weight_grads,) = call(
        functools.partial(widen_body, 0), [whole], [SM, VM], (core1, mine), 1 << 20, 3 << 20, "widen_own",
        wide, [HB],
    )
    (weight_grads,) = call(
        functools.partial(widen_body, 1), [whole], [SM, VM, HB], (core1, theirs, weight_grads),
        1 << 20, 3 << 20, "widen_other", wide, [HB], {2: 0},
    )
    return mesh_out, mesh_grad, grid_grad, weight_grads


def solution(mesh):
    split = Mesh(mesh.devices.reshape(4, 4, 2, mesh.shape["sub"]), ALL)
    rows = P(ALL, None)
    return jax.shard_map(
        shards,
        mesh=split,
        in_specs=(rows, rows, P(), P(), P(), P(), P(), P(), rows, rows, rows,
                  P(ALL, None, None, None), rows),
        out_specs=(rows, rows, rows, P()),
        check_vma=False,
    )
```

```python
import functools

import jax
import jax.numpy as jnp
from jax import lax
from jax.experimental import pallas as pl
from jax.experimental.pallas import tpu as pltpu
from jax.sharding import Mesh
from jax.sharding import PartitionSpec as P

SLAB = ("gx", "gy", "gc")
PLANE = ("gx", "gy")
ALL = ("gx", "gy", "gc", "z")

EPSILON = 1e-06
ABSENT = -1e30
F32 = jnp.float32
BF16 = jnp.bfloat16

VM = pl.BlockSpec(memory_space=pltpu.VMEM)
SM = pl.BlockSpec(memory_space=pltpu.SMEM)
HB = pl.BlockSpec(memory_space=pltpu.HBM)


def nn(a, b):
    return lax.dot_general(a, b, (((1,), (0,)), ((), ())), preferred_element_type=F32)


def nt(a, b):
    return lax.dot_general(a, b, (((1,), (1,)), ((), ())), preferred_element_type=F32)


def tn(a, b):
    return lax.dot_general(a, b, (((0,), (0,)), ((), ())), preferred_element_type=F32)


def inv_rms(wide):
    return lax.rsqrt(jnp.mean(wide * wide, axis=-1, keepdims=True) + EPSILON)


def norm_back(wide, factor, gain_row, upstream):
    scaled = gain_row * upstream
    inner = jnp.mean(wide * scaled, axis=-1, keepdims=True)
    return factor * scaled - wide * (factor * factor * factor * inner)


def call(body, outs, in_specs, args, flops, nbytes, name, scratch=(), out_specs=None, aliases=None):
    return pl.pallas_call(
        body,
        out_shape=outs,
        in_specs=in_specs,
        out_specs=out_specs or [VM] * len(outs),
        scratch_shapes=list(scratch),
        input_output_aliases=aliases or {},
        compiler_params=pltpu.CompilerParams(vmem_limit_bytes=24 << 20),
        cost_estimate=pl.CostEstimate(flops=flops, bytes_accessed=nbytes, transcendentals=0),
        name=name,
    )(*args)


def fetch(sources, targets, sems):
    copies = []
    for i, (source, target) in enumerate(zip(sources, targets)):
        copies.append(pltpu.make_async_copy(source, target, sems.at[i]))
        copies[-1].start()
    return copies


def held(*args):
    return [pltpu.VMEM(a.shape, a.dtype) for a in args] + [pltpu.SemaphoreType.DMA((len(args),))]


def gather_body(sub_ref, rows_hbm, gain_hbm, x_hbm, p0, p1, p2, p3,
                rows_ref, gain_ref, x_ref, sems):
    half = x_ref.shape[0] // 2
    cap = rows_ref.shape[3]
    parts = [pl.ds(i * half, half) for i in range(2)]
    copies = fetch(
        [rows_hbm, gain_hbm] + [x_hbm.at[p] for p in parts],
        [rows_ref, gain_ref] + [x_ref.at[p] for p in parts],
        sems,
    )
    copies[0].wait()
    copies[1].wait()
    me = sub_ref[0]
    eye = lax.broadcasted_iota(jnp.int32, (cap, cap), 0) == lax.broadcasted_iota(
        jnp.int32, (cap, cap), 1
    )
    gain = gain_ref[...]
    for step, (o, first, count) in enumerate(((0, 0, half), (2, half, half), (1, 0, 2 * half))):
        cols = []
        for k in range(4):
            s = lax.rem(me + k, 4)
            row = rows_ref[0, o, pl.ds(s, 1), :].astype(F32)
            cols.append(jnp.sum(jnp.where(eye, row, 0.0), axis=1, keepdims=True))
        col = jnp.concatenate(cols, axis=0).astype(jnp.int32) - first
        lanes = lax.broadcasted_iota(jnp.int32, (4 * cap, count), 1)
        onehot = jnp.where(lanes == col, 1.0, 0.0).astype(BF16)
        if step < 2:
            copies[2 + step].wait()
        wide = nn(onehot, x_ref[first : first + count, :])
        normed = (wide * inv_rms(wide) * gain).astype(BF16)
        for k in range(4):
            (p0, p1, p2, p3)[k][o] = normed[k * cap : (k + 1) * cap]


def prep_body(sub_ref, mesh_hbm, gain_hbm, wq_hbm, wo_hbm, og_hbm, nbr_hbm, valid_hbm, bias_hbm,
              normed_ref, q_ref, ag_ref, dense_ref, inv_ref, edge_ref,
              nbr_ref, valid_ref, bias_ref, mesh_ref, gain_ref, wq_ref, wo_ref, og_ref, sems):
    copies = fetch(
        (nbr_hbm, valid_hbm, bias_hbm, mesh_hbm, gain_hbm, wq_hbm, wo_hbm, og_hbm),
        (nbr_ref, valid_ref, bias_ref, mesh_ref, gain_ref, wq_ref, wo_ref, og_ref),
        sems,
    )
    heads, nodes, slots = dense_ref.shape
    fan = nbr_ref.shape[1]
    for copy in copies[:3]:
        copy.wait()
    slot = nbr_ref[...]
    slot = (slot & ~192) | (((sub_ref[0] - (slot >> 6)) & 3) << 6)
    high, low = slot >> 7, slot & 127
    blocks = lax.broadcasted_iota(jnp.int32, (8, fan), 0)
    lanes = lax.broadcasted_iota(jnp.int32, (128, fan), 0)
    edge = lax.broadcasted_iota(jnp.int32, (8, fan), 1).astype(F32) + 1.0
    for m in range(nodes):
        named = jnp.where(high[m : m + 1, :] == blocks, edge, 0.0).astype(BF16)
        places = jnp.where(low[m : m + 1, :] == lanes, 1.0, 0.0).astype(BF16)
        inv_ref[m * 8 : (m + 1) * 8, :] = nt(named, places)
    live = valid_ref[...] == 1
    for h in range(heads):
        edge_ref[h, :, 0:fan] = jnp.where(live, bias_ref[:, h * fan : (h + 1) * fan], ABSENT)
    for b in range(slots // 128):
        at = inv_ref[pl.ds(b, nodes, stride=8), :].astype(jnp.int32) - 1
        here = at >= 0
        at = jnp.maximum(at, 0)
        for h in range(heads):
            got = jnp.take_along_axis(edge_ref[h], at, axis=1, mode="promise_in_bounds")
            dense_ref[h, :, b * 128 : (b + 1) * 128] = jnp.where(here, got, ABSENT)
    for copy in copies[3:]:
        copy.wait()
    wide = mesh_ref[...].astype(F32)
    normed = (wide * inv_rms(wide) * gain_ref[...]).astype(BF16)
    normed_ref[...] = normed
    q_ref[...] = (nn(normed, wq_ref[...]) * (128 ** -0.5)).astype(BF16)
    ag_ref[...] = nt(og_ref[...], wo_ref[...]).astype(BF16)


def middle_body(core_ref, near, far, b0, b1, b2, b3, q_ref, ag_ref, mn_ref, bias_ref,
                wk_hbm, wv_hbm, og_hbm, keep_ref, send_ref, part_ref, att_ref, qg_ref,
                wkv_ref, og_ref, rows, keys, vals, sems):
    width = q_ref.shape[1]
    copies = fetch(
        (wk_hbm, wv_hbm, og_hbm),
        (wkv_ref.at[:, pl.ds(0, width)], wkv_ref.at[:, pl.ds(width, width)], og_ref),
        sems,
    )
    heads = bias_ref.shape[0]
    block = near.shape[0]
    cap = b0.shape[1]
    core = core_ref[0]
    rows[pl.ds(pl.multiple_of(core * (2 * block), block), block), :] = near[...]
    rows[pl.ds(pl.multiple_of((1 - core) * (2 * block), block), block), :] = far[...]
    for k, piece in enumerate((b0, b1, b2, b3)):
        rows[block + k * cap : block + (k + 1) * cap] = piece[1]
    copies[0].wait()
    keys[...] = nn(rows[...], wkv_ref[:, :width]).astype(BF16)
    copies[1].wait()
    copies[2].wait()
    vals[...] = nn(rows[...], wkv_ref[:, width:]).astype(BF16)
    for h in range(heads):
        at = slice(h * 128, (h + 1) * 128)
        q, ag = q_ref[:, at], ag_ref[:, at]
        kh, vh = keys[:, at], vals[:, at]
        scores = nt(q, kh) + bias_ref[h]
        peak = jnp.max(scores, axis=1, keepdims=True)
        terms = jnp.exp(scores - peak)
        probs = terms / jnp.sum(terms, axis=1, keepdims=True)
        probs_b = probs.astype(BF16)
        att_ref[:, at] = nn(probs_b, vh).astype(BF16)
        pg = nt(ag, vh)
        sg = (probs * (pg - jnp.sum(probs * pg, axis=1, keepdims=True))).astype(BF16)
        qg_ref[:, at] = (nn(sg, kh) * (128 ** -0.5)).astype(BF16)
        part_ref[:, at] = tn(sg, q).astype(BF16)
        part_ref[:, width + h * 128 : width + (h + 1) * 128] = tn(probs_b, ag).astype(BF16)

    def place(half, row, value):
        @pl.when(core == half)
        def _():
            keep_ref[row : row + width, :] = value

        @pl.when(core != half)
        def _():
            send_ref[row : row + width, :] = value

    both = tn(rows[...], part_ref[...]).astype(BF16)
    place(0, 0, tn(mn_ref[...], qg_ref[...]).astype(BF16))
    place(0, width, both[:, :width])
    place(1, 0, both[:, width:])
    place(1, width, tn(att_ref[...], og_ref[...]).astype(BF16))


def tail_body(part_ref, att_ref, qg_ref, wkv_ref, og_ref, wo_hbm, wq_hbm, mesh_hbm,
              gain_hbm, out_ref, grad_ref, s0, s1, s2, s3,
              wo_ref, wq_ref, mesh_ref, gain_ref, sems):
    copies = fetch(
        (wo_hbm, wq_hbm, mesh_hbm, gain_hbm), (wo_ref, wq_ref, mesh_ref, gain_ref), sems
    )
    cap = s0.shape[1]
    back = nt(part_ref[...], wkv_ref[...]).astype(BF16)
    for o in range(3):
        for k, piece in enumerate((s0, s1, s2, s3)):
            first = (o * 4 + k) * cap
            piece[o] = back[first : first + cap]
    for copy in copies:
        copy.wait()
    wide = mesh_ref[...].astype(F32)
    out_ref[...] = (wide + nn(att_ref[...], wo_ref[...])).astype(BF16)
    upstream = nt(qg_ref[...], wq_ref[...])
    back = norm_back(wide, inv_rms(wide), gain_ref[...], upstream)
    grad_ref[...] = (og_ref[...].astype(F32) + back).astype(BF16)


def pack_body(near_if_first, core_ref, p0, p1, p2, p3, near_ref, far_ref):
    cap = p0.shape[1]
    near = lax.select(core_ref[0] == 0, near_if_first, 2 - near_if_first)
    for k, piece in enumerate((p0, p1, p2, p3)):
        near_ref[k * cap : (k + 1) * cap, :] = piece[near]
        far_ref[k * cap : (k + 1) * cap, :] = piece[2 - near]


def grid_body(sub_ref, core_ref, near, far, s0, s1, s2, s3, rows_hbm, gain_hbm, x_hbm, out_hbm,
              got, done_ref, done_sems, rows_ref, gain_ref, x_ref, sems):
    copies = fetch((rows_hbm, gain_hbm, x_hbm), (rows_ref, gain_ref, x_ref), sems)
    points = x_ref.shape[0]
    half = points // 2
    cap = rows_ref.shape[3]
    block = 4 * cap
    me = sub_ref[0]
    core = core_ref[0]
    got[pl.ds(pl.multiple_of((1 - core) * (2 * block), block), block), :] = near[...]
    got[pl.ds(pl.multiple_of(core * (2 * block), block), block), :] = far[...]
    for k, piece in enumerate((s0, s1, s2, s3)):
        got[block + k * cap : block + (k + 1) * cap] = piece[1]
    for copy in copies:
        copy.wait()
    gain = gain_ref[...]
    idx = []
    for o in range(3):
        for k in range(4):
            idx.append(rows_ref[0, o, pl.ds(lax.rem(me + k, 4), 1), :])
    idx = jnp.concatenate(idx, axis=1)
    tile = 256
    stores = []
    for t in range(points // tile):
        first = t * tile
        low = 0 if first < half else block
        ids = lax.broadcasted_iota(jnp.int32, (tile, 2 * block), 0) + first
        onehot = jnp.where(ids == idx[:, low : low + 2 * block], 1.0, 0.0).astype(BF16)
        upstream = nn(onehot, got[low : low + 2 * block, :])
        wide = x_ref[first : first + tile, :].astype(F32)
        part = slice(first, first + tile)
        done_ref[part, :] = norm_back(wide, inv_rms(wide), gain, upstream).astype(BF16)
        stores.append(
            pltpu.make_async_copy(done_ref.at[part], out_hbm.at[part], done_sems.at[t])
        )
        stores[-1].start()
    for store in stores:
        store.wait()


def widen_body(turn, core_ref, half_ref, *refs):
    out_hbm, wide, sems = refs[-3:]
    count, width, _ = wide.shape
    first = (core_ref[0] ^ turn) * count
    part = width // 2
    copies = []
    for i in range(2 * count):
        m, rows = i // 2, pl.ds((i % 2) * part, part)
        wide[m, rows, :] = half_ref[i * part : (i + 1) * part, :].astype(F32)
        copies.append(
            pltpu.make_async_copy(wide.at[m, rows], out_hbm.at[first + m, rows], sems.at[i])
        )
        copies[-1].start()
    for copy in copies:
        copy.wait()


def pair_body(keep_ref, other_ref, out_hbm, sums, sems):
    part = sums.shape[0] // 4
    copies = []
    for i in range(4):
        at = slice(i * part, (i + 1) * part)
        sums[at, :] = (keep_ref[at, :].astype(F32) + other_ref[at, :].astype(F32)).astype(BF16)
        copies.append(pltpu.make_async_copy(sums.at[at], out_hbm.at[at], sems.at[i]))
        copies[-1].start()
    for copy in copies:
        copy.wait()


def spread_body(p0, p1, p2, p3, out_hbm, total, sems):
    even = p0[...].astype(F32) + p2[...].astype(F32)
    odd = p1[...].astype(F32) + p3[...].astype(F32)
    total[...] = (even + odd).astype(BF16)
    copies = []
    for i in range(out_hbm.shape[0]):
        copies.append(pltpu.make_async_copy(total, out_hbm.at[i], sems.at[i]))
        copies[-1].start()
    for copy in copies:
        copy.wait()


def shifted(block, axis, k):
    n = lax.axis_size(axis)
    return lax.ppermute(block, axis, [(i, (i + k) % n) for i in range(n)])


def swapped_far(block):
    n = lax.axis_size(SLAB)
    pairs = [(i, i + 1) for i in range(1, n - 1, 2)]
    return lax.ppermute(block, SLAB, pairs + [(j, i) for i, j in pairs])


def sds(shape, dtype=BF16):
    return jax.ShapeDtypeStruct(shape, dtype)


def shards(grid_x, mesh_h, gain_grid, gain_mesh, w_query, w_key, w_value, w_out, edge_bias,
           neighbours, valid, send_rows, out_grad):
    points, width = grid_x.shape
    nodes, fan = neighbours.shape
    cap = send_rows.shape[3]
    block = 4 * cap
    slots = 3 * block
    heads = edge_bias.shape[1] // fan
    sub1 = lax.axis_index("z").astype(jnp.int32).reshape(1)
    core1 = lax.axis_index("gc").astype(jnp.int32).reshape(1)
    gain_g, gain_m = gain_grid.reshape(1, width), gain_mesh.reshape(1, width)
    (grid_x, mesh_h, out_grad, send_rows, w_key, w_value, w_query, w_out, gain_g, gain_m, edge_bias,
     neighbours, valid) = (
        pltpu.with_memory_space_constraint(a, pltpu.HBM)
        for a in (grid_x, mesh_h, out_grad, send_rows, w_key, w_value, w_query, w_out, gain_g, gain_m,
                  edge_bias, neighbours, valid)
    )

    piece = sds((3, cap, width))
    b0, b1, b2, b3 = call(
        gather_body, [piece] * 4, [SM, HB, HB, HB],
        (sub1, send_rows, gain_g, grid_x), 1 << 30, 4 << 20, "gather_rows",
        held(send_rows, gain_g, grid_x)[:-1] + [pltpu.SemaphoreType.DMA((4,))],
    )
    b1, b2, b3 = (shifted(b, "z", k) for k, b in ((1, b1), (2, b2), (3, b3)))
    sub2, b0 = lax.optimization_barrier((sub1, b0))
    prep_args = (mesh_h, gain_m, w_query, w_out, out_grad, neighbours, valid, edge_bias)
    mesh_normed, queries, att_grad, dense = call(
        prep_body,
        [sds((nodes, width))] * 3 + [sds((heads, nodes, slots), F32)],
        [SM] + [HB] * 8, (sub2, *prep_args), 1 << 30, 8 << 20, "prep",
        [pltpu.VMEM((nodes * 8, 128), F32), pltpu.VMEM((heads, nodes, 128), F32)]
        + held(neighbours, valid, edge_bias, mesh_h, gain_m, w_query, w_out, out_grad),
    )
    b1, b2, b3, dense = lax.optimization_barrier((b1, b2, b3, dense))

    def packed(near_if_first, *pieces):
        body = functools.partial(pack_body, near_if_first)
        return call(body, [sds((block, width))] * 2, [SM] + [VM] * 4, (core1, *pieces), 0, 1 << 20, "pack")

    near, far = packed(2, b0, b1, b2, b3)
    far = swapped_far(far)
    near = shifted(near, "gc", 1)
    keep, send, part_grads, attended, query_grad, weights_near, og_near = call(
        middle_body,
        [sds((2 * width, width))] * 2 + [sds((slots, 2 * width))] + [sds((nodes, width))] * 2
        + [sds((width, 2 * width)), sds((nodes, width))],
        [SM] + [VM] * 10 + [HB] * 3,
        (core1, near, far, b0, b1, b2, b3, queries, att_grad, mesh_normed, dense, w_key, w_value,
         out_grad),
        3 << 30, 8 << 20, "middle",
        [pltpu.VMEM((slots, width), BF16)] * 3 + [pltpu.SemaphoreType.DMA((3,))],
    )

    other = shifted(send, "gc", 1)
    mesh_out, mesh_grad, s0, s1, s2, s3 = call(
        tail_body, [sds((nodes, width))] * 2 + [piece] * 4, [VM] * 5 + [HB] * 4,
        (part_grads, attended, query_grad, weights_near, og_near, w_out, w_query, mesh_h, gain_m),
        1 << 30, 5 << 20, "tail", held(w_out, w_query, mesh_h, gain_m),
    )
    other, s1 = lax.optimization_barrier((other, s1))
    (own,) = call(
        pair_body, [sds((2 * width, width))], [VM] * 2, (keep, other), 1 << 20, 3 << 20, "pair",
        [pltpu.VMEM((2 * width, width), BF16), pltpu.SemaphoreType.DMA((4,))], [HB],
    )
    plane = lax.axis_size(PLANE)
    share = 2 * width // plane
    parts = lax.all_to_all(own.reshape(plane, share, width), PLANE, 0, 0, tiled=True)

    t1, t2, t3 = (shifted(s, "z", -k) for k, s in ((1, s1), (2, s2), (3, s3)))
    near, far = packed(0, s0, t1, t2, t3)
    parts, near, far = lax.optimization_barrier((parts, near, far))
    far = swapped_far(far)
    near = shifted(near, "gc", 1)
    part = jnp.sum(parts.astype(F32), axis=0).astype(BF16)
    p1, p2, p3 = (shifted(part, "z", k) for k in (1, 2, 3))
    p1, near, far = lax.optimization_barrier((p1, near, far))
    (spread,) = call(
        spread_body, [sds((plane, share, width))], [VM] * 4, (part, p1, p2, p3), 1 << 18, 1 << 20,
        "spread", [pltpu.VMEM((share, width), BF16), pltpu.SemaphoreType.DMA((plane,))], [HB],
    )
    mine = lax.all_to_all(spread, PLANE, 0, 0, tiled=True).reshape(2 * width, width)
    (grid_grad,) = call(
        grid_body, [sds((points, width))], [SM] * 2 + [VM] * 6 + [HB] * 3,
        (sub1, core1, near, far, s0, t1, t2, t3, send_rows, gain_g, grid_x),
        1 << 30, 5 << 20, "grid_grad",
        [pltpu.VMEM((slots, width), BF16), pltpu.VMEM((points, width), BF16),
         pltpu.SemaphoreType.DMA((points // 256,))] + held(send_rows, gain_g, grid_x),
        [HB],
    )
    mine, grid_grad = lax.optimization_barrier((mine, grid_grad))
    theirs = shifted(mine, "gc", 1)
    whole = sds((4, width, width), F32)
    wide = [pltpu.VMEM((2, width, width), F32), pltpu.SemaphoreType.DMA((4,))]
    (weight_grads,) = call(
        functools.partial(widen_body, 0), [whole], [SM, VM], (core1, mine), 1 << 20, 3 << 20, "widen_own",
        wide, [HB],
    )
    (weight_grads,) = call(
        functools.partial(widen_body, 1), [whole], [SM, VM, HB], (core1, theirs, weight_grads),
        1 << 20, 3 << 20, "widen_other", wide, [HB], {2: 0},
    )
    return mesh_out, mesh_grad, grid_grad, weight_grads


def solution(mesh):
    split = Mesh(mesh.devices.reshape(4, 4, 2, mesh.shape["sub"]), ALL)
    rows = P(ALL, None)
    return jax.shard_map(
        shards,
        mesh=split,
        in_specs=(rows, rows, P(), P(), P(), P(), P(), P(), rows, rows, rows,
                  P(ALL, None, None, None), rows),
        out_specs=(rows, rows, rows, P()),
        check_vma=False,
    )
```

```python
import functools

import jax
import jax.numpy as jnp
from jax import lax
from jax.experimental import pallas as pl
from jax.experimental.pallas import tpu as pltpu
from jax.sharding import Mesh
from jax.sharding import PartitionSpec as P

SLAB = ("gx", "gy", "gc")
PLANE = ("gx", "gy")
ALL = ("gx", "gy", "gc", "z")

EPSILON = 1e-06
ABSENT = -1e30
F32 = jnp.float32
BF16 = jnp.bfloat16

VM = pl.BlockSpec(memory_space=pltpu.VMEM)
SM = pl.BlockSpec(memory_space=pltpu.SMEM)
HB = pl.BlockSpec(memory_space=pltpu.HBM)


def nn(a, b):
    return lax.dot_general(a, b, (((1,), (0,)), ((), ())), preferred_element_type=F32)


def nt(a, b):
    return lax.dot_general(a, b, (((1,), (1,)), ((), ())), preferred_element_type=F32)


def tn(a, b):
    return lax.dot_general(a, b, (((0,), (0,)), ((), ())), preferred_element_type=F32)


def inv_rms(wide):
    return lax.rsqrt(jnp.mean(wide * wide, axis=-1, keepdims=True) + EPSILON)


def norm_back(wide, factor, gain_row, upstream):
    scaled = gain_row * upstream
    inner = jnp.mean(wide * scaled, axis=-1, keepdims=True)
    return factor * scaled - wide * (factor * factor * factor * inner)


def call(body, outs, in_specs, args, flops, nbytes, name, scratch=(), out_specs=None, aliases=None):
    return pl.pallas_call(
        body,
        out_shape=outs,
        in_specs=in_specs,
        out_specs=out_specs or [VM] * len(outs),
        scratch_shapes=list(scratch),
        input_output_aliases=aliases or {},
        compiler_params=pltpu.CompilerParams(vmem_limit_bytes=24 << 20),
        cost_estimate=pl.CostEstimate(flops=flops, bytes_accessed=nbytes, transcendentals=0),
        name=name,
    )(*args)


def fetch(sources, targets, sems):
    copies = []
    for i, (source, target) in enumerate(zip(sources, targets)):
        copies.append(pltpu.make_async_copy(source, target, sems.at[i]))
        copies[-1].start()
    return copies


def held(*args):
    return [pltpu.VMEM(a.shape, a.dtype) for a in args] + [pltpu.SemaphoreType.DMA((len(args),))]


def assemble(rows, near_first, near, far, own, m1, m2, m3, f1, f2, f3):
    block = near.shape[0]
    cap = block // 4
    near_at = pl.multiple_of((1 - near_first) * (2 * block), block)
    far_at = pl.multiple_of(near_first * (2 * block), block)
    rows[block : block + cap] = own[0:cap]
    rows[pl.ds(near_at, cap), :] = near[0:cap]
    rows[pl.ds(far_at, cap), :] = far[0:cap]
    for k, (mixed, outer) in enumerate(((m1, f1), (m2, f2), (m3, f3)), 1):
        rows[block + k * cap : block + (k + 1) * cap] = mixed[0:cap]
        rows[pl.ds(near_at + k * cap, cap), :] = mixed[cap : 2 * cap]
        rows[pl.ds(far_at + k * cap, cap), :] = outer[...]


def gather_body(sub_ref, core_ref, rows_hbm, gain_hbm, x_hbm, near_ref, far_ref, own_ref,
                rows_ref, gain_ref, x_ref, sems):
    half = x_ref.shape[0] // 2
    cap = rows_ref.shape[3]
    parts = [pl.ds(i * half, half) for i in range(2)]
    copies = fetch(
        [rows_hbm, gain_hbm] + [x_hbm.at[p] for p in parts],
        [rows_ref, gain_ref] + [x_ref.at[p] for p in parts],
        sems,
    )
    copies[0].wait()
    copies[1].wait()
    me = sub_ref[0]
    eye = lax.broadcasted_iota(jnp.int32, (cap, cap), 0) == lax.broadcasted_iota(
        jnp.int32, (cap, cap), 1
    )
    gain = gain_ref[...]
    for step, (o, first, count) in enumerate(((0, 0, half), (2, half, half), (1, 0, 2 * half))):
        cols = []
        for k in range(4):
            s = lax.rem(me + k, 4)
            row = rows_ref[0, o, pl.ds(s, 1), :].astype(F32)
            cols.append(jnp.sum(jnp.where(eye, row, 0.0), axis=1, keepdims=True))
        col = jnp.concatenate(cols, axis=0).astype(jnp.int32) - first
        lanes = lax.broadcasted_iota(jnp.int32, (4 * cap, count), 1)
        onehot = jnp.where(lanes == col, 1.0, 0.0).astype(BF16)
        if step < 2:
            copies[2 + step].wait()
        wide = nn(onehot, x_ref[first : first + count, :])
        normed = (wide * inv_rms(wide) * gain).astype(BF16)
        if o == 1:
            own_ref[...] = normed
            continue
        to_near = core_ref[0] == (2 - o) // 2

        @pl.when(to_near)
        def _():
            near_ref[...] = normed

        @pl.when(jnp.logical_not(to_near))
        def _():
            far_ref[...] = normed


def prep_body(sub_ref, mesh_hbm, gain_hbm, wq_hbm, wo_hbm, og_hbm, nbr_hbm, valid_hbm, bias_hbm,
              normed_ref, q_ref, ag_ref, dense_ref, inv_ref, edge_ref,
              nbr_ref, valid_ref, bias_ref, mesh_ref, gain_ref, wq_ref, wo_ref, og_ref, sems):
    copies = fetch(
        (nbr_hbm, valid_hbm, bias_hbm, mesh_hbm, gain_hbm, wq_hbm, wo_hbm, og_hbm),
        (nbr_ref, valid_ref, bias_ref, mesh_ref, gain_ref, wq_ref, wo_ref, og_ref),
        sems,
    )
    heads, nodes, slots = dense_ref.shape
    fan = nbr_ref.shape[1]
    for copy in copies[:3]:
        copy.wait()
    slot = nbr_ref[...]
    slot = (slot & ~192) | (((sub_ref[0] - (slot >> 6)) & 3) << 6)
    high, low = slot >> 7, slot & 127
    blocks = lax.broadcasted_iota(jnp.int32, (8, fan), 0)
    lanes = lax.broadcasted_iota(jnp.int32, (128, fan), 0)
    edge = lax.broadcasted_iota(jnp.int32, (8, fan), 1).astype(F32) + 1.0
    for m in range(nodes):
        named = jnp.where(high[m : m + 1, :] == blocks, edge, 0.0).astype(BF16)
        places = jnp.where(low[m : m + 1, :] == lanes, 1.0, 0.0).astype(BF16)
        inv_ref[m * 8 : (m + 1) * 8, :] = nt(named, places)
    live = valid_ref[...] == 1
    for h in range(heads):
        edge_ref[h, :, 0:fan] = jnp.where(live, bias_ref[:, h * fan : (h + 1) * fan], ABSENT)
    for b in range(slots // 128):
        at = inv_ref[pl.ds(b, nodes, stride=8), :].astype(jnp.int32) - 1
        here = at >= 0
        at = jnp.maximum(at, 0)
        for h in range(heads):
            got = jnp.take_along_axis(edge_ref[h], at, axis=1, mode="promise_in_bounds")
            dense_ref[h, :, b * 128 : (b + 1) * 128] = jnp.where(here, got, ABSENT)
    for copy in copies[3:]:
        copy.wait()
    wide = mesh_ref[...].astype(F32)
    normed = (wide * inv_rms(wide) * gain_ref[...]).astype(BF16)
    normed_ref[...] = normed
    q_ref[...] = (nn(normed, wq_ref[...]) * (128 ** -0.5)).astype(BF16)
    ag_ref[...] = nt(og_ref[...], wo_ref[...]).astype(BF16)


def middle_body(core_ref, near, far, own, m1, m2, m3, f1, f2, f3, q_ref, ag_ref, mn_ref, bias_ref,
                wk_hbm, wv_hbm, og_hbm, keep_ref, send_ref, part_ref, att_ref, qg_ref,
                wkv_ref, og_ref, rows, keys, vals, sems):
    width = q_ref.shape[1]
    copies = fetch(
        (wk_hbm, wv_hbm, og_hbm),
        (wkv_ref.at[:, pl.ds(0, width)], wkv_ref.at[:, pl.ds(width, width)], og_ref),
        sems,
    )
    heads = bias_ref.shape[0]
    core = core_ref[0]
    assemble(rows, 1 - core, near, far, own, m1, m2, m3, f1, f2, f3)
    copies[0].wait()
    keys[...] = nn(rows[...], wkv_ref[:, :width]).astype(BF16)
    copies[1].wait()
    copies[2].wait()
    vals[...] = nn(rows[...], wkv_ref[:, width:]).astype(BF16)
    for h in range(heads):
        at = slice(h * 128, (h + 1) * 128)
        q, ag = q_ref[:, at], ag_ref[:, at]
        kh, vh = keys[:, at], vals[:, at]
        scores = nt(q, kh) + bias_ref[h]
        peak = jnp.max(scores, axis=1, keepdims=True)
        terms = jnp.exp(scores - peak)
        probs = terms / jnp.sum(terms, axis=1, keepdims=True)
        probs_b = probs.astype(BF16)
        att_ref[:, at] = nn(probs_b, vh).astype(BF16)
        pg = nt(ag, vh)
        sg = (probs * (pg - jnp.sum(probs * pg, axis=1, keepdims=True))).astype(BF16)
        qg_ref[:, at] = (nn(sg, kh) * (128 ** -0.5)).astype(BF16)
        part_ref[:, at] = tn(sg, q).astype(BF16)
        part_ref[:, width + h * 128 : width + (h + 1) * 128] = tn(probs_b, ag).astype(BF16)

    def place(half, row, value):
        @pl.when(core == half)
        def _():
            keep_ref[row : row + width, :] = value

        @pl.when(core != half)
        def _():
            send_ref[row : row + width, :] = value

    both = tn(rows[...], part_ref[...]).astype(BF16)
    place(0, 0, tn(mn_ref[...], qg_ref[...]).astype(BF16))
    place(0, width, both[:, :width])
    place(1, 0, both[:, width:])
    place(1, width, tn(att_ref[...], og_ref[...]).astype(BF16))


def tail_body(core_ref, part_ref, att_ref, qg_ref, wkv_ref, og_ref, wo_hbm, wq_hbm, mesh_hbm,
              gain_hbm, out_ref, grad_ref, near_ref, far_ref, own_ref, back_ref, wo_ref, wq_ref, mesh_ref, gain_ref, sems):
    copies = fetch(
        (wo_hbm, wq_hbm, mesh_hbm, gain_hbm), (wo_ref, wq_ref, mesh_ref, gain_ref), sems
    )
    block = own_ref.shape[0]
    back_ref[...] = nt(part_ref[...], wkv_ref[...]).astype(BF16)
    near_at = core_ref[0] * (2 * block)
    far_at = (1 - core_ref[0]) * (2 * block)
    near_ref[...] = back_ref[pl.ds(pl.multiple_of(near_at, block), block), :]
    far_ref[...] = back_ref[pl.ds(pl.multiple_of(far_at, block), block), :]
    own_ref[...] = back_ref[block : 2 * block, :]
    for copy in copies:
        copy.wait()
    wide = mesh_ref[...].astype(F32)
    out_ref[...] = (wide + nn(att_ref[...], wo_ref[...])).astype(BF16)
    upstream = nt(qg_ref[...], wq_ref[...])
    back = norm_back(wide, inv_rms(wide), gain_ref[...], upstream)
    grad_ref[...] = (og_ref[...].astype(F32) + back).astype(BF16)


def mix_body(own, near, m1, m2, m3):
    cap = m1.shape[0] // 2
    for k, mixed in enumerate((m1, m2, m3), 1):
        mixed[0:cap] = own[k * cap : (k + 1) * cap]
        mixed[cap : 2 * cap] = near[k * cap : (k + 1) * cap]


def split_body(block, f1, f2, f3):
    cap = f1.shape[0]
    for k, piece in enumerate((f1, f2, f3), 1):
        piece[...] = block[k * cap : (k + 1) * cap]


def grid_body(sub_ref, core_ref, near, far, own, m1, m2, m3, f1, f2, f3, rows_hbm, gain_hbm, x_hbm, out_hbm,
              got, done_ref, done_sems, rows_ref, gain_ref, x_ref, sems):
    copies = fetch((rows_hbm, gain_hbm, x_hbm), (rows_ref, gain_ref, x_ref), sems)
    points = x_ref.shape[0]
    half = points // 2
    cap = rows_ref.shape[3]
    block = 4 * cap
    me = sub_ref[0]
    assemble(got, core_ref[0], near, far, own, m1, m2, m3, f1, f2, f3)
    for copy in copies:
        copy.wait()
    gain = gain_ref[...]
    idx = []
    for o in range(3):
        for k in range(4):
            idx.append(rows_ref[0, o, pl.ds(lax.rem(me + k, 4), 1), :])
    idx = jnp.concatenate(idx, axis=1)
    tile = 256
    stores = []
    for t in range(points // tile):
        first = t * tile
        low = 0 if first < half else block
        ids = lax.broadcasted_iota(jnp.int32, (tile, 2 * block), 0) + first
        onehot = jnp.where(ids == idx[:, low : low + 2 * block], 1.0, 0.0).astype(BF16)
        upstream = nn(onehot, got[low : low + 2 * block, :])
        wide = x_ref[first : first + tile, :].astype(F32)
        part = slice(first, first + tile)
        done_ref[part, :] = norm_back(wide, inv_rms(wide), gain, upstream).astype(BF16)
        stores.append(
            pltpu.make_async_copy(done_ref.at[part], out_hbm.at[part], done_sems.at[t])
        )
        stores[-1].start()
    for store in stores:
        store.wait()


def widen_body(turn, core_ref, half_ref, *refs):
    out_hbm, wide, sems = refs[-3:]
    count, width, _ = wide.shape
    first = (core_ref[0] ^ turn) * count
    part = width // 2
    copies = []
    for i in range(2 * count):
        m, rows = i // 2, pl.ds((i % 2) * part, part)
        wide[m, rows, :] = half_ref[i * part : (i + 1) * part, :].astype(F32)
        copies.append(
            pltpu.make_async_copy(wide.at[m, rows], out_hbm.at[first + m, rows], sems.at[i])
        )
        copies[-1].start()
    for copy in copies:
        copy.wait()


def pair_body(keep_ref, other_ref, out_hbm, sums, sems):
    part = sums.shape[0] // 4
    copies = []
    for i in range(4):
        at = slice(i * part, (i + 1) * part)
        sums[at, :] = (keep_ref[at, :].astype(F32) + other_ref[at, :].astype(F32)).astype(BF16)
        copies.append(pltpu.make_async_copy(sums.at[at], out_hbm.at[at], sems.at[i]))
        copies[-1].start()
    for copy in copies:
        copy.wait()


def spread_body(p0, p1, p2, p3, out_hbm, total, sems):
    even = p0[...].astype(F32) + p2[...].astype(F32)
    odd = p1[...].astype(F32) + p3[...].astype(F32)
    total[...] = (even + odd).astype(BF16)
    copies = []
    for i in range(out_hbm.shape[0]):
        copies.append(pltpu.make_async_copy(total, out_hbm.at[i], sems.at[i]))
        copies[-1].start()
    for copy in copies:
        copy.wait()


def shifted(block, axis, k):
    n = lax.axis_size(axis)
    return lax.ppermute(block, axis, [(i, (i + k) % n) for i in range(n)])


def swapped_far(block):
    n = lax.axis_size(SLAB)
    pairs = [(i, i + 1) for i in range(1, n - 1, 2)]
    return lax.ppermute(block, SLAB, pairs + [(j, i) for i, j in pairs])


def sds(shape, dtype=BF16):
    return jax.ShapeDtypeStruct(shape, dtype)


def shards(grid_x, mesh_h, gain_grid, gain_mesh, w_query, w_key, w_value, w_out, edge_bias,
           neighbours, valid, send_rows, out_grad):
    points, width = grid_x.shape
    nodes, fan = neighbours.shape
    cap = send_rows.shape[3]
    block = 4 * cap
    slots = 3 * block
    heads = edge_bias.shape[1] // fan
    sub1 = lax.axis_index("z").astype(jnp.int32).reshape(1)
    core1 = lax.axis_index("gc").astype(jnp.int32).reshape(1)
    gain_g, gain_m = gain_grid.reshape(1, width), gain_mesh.reshape(1, width)
    (grid_x, mesh_h, out_grad, send_rows, w_key, w_value, w_query, w_out, gain_g, gain_m, edge_bias,
     neighbours, valid) = (
        pltpu.with_memory_space_constraint(a, pltpu.HBM)
        for a in (grid_x, mesh_h, out_grad, send_rows, w_key, w_value, w_query, w_out, gain_g, gain_m,
                  edge_bias, neighbours, valid)
    )

    one, two, four = sds((cap, width)), sds((2 * cap, width)), sds((block, width))
    near, far, own = call(
        gather_body, [four] * 3, [SM, SM, HB, HB, HB],
        (sub1, core1, send_rows, gain_g, grid_x), 1 << 30, 4 << 20, "gather_rows",
        held(send_rows, gain_g, grid_x)[:-1] + [pltpu.SemaphoreType.DMA((4,))],
    )

    def exchange(near, far, own, sign):
        far = swapped_far(far)
        near = shifted(near, "gc", 1)
        mixed = call(mix_body, [two] * 3, [VM] * 2, (own, near), 0, 1 << 20, "mix")
        mixed = [shifted(m, "z", sign * k) for k, m in enumerate(mixed, 1)]
        far, mixed[0] = lax.optimization_barrier((far, mixed[0]))
        outer = call(split_body, [one] * 3, [VM], (far,), 0, 1 << 19, "split")
        outer = [shifted(f, "z", sign * k) for k, f in enumerate(outer, 1)]
        return near, far, own, *mixed, *outer

    received = exchange(near, far, own, 1)
    sub2, near = lax.optimization_barrier((sub1, received[1]))
    prep_args = (mesh_h, gain_m, w_query, w_out, out_grad, neighbours, valid, edge_bias)
    mesh_normed, queries, att_grad, dense = call(
        prep_body,
        [sds((nodes, width))] * 3 + [sds((heads, nodes, slots), F32)],
        [SM] + [HB] * 8, (sub2, *prep_args), 1 << 30, 8 << 20, "prep",
        [pltpu.VMEM((nodes * 8, 128), F32), pltpu.VMEM((heads, nodes, 128), F32)]
        + held(neighbours, valid, edge_bias, mesh_h, gain_m, w_query, w_out, out_grad),
    )
    keep, send, part_grads, attended, query_grad, weights_near, og_near = call(
        middle_body,
        [sds((2 * width, width))] * 2 + [sds((slots, 2 * width))] + [sds((nodes, width))] * 2
        + [sds((width, 2 * width)), sds((nodes, width))],
        [SM] + [VM] * 13 + [HB] * 3,
        (core1, *received, queries, att_grad, mesh_normed, dense, w_key, w_value,
         out_grad),
        3 << 30, 8 << 20, "middle",
        [pltpu.VMEM((slots, width), BF16)] * 3 + [pltpu.SemaphoreType.DMA((3,))],
    )

    other = shifted(send, "gc", 1)
    mesh_out, mesh_grad, near, far, back_own = call(
        tail_body, [sds((nodes, width))] * 2 + [four] * 3, [SM] + [VM] * 5 + [HB] * 4,
        (core1, part_grads, attended, query_grad, weights_near, og_near, w_out, w_query, mesh_h, gain_m),
        1 << 30, 5 << 20, "tail",
        [pltpu.VMEM((slots, width), BF16)] + held(w_out, w_query, mesh_h, gain_m),
    )
    other, near = lax.optimization_barrier((other, near))
    (own,) = call(
        pair_body, [sds((2 * width, width))], [VM] * 2, (keep, other), 1 << 20, 3 << 20, "pair",
        [pltpu.VMEM((2 * width, width), BF16), pltpu.SemaphoreType.DMA((4,))], [HB],
    )
    plane = lax.axis_size(PLANE)
    share = 2 * width // plane
    parts = lax.all_to_all(own.reshape(plane, share, width), PLANE, 0, 0, tiled=True)

    returned = exchange(near, far, back_own, -1)
    parts, *returned = lax.optimization_barrier((parts, *returned))
    part = jnp.sum(parts.astype(F32), axis=0).astype(BF16)
    p1, p2, p3 = (shifted(part, "z", k) for k in (1, 2, 3))
    (spread,) = call(
        spread_body, [sds((plane, share, width))], [VM] * 4, (part, p1, p2, p3), 1 << 18, 1 << 20,
        "spread", [pltpu.VMEM((share, width), BF16), pltpu.SemaphoreType.DMA((plane,))], [HB],
    )
    mine = lax.all_to_all(spread, PLANE, 0, 0, tiled=True).reshape(2 * width, width)
    (grid_grad,) = call(
        grid_body, [sds((points, width))], [SM] * 2 + [VM] * 9 + [HB] * 3,
        (sub1, core1, *returned, send_rows, gain_g, grid_x),
        1 << 30, 5 << 20, "grid_grad",
        [pltpu.VMEM((slots, width), BF16), pltpu.VMEM((points, width), BF16),
         pltpu.SemaphoreType.DMA((points // 256,))] + held(send_rows, gain_g, grid_x),
        [HB],
    )
    mine, grid_grad = lax.optimization_barrier((mine, grid_grad))
    theirs = shifted(mine, "gc", 1)
    whole = sds((4, width, width), F32)
    wide = [pltpu.VMEM((2, width, width), F32), pltpu.SemaphoreType.DMA((4,))]
    (weight_grads,) = call(
        functools.partial(widen_body, 0), [whole], [SM, VM], (core1, mine), 1 << 20, 3 << 20, "widen_own",
        wide, [HB],
    )
    (weight_grads,) = call(
        functools.partial(widen_body, 1), [whole], [SM, VM, HB], (core1, theirs, weight_grads),
        1 << 20, 3 << 20, "widen_other", wide, [HB], {2: 0},
    )
    return mesh_out, mesh_grad, grid_grad, weight_grads


def solution(mesh):
    split = Mesh(mesh.devices.reshape(4, 4, 2, mesh.shape["sub"]), ALL)
    rows = P(ALL, None)
    return jax.shard_map(
        shards,
        mesh=split,
        in_specs=(rows, rows, P(), P(), P(), P(), P(), P(), rows, rows, rows,
                  P(ALL, None, None, None), rows),
        out_specs=(rows, rows, rows, P()),
        check_vma=False,
    )
```

```python
import functools

import jax
import jax.numpy as jnp
from jax import lax
from jax.experimental import pallas as pl
from jax.experimental.pallas import tpu as pltpu
from jax.sharding import Mesh
from jax.sharding import PartitionSpec as P

SLAB = ("gx", "gy", "gc")
PLANE = ("gx", "gy")
ALL = ("gx", "gy", "gc", "z")

EPSILON = 1e-06
ABSENT = -1e30
F32 = jnp.float32
BF16 = jnp.bfloat16

VM = pl.BlockSpec(memory_space=pltpu.VMEM)
SM = pl.BlockSpec(memory_space=pltpu.SMEM)
HB = pl.BlockSpec(memory_space=pltpu.HBM)


def nn(a, b):
    return lax.dot_general(a, b, (((1,), (0,)), ((), ())), preferred_element_type=F32)


def nt(a, b):
    return lax.dot_general(a, b, (((1,), (1,)), ((), ())), preferred_element_type=F32)


def tn(a, b):
    return lax.dot_general(a, b, (((0,), (0,)), ((), ())), preferred_element_type=F32)


def inv_rms(wide):
    return lax.rsqrt(jnp.mean(wide * wide, axis=-1, keepdims=True) + EPSILON)


def norm_back(wide, factor, gain_row, upstream):
    scaled = gain_row * upstream
    inner = jnp.mean(wide * scaled, axis=-1, keepdims=True)
    return factor * scaled - wide * (factor * factor * factor * inner)


def call(body, outs, in_specs, args, flops, nbytes, name, scratch=(), out_specs=None, aliases=None):
    return pl.pallas_call(
        body,
        out_shape=outs,
        in_specs=in_specs,
        out_specs=out_specs or [VM] * len(outs),
        scratch_shapes=list(scratch),
        input_output_aliases=aliases or {},
        compiler_params=pltpu.CompilerParams(vmem_limit_bytes=24 << 20),
        cost_estimate=pl.CostEstimate(flops=flops, bytes_accessed=nbytes, transcendentals=0),
        name=name,
    )(*args)


def fetch(sources, targets, sems):
    copies = []
    for i, (source, target) in enumerate(zip(sources, targets)):
        copies.append(pltpu.make_async_copy(source, target, sems.at[i]))
        copies[-1].start()
    return copies


def held(*args):
    return [pltpu.VMEM(a.shape, a.dtype) for a in args] + [pltpu.SemaphoreType.DMA((len(args),))]


def assemble(rows, near_first, near, far, own, *pieces):
    block = near.shape[0]
    cap = block // 4
    near_at = pl.multiple_of((1 - near_first) * (2 * block), block)
    far_at = pl.multiple_of(near_first * (2 * block), block)
    rows[block : block + cap] = own[0:cap]
    rows[pl.ds(near_at, cap), :] = near[0:cap]
    rows[pl.ds(far_at, cap), :] = far[0:cap]
    for k in range(1, 4):
        mixed, last = pieces[k - 1], pieces[len(pieces) - 4 + k]
        rows[block + k * cap : block + (k + 1) * cap] = mixed[0:cap]
        rows[pl.ds(near_at + k * cap, cap), :] = mixed[cap : 2 * cap]
        rows[pl.ds(far_at + k * cap, cap), :] = last[last.shape[0] - cap :]


def gather_body(sub_ref, core_ref, rows_hbm, gain_hbm, x_hbm, near_ref, far_ref, own_ref,
                rows_ref, gain_ref, x_ref, sems):
    half = x_ref.shape[0] // 2
    cap = rows_ref.shape[3]
    core = core_ref[0]
    firsts = [pl.multiple_of((1 - core) * half, half), pl.multiple_of(core * half, half)]
    parts = [pl.ds(first, half) for first in firsts]
    copies = fetch(
        [rows_hbm, gain_hbm] + [x_hbm.at[p] for p in parts],
        [rows_ref, gain_ref] + [x_ref.at[p] for p in parts],
        sems,
    )
    copies[0].wait()
    copies[1].wait()
    me = sub_ref[0]
    eye = lax.broadcasted_iota(jnp.int32, (cap, cap), 0) == lax.broadcasted_iota(
        jnp.int32, (cap, cap), 1
    )
    gain = gain_ref[...]
    steps = (
        (2 - 2 * core, firsts[0], half, near_ref),
        (2 * core, firsts[1], half, far_ref),
        (1, 0, 2 * half, own_ref),
    )
    for step, (o, first, count, out_ref) in enumerate(steps):
        cols = []
        for k in range(4):
            s = lax.rem(me + k, 4)
            row = rows_ref[0, o, pl.ds(s, 1), :].astype(F32)
            cols.append(jnp.sum(jnp.where(eye, row, 0.0), axis=1, keepdims=True))
        col = jnp.concatenate(cols, axis=0).astype(jnp.int32) - first
        lanes = lax.broadcasted_iota(jnp.int32, (4 * cap, count), 1)
        onehot = jnp.where(lanes == col, 1.0, 0.0).astype(BF16)
        if step < 2:
            copies[2 + step].wait()
        wide = nn(onehot, x_ref[pl.ds(first, count), :])
        out_ref[...] = (wide * inv_rms(wide) * gain).astype(BF16)


def prep_body(sub_ref, mesh_hbm, gain_hbm, wq_hbm, wo_hbm, og_hbm, nbr_hbm, valid_hbm, bias_hbm,
              normed_ref, q_ref, ag_ref, dense_ref, inv_ref, edge_ref,
              nbr_ref, valid_ref, bias_ref, mesh_ref, gain_ref, wq_ref, wo_ref, og_ref, sems):
    copies = fetch(
        (nbr_hbm, valid_hbm, bias_hbm, mesh_hbm, gain_hbm, wq_hbm, wo_hbm, og_hbm),
        (nbr_ref, valid_ref, bias_ref, mesh_ref, gain_ref, wq_ref, wo_ref, og_ref),
        sems,
    )
    heads, nodes, slots = dense_ref.shape
    fan = nbr_ref.shape[1]
    for copy in copies[:3]:
        copy.wait()
    slot = nbr_ref[...]
    slot = (slot & ~192) | (((sub_ref[0] - (slot >> 6)) & 3) << 6)
    high, low = slot >> 7, slot & 127
    blocks = lax.broadcasted_iota(jnp.int32, (8, fan), 0)
    lanes = lax.broadcasted_iota(jnp.int32, (128, fan), 0)
    edge = lax.broadcasted_iota(jnp.int32, (8, fan), 1).astype(F32) + 1.0
    for m in range(nodes):
        named = jnp.where(high[m : m + 1, :] == blocks, edge, 0.0).astype(BF16)
        places = jnp.where(low[m : m + 1, :] == lanes, 1.0, 0.0).astype(BF16)
        inv_ref[m * 8 : (m + 1) * 8, :] = nt(named, places)
    live = valid_ref[...] == 1
    for h in range(heads):
        edge_ref[h, :, 0:fan] = jnp.where(live, bias_ref[:, h * fan : (h + 1) * fan], ABSENT)
    for b in range(slots // 128):
        at = inv_ref[pl.ds(b, nodes, stride=8), :].astype(jnp.int32) - 1
        here = at >= 0
        at = jnp.maximum(at, 0)
        for h in range(heads):
            got = jnp.take_along_axis(edge_ref[h], at, axis=1, mode="promise_in_bounds")
            dense_ref[h, :, b * 128 : (b + 1) * 128] = jnp.where(here, got, ABSENT)
    for copy in copies[3:]:
        copy.wait()
    wide = mesh_ref[...].astype(F32)
    normed = (wide * inv_rms(wide) * gain_ref[...]).astype(BF16)
    normed_ref[...] = normed
    q_ref[...] = (nn(normed, wq_ref[...]) * (128 ** -0.5)).astype(BF16)
    ag_ref[...] = nt(og_ref[...], wo_ref[...]).astype(BF16)


def middle_body(core_ref, near, far, own, m1, m2, m3, f1, f2, f3, q_ref, ag_ref, mn_ref, bias_ref,
                wk_hbm, wv_hbm, og_hbm, keep_ref, send_ref, part_ref, att_ref, qg_ref,
                wkv_ref, og_ref, rows, keys, vals, sems):
    width = q_ref.shape[1]
    copies = fetch(
        (wk_hbm, wv_hbm, og_hbm),
        (wkv_ref.at[:, pl.ds(0, width)], wkv_ref.at[:, pl.ds(width, width)], og_ref),
        sems,
    )
    heads = bias_ref.shape[0]
    core = core_ref[0]
    assemble(rows, 1 - core, near, far, own, m1, m2, m3, f1, f2, f3)
    copies[0].wait()
    keys[...] = nn(rows[...], wkv_ref[:, :width]).astype(BF16)
    copies[1].wait()
    copies[2].wait()
    vals[...] = nn(rows[...], wkv_ref[:, width:]).astype(BF16)
    for h in range(heads):
        at = slice(h * 128, (h + 1) * 128)
        q, ag = q_ref[:, at], ag_ref[:, at]
        kh, vh = keys[:, at], vals[:, at]
        scores = nt(q, kh) + bias_ref[h]
        peak = jnp.max(scores, axis=1, keepdims=True)
        terms = jnp.exp(scores - peak)
        probs = terms / jnp.sum(terms, axis=1, keepdims=True)
        probs_b = probs.astype(BF16)
        att_ref[:, at] = nn(probs_b, vh).astype(BF16)
        pg = nt(ag, vh)
        sg = (probs * (pg - jnp.sum(probs * pg, axis=1, keepdims=True))).astype(BF16)
        qg_ref[:, at] = (nn(sg, kh) * (128 ** -0.5)).astype(BF16)
        part_ref[:, at] = tn(sg, q).astype(BF16)
        part_ref[:, width + h * 128 : width + (h + 1) * 128] = tn(probs_b, ag).astype(BF16)

    def place(half, row, value):
        @pl.when(core == half)
        def _():
            keep_ref[row : row + width, :] = value

        @pl.when(core != half)
        def _():
            send_ref[row : row + width, :] = value

    both = tn(rows[...], part_ref[...]).astype(BF16)
    place(0, 0, tn(mn_ref[...], qg_ref[...]).astype(BF16))
    place(0, width, both[:, :width])
    place(1, 0, both[:, width:])
    place(1, width, tn(att_ref[...], og_ref[...]).astype(BF16))


def back_body(part_ref, wkv_ref, s0, s1, s2, s3):
    cap = s0.shape[1]
    for o in range(3):
        rows = slice(o * 4 * cap, (o + 1) * 4 * cap)
        back = nt(part_ref[rows, :], wkv_ref[...]).astype(BF16)
        for k, piece in enumerate((s0, s1, s2, s3)):
            piece[o] = back[k * cap : (k + 1) * cap]


def mesh_body(att_ref, qg_ref, og_ref, wo_hbm, wq_hbm, mesh_hbm, gain_hbm, out_ref, grad_ref,
              wo_ref, wq_ref, mesh_ref, gain_ref, sems):
    copies = fetch(
        (wo_hbm, wq_hbm, mesh_hbm, gain_hbm), (wo_ref, wq_ref, mesh_ref, gain_ref), sems
    )
    for copy in copies:
        copy.wait()
    wide = mesh_ref[...].astype(F32)
    out_ref[...] = (wide + nn(att_ref[...], wo_ref[...])).astype(BF16)
    upstream = nt(qg_ref[...], wq_ref[...])
    back = norm_back(wide, inv_rms(wide), gain_ref[...], upstream)
    grad_ref[...] = (og_ref[...].astype(F32) + back).astype(BF16)


def pack_body(core_ref, p0, p1, p2, p3, near_ref, far_ref):
    cap = p0.shape[1]
    near = core_ref[0] * 2
    for k, piece in enumerate((p0, p1, p2, p3)):
        near_ref[k * cap : (k + 1) * cap, :] = piece[near]
        far_ref[k * cap : (k + 1) * cap, :] = piece[2 - near]


def mix_body(own, near, m1, m2, m3):
    cap = m1.shape[0] // 2
    for k, mixed in enumerate((m1, m2, m3), 1):
        mixed[0:cap] = own[k * cap : (k + 1) * cap]
        mixed[cap : 2 * cap] = near[k * cap : (k + 1) * cap]


def split_body(block, f1, f2, f3):
    cap = f1.shape[0]
    for k, piece in enumerate((f1, f2, f3), 1):
        piece[...] = block[k * cap : (k + 1) * cap]


def grid_body(sub_ref, core_ref, near, far, s0, s1, s2, s3, rows_hbm, gain_hbm, x_hbm, out_hbm,
              got, done_ref, done_sems, rows_ref, gain_ref, x_ref, sems):
    copies = fetch((rows_hbm, gain_hbm, x_hbm), (rows_ref, gain_ref, x_ref), sems)
    points = x_ref.shape[0]
    half = points // 2
    cap = rows_ref.shape[3]
    block = 4 * cap
    me = sub_ref[0]
    core = core_ref[0]
    got[pl.ds(pl.multiple_of((1 - core) * (2 * block), block), block), :] = near[...]
    got[pl.ds(pl.multiple_of(core * (2 * block), block), block), :] = far[...]
    for k, piece in enumerate((s0, s1, s2, s3)):
        got[block + k * cap : block + (k + 1) * cap] = piece[1]
    for copy in copies:
        copy.wait()
    gain = gain_ref[...]
    idx = []
    for o in range(3):
        for k in range(4):
            idx.append(rows_ref[0, o, pl.ds(lax.rem(me + k, 4), 1), :])
    idx = jnp.concatenate(idx, axis=1)
    tile = 256
    stores = []
    for t in range(points // tile):
        first = t * tile
        low = 0 if first < half else block
        ids = lax.broadcasted_iota(jnp.int32, (tile, 2 * block), 0) + first
        onehot = jnp.where(ids == idx[:, low : low + 2 * block], 1.0, 0.0).astype(BF16)
        upstream = nn(onehot, got[low : low + 2 * block, :])
        wide = x_ref[first : first + tile, :].astype(F32)
        part = slice(first, first + tile)
        done_ref[part, :] = norm_back(wide, inv_rms(wide), gain, upstream).astype(BF16)
        stores.append(
            pltpu.make_async_copy(done_ref.at[part], out_hbm.at[part], done_sems.at[t])
        )
        stores[-1].start()
    for store in stores:
        store.wait()


def widen_body(turn, core_ref, half_ref, *refs):
    out_hbm, wide, sems = refs[-3:]
    count, width, _ = wide.shape
    first = (core_ref[0] ^ turn) * count
    part = width // 2
    copies = []
    for i in range(2 * count):
        m, rows = i // 2, pl.ds((i % 2) * part, part)
        wide[m, rows, :] = half_ref[i * part : (i + 1) * part, :].astype(F32)
        copies.append(
            pltpu.make_async_copy(wide.at[m, rows], out_hbm.at[first + m, rows], sems.at[i])
        )
        copies[-1].start()
    for copy in copies:
        copy.wait()


def pair_body(keep_ref, other_ref, out_hbm, sums, sems):
    part = sums.shape[0] // 4
    copies = []
    for i in range(4):
        at = slice(i * part, (i + 1) * part)
        sums[at, :] = (keep_ref[at, :].astype(F32) + other_ref[at, :].astype(F32)).astype(BF16)
        copies.append(pltpu.make_async_copy(sums.at[at], out_hbm.at[at], sems.at[i]))
        copies[-1].start()
    for copy in copies:
        copy.wait()


def spread_body(p0, p1, p2, p3, out_hbm, total, sems):
    even = p0[...].astype(F32) + p2[...].astype(F32)
    odd = p1[...].astype(F32) + p3[...].astype(F32)
    total[...] = (even + odd).astype(BF16)
    copies = []
    for i in range(out_hbm.shape[0]):
        copies.append(pltpu.make_async_copy(total, out_hbm.at[i], sems.at[i]))
        copies[-1].start()
    for copy in copies:
        copy.wait()


def shifted(block, axis, k):
    n = lax.axis_size(axis)
    return lax.ppermute(block, axis, [(i, (i + k) % n) for i in range(n)])


def swapped_far(block):
    n = lax.axis_size(SLAB)
    pairs = [(i, i + 1) for i in range(1, n - 1, 2)]
    return lax.ppermute(block, SLAB, pairs + [(j, i) for i, j in pairs])


def sds(shape, dtype=BF16):
    return jax.ShapeDtypeStruct(shape, dtype)


def shards(grid_x, mesh_h, gain_grid, gain_mesh, w_query, w_key, w_value, w_out, edge_bias,
           neighbours, valid, send_rows, out_grad):
    points, width = grid_x.shape
    nodes, fan = neighbours.shape
    cap = send_rows.shape[3]
    block = 4 * cap
    slots = 3 * block
    heads = edge_bias.shape[1] // fan
    sub1 = lax.axis_index("z").astype(jnp.int32).reshape(1)
    core1 = lax.axis_index("gc").astype(jnp.int32).reshape(1)
    gain_g, gain_m = gain_grid.reshape(1, width), gain_mesh.reshape(1, width)
    (grid_x, mesh_h, out_grad, send_rows, w_key, w_value, w_query, w_out, gain_g, gain_m, edge_bias,
     neighbours, valid) = (
        pltpu.with_memory_space_constraint(a, pltpu.HBM)
        for a in (grid_x, mesh_h, out_grad, send_rows, w_key, w_value, w_query, w_out, gain_g, gain_m,
                  edge_bias, neighbours, valid)
    )

    one, two, four = sds((cap, width)), sds((2 * cap, width)), sds((block, width))
    near, far, own = call(
        gather_body, [four] * 3, [SM, SM, HB, HB, HB],
        (sub1, core1, send_rows, gain_g, grid_x), 1 << 30, 4 << 20, "gather_rows",
        held(send_rows, gain_g, grid_x)[:-1] + [pltpu.SemaphoreType.DMA((4,))],
    )

    far = swapped_far(far)
    near = shifted(near, "gc", 1)
    mixed = call(mix_body, [two] * 3, [VM] * 2, (own, near), 0, 1 << 20, "mix")
    mixed = [shifted(m, "z", k) for k, m in enumerate(mixed, 1)]
    far, mixed[0] = lax.optimization_barrier((far, mixed[0]))
    outer = call(split_body, [one] * 3, [VM], (far,), 0, 1 << 19, "split")
    outer = [shifted(f, "z", k) for k, f in enumerate(outer, 1)]
    received = near, far, own, *mixed, *outer
    sub2, far = lax.optimization_barrier((sub1, far))
    prep_args = (mesh_h, gain_m, w_query, w_out, out_grad, neighbours, valid, edge_bias)
    mesh_normed, queries, att_grad, dense = call(
        prep_body,
        [sds((nodes, width))] * 3 + [sds((heads, nodes, slots), F32)],
        [SM] + [HB] * 8, (sub2, *prep_args), 1 << 30, 8 << 20, "prep",
        [pltpu.VMEM((nodes * 8, 128), F32), pltpu.VMEM((heads, nodes, 128), F32)]
        + held(neighbours, valid, edge_bias, mesh_h, gain_m, w_query, w_out, out_grad),
    )
    keep, send, part_grads, attended, query_grad, weights_near, og_near = call(
        middle_body,
        [sds((2 * width, width))] * 2 + [sds((slots, 2 * width))] + [sds((nodes, width))] * 2
        + [sds((width, 2 * width)), sds((nodes, width))],
        [SM] + [VM] * 13 + [HB] * 3,
        (core1, *received, queries, att_grad, mesh_normed, dense, w_key, w_value,
         out_grad),
        3 << 30, 8 << 20, "middle",
        [pltpu.VMEM((slots, width), BF16)] * 3 + [pltpu.SemaphoreType.DMA((3,))],
    )

    other = shifted(send, "gc", 1)
    s0, s1, s2, s3 = call(
        back_body, [sds((3, cap, width))] * 4, [VM] * 2, (part_grads, weights_near),
        1 << 30, 3 << 20, "back",
    )
    other, s1 = lax.optimization_barrier((other, s1))
    (own,) = call(
        pair_body, [sds((2 * width, width))], [VM] * 2, (keep, other), 1 << 20, 3 << 20, "pair",
        [pltpu.VMEM((2 * width, width), BF16), pltpu.SemaphoreType.DMA((4,))], [HB],
    )
    plane = lax.axis_size(PLANE)
    share = 2 * width // plane
    parts = lax.all_to_all(own.reshape(plane, share, width), PLANE, 0, 0, tiled=True)

    attended, own = lax.optimization_barrier((attended, own))
    mesh_out, mesh_grad = call(
        mesh_body, [sds((nodes, width))] * 2, [VM] * 3 + [HB] * 4,
        (attended, query_grad, og_near, w_out, w_query, mesh_h, gain_m), 1 << 28, 2 << 20, "mesh",
        held(w_out, w_query, mesh_h, gain_m),
    )
    s1, s2, s3 = (shifted(s, "z", -k) for k, s in ((1, s1), (2, s2), (3, s3)))
    s1, mesh_out = lax.optimization_barrier((s1, mesh_out))
    near, far = call(
        pack_body, [four] * 2, [SM] + [VM] * 4, (core1, s0, s1, s2, s3), 0, 1 << 20, "pack"
    )
    far = swapped_far(far)
    near = shifted(near, "gc", 1)
    parts, near = lax.optimization_barrier((parts, near))
    part = jnp.sum(parts.astype(F32), axis=0).astype(BF16)
    p1, p2, p3 = (shifted(part, "z", k) for k in (1, 2, 3))
    p1, far = lax.optimization_barrier((p1, far))
    (spread,) = call(
        spread_body, [sds((plane, share, width))], [VM] * 4, (part, p1, p2, p3), 1 << 18, 1 << 20,
        "spread", [pltpu.VMEM((share, width), BF16), pltpu.SemaphoreType.DMA((plane,))], [HB],
    )
    mine = lax.all_to_all(spread, PLANE, 0, 0, tiled=True).reshape(2 * width, width)
    (grid_grad,) = call(
        grid_body, [sds((points, width))], [SM] * 2 + [VM] * 6 + [HB] * 3,
        (sub1, core1, near, far, s0, s1, s2, s3, send_rows, gain_g, grid_x),
        1 << 30, 5 << 20, "grid_grad",
        [pltpu.VMEM((slots, width), BF16), pltpu.VMEM((points, width), BF16),
         pltpu.SemaphoreType.DMA((points // 256,))] + held(send_rows, gain_g, grid_x),
        [HB],
    )
    mine, grid_grad = lax.optimization_barrier((mine, grid_grad))
    theirs = shifted(mine, "gc", 1)
    whole = sds((4, width, width), F32)
    wide = [pltpu.VMEM((2, width, width), F32), pltpu.SemaphoreType.DMA((4,))]
    (weight_grads,) = call(
        functools.partial(widen_body, 0), [whole], [SM, VM], (core1, mine), 1 << 20, 3 << 20, "widen_own",
        wide, [HB],
    )
    (weight_grads,) = call(
        functools.partial(widen_body, 1), [whole], [SM, VM, HB], (core1, theirs, weight_grads),
        1 << 20, 3 << 20, "widen_other", wide, [HB], {2: 0},
    )
    return mesh_out, mesh_grad, grid_grad, weight_grads


def solution(mesh):
    split = Mesh(mesh.devices.reshape(4, 4, 2, mesh.shape["sub"]), ALL)
    rows = P(ALL, None)
    return jax.shard_map(
        shards,
        mesh=split,
        in_specs=(rows, rows, P(), P(), P(), P(), P(), P(), rows, rows, rows,
                  P(ALL, None, None, None), rows),
        out_specs=(rows, rows, rows, P()),
        check_vma=False,
    )
```

```python
import functools

import jax
import jax.numpy as jnp
from jax import lax
from jax.experimental import pallas as pl
from jax.experimental.pallas import tpu as pltpu
from jax.sharding import Mesh
from jax.sharding import PartitionSpec as P

SLAB = ("gx", "gy", "gc")
PLANE = ("gx", "gy")
ALL = ("gx", "gy", "gc", "z")

EPSILON = 1e-06
ABSENT = -1e30
F32 = jnp.float32
BF16 = jnp.bfloat16

VM = pl.BlockSpec(memory_space=pltpu.VMEM)
SM = pl.BlockSpec(memory_space=pltpu.SMEM)
HB = pl.BlockSpec(memory_space=pltpu.HBM)


def nn(a, b):
    return lax.dot_general(a, b, (((1,), (0,)), ((), ())), preferred_element_type=F32)


def nt(a, b):
    return lax.dot_general(a, b, (((1,), (1,)), ((), ())), preferred_element_type=F32)


def tn(a, b):
    return lax.dot_general(a, b, (((0,), (0,)), ((), ())), preferred_element_type=F32)


def inv_rms(wide):
    return lax.rsqrt(jnp.mean(wide * wide, axis=-1, keepdims=True) + EPSILON)


def norm_back(wide, factor, gain_row, upstream):
    scaled = gain_row * upstream
    inner = jnp.mean(wide * scaled, axis=-1, keepdims=True)
    return factor * scaled - wide * (factor * factor * factor * inner)


def call(body, outs, in_specs, args, flops, nbytes, name, scratch=(), out_specs=None, aliases=None):
    return pl.pallas_call(
        body,
        out_shape=outs,
        in_specs=in_specs,
        out_specs=out_specs or [VM] * len(outs),
        scratch_shapes=list(scratch),
        input_output_aliases=aliases or {},
        compiler_params=pltpu.CompilerParams(vmem_limit_bytes=24 << 20),
        cost_estimate=pl.CostEstimate(flops=flops, bytes_accessed=nbytes, transcendentals=0),
        name=name,
    )(*args)


def fetch(sources, targets, sems):
    copies = []
    for i, (source, target) in enumerate(zip(sources, targets)):
        copies.append(pltpu.make_async_copy(source, target, sems.at[i]))
        copies[-1].start()
    return copies


def held(*args):
    return [pltpu.VMEM(a.shape, a.dtype) for a in args] + [pltpu.SemaphoreType.DMA((len(args),))]


def assemble(rows, near_first, near, far, own, *pieces):
    block = near.shape[0]
    cap = block // 4
    near_at = pl.multiple_of((1 - near_first) * (2 * block), block)
    far_at = pl.multiple_of(near_first * (2 * block), block)
    rows[block : block + cap] = own[0:cap]
    rows[pl.ds(near_at, cap), :] = near[0:cap]
    rows[pl.ds(far_at, cap), :] = far[0:cap]
    for k in range(1, 4):
        mixed, last = pieces[k - 1], pieces[len(pieces) - 4 + k]
        rows[block + k * cap : block + (k + 1) * cap] = mixed[0:cap]
        rows[pl.ds(near_at + k * cap, cap), :] = mixed[cap : 2 * cap]
        rows[pl.ds(far_at + k * cap, cap), :] = last[last.shape[0] - cap :]


def gather_body(sub_ref, core_ref, rows_hbm, gain_hbm, x_hbm, near_ref, far_ref, own_ref,
                rows_ref, gain_ref, x_ref, sems):
    half = x_ref.shape[0] // 2
    cap = rows_ref.shape[3]
    core = core_ref[0]
    firsts = [pl.multiple_of((1 - core) * half, half), pl.multiple_of(core * half, half)]
    parts = [pl.ds(first, half) for first in firsts]
    copies = fetch(
        [rows_hbm, gain_hbm] + [x_hbm.at[p] for p in parts],
        [rows_ref, gain_ref] + [x_ref.at[p] for p in parts],
        sems,
    )
    copies[0].wait()
    copies[1].wait()
    me = sub_ref[0]
    eye = lax.broadcasted_iota(jnp.int32, (cap, cap), 0) == lax.broadcasted_iota(
        jnp.int32, (cap, cap), 1
    )
    gain = gain_ref[...]
    steps = (
        (2 - 2 * core, firsts[0], half, near_ref),
        (2 * core, firsts[1], half, far_ref),
        (1, 0, 2 * half, own_ref),
    )
    for step, (o, first, count, out_ref) in enumerate(steps):
        cols = []
        for k in range(4):
            s = lax.rem(me + k, 4)
            row = rows_ref[0, o, pl.ds(s, 1), :].astype(F32)
            cols.append(jnp.sum(jnp.where(eye, row, 0.0), axis=1, keepdims=True))
        col = jnp.concatenate(cols, axis=0).astype(jnp.int32) - first
        lanes = lax.broadcasted_iota(jnp.int32, (4 * cap, count), 1)
        onehot = jnp.where(lanes == col, 1.0, 0.0).astype(BF16)
        if step < 2:
            copies[2 + step].wait()
        wide = nn(onehot, x_ref[pl.ds(first, count), :])
        out_ref[...] = (wide * inv_rms(wide) * gain).astype(BF16)


def mesh_in_body(mesh_hbm, gain_hbm, wq_hbm, wo_hbm, og_hbm, normed_ref, q_ref, ag_ref, og_ref,
                 mesh_ref, gain_ref, wq_ref, wo_ref, sems):
    copies = fetch(
        (mesh_hbm, gain_hbm, wq_hbm, wo_hbm, og_hbm), (mesh_ref, gain_ref, wq_ref, wo_ref, og_ref), sems
    )
    for copy in copies:
        copy.wait()
    wide = mesh_ref[...].astype(F32)
    normed = (wide * inv_rms(wide) * gain_ref[...]).astype(BF16)
    normed_ref[...] = normed
    q_ref[...] = (nn(normed, wq_ref[...]) * (128 ** -0.5)).astype(BF16)
    ag_ref[...] = nt(og_ref[...], wo_ref[...]).astype(BF16)


def slots_body(sub_ref, nbr_hbm, valid_hbm, bias_hbm, dense_ref, inv_ref, edge_ref,
               nbr_ref, valid_ref, bias_ref, sems):
    copies = fetch((nbr_hbm, valid_hbm, bias_hbm), (nbr_ref, valid_ref, bias_ref), sems)
    heads, nodes, slots = dense_ref.shape
    fan = nbr_ref.shape[1]
    for copy in copies:
        copy.wait()
    slot = nbr_ref[...]
    slot = (slot & ~192) | (((sub_ref[0] - (slot >> 6)) & 3) << 6)
    high, low = slot >> 7, slot & 127
    blocks = lax.broadcasted_iota(jnp.int32, (8, fan), 0)
    lanes = lax.broadcasted_iota(jnp.int32, (128, fan), 0)
    edge = lax.broadcasted_iota(jnp.int32, (8, fan), 1).astype(F32) + 1.0
    for m in range(nodes):
        named = jnp.where(high[m : m + 1, :] == blocks, edge, 0.0).astype(BF16)
        places = jnp.where(low[m : m + 1, :] == lanes, 1.0, 0.0).astype(BF16)
        inv_ref[m * 8 : (m + 1) * 8, :] = nt(named, places)
    live = valid_ref[...] == 1
    for h in range(heads):
        edge_ref[h, :, 0:fan] = jnp.where(live, bias_ref[:, h * fan : (h + 1) * fan], ABSENT)
    for b in range(slots // 128):
        at = inv_ref[pl.ds(b, nodes, stride=8), :].astype(jnp.int32) - 1
        here = at >= 0
        at = jnp.maximum(at, 0)
        for h in range(heads):
            got = jnp.take_along_axis(edge_ref[h], at, axis=1, mode="promise_in_bounds")
            dense_ref[h, :, b * 128 : (b + 1) * 128] = jnp.where(here, got, ABSENT)


def middle_body(core_ref, near, far, own, m1, m2, m3, f1, f2, f3, q_ref, ag_ref, mn_ref, og_ref,
                bias_ref, wk_hbm, wv_hbm, send_ref, part_ref, att_ref, qg_ref, wkv_ref, rows,
                keys, vals, sems):
    width = q_ref.shape[1]
    copies = fetch(
        (wk_hbm, wv_hbm), (wkv_ref.at[:, pl.ds(0, width)], wkv_ref.at[:, pl.ds(width, width)]), sems
    )
    heads = bias_ref.shape[0]
    core = core_ref[0]
    assemble(rows, 1 - core, near, far, own, m1, m2, m3, f1, f2, f3)
    copies[0].wait()
    keys[...] = nn(rows[...], wkv_ref[:, :width]).astype(BF16)
    copies[1].wait()
    vals[...] = nn(rows[...], wkv_ref[:, width:]).astype(BF16)
    for h in range(heads):
        at = slice(h * 128, (h + 1) * 128)
        q, ag = q_ref[:, at], ag_ref[:, at]
        kh, vh = keys[:, at], vals[:, at]
        scores = nt(q, kh) + bias_ref[h]
        peak = jnp.max(scores, axis=1, keepdims=True)
        terms = jnp.exp(scores - peak)
        probs = terms / jnp.sum(terms, axis=1, keepdims=True)
        probs_b = probs.astype(BF16)
        att_ref[:, at] = nn(probs_b, vh).astype(BF16)
        pg = nt(ag, vh)
        sg = (probs * (pg - jnp.sum(probs * pg, axis=1, keepdims=True))).astype(BF16)
        qg_ref[:, at] = (nn(sg, kh) * (128 ** -0.5)).astype(BF16)
        part_ref[:, at] = tn(sg, q).astype(BF16)
        part_ref[:, width + h * 128 : width + (h + 1) * 128] = tn(probs_b, ag).astype(BF16)
    half_grads(1 - core, send_ref, rows, part_ref, mn_ref, qg_ref, att_ref, og_ref)


def half_grads(half, out_ref, rows, part_ref, mn_ref, qg_ref, att_ref, og_ref):
    width = mn_ref.shape[1]
    first = half == 0
    left = jnp.where(first, mn_ref[...].astype(F32), att_ref[...].astype(F32)).astype(BF16)
    right = jnp.where(first, qg_ref[...].astype(F32), og_ref[...].astype(F32)).astype(BF16)
    columns = pl.ds(pl.multiple_of(half * width, width), width)
    out_ref[0:width] = tn(left, right).astype(BF16)
    out_ref[width : 2 * width] = tn(rows[...], part_ref[:, columns]).astype(BF16)


def keep_body(core_ref, rows, part_ref, mn_ref, qg_ref, att_ref, og_ref, keep_ref):
    half_grads(core_ref[0], keep_ref, rows, part_ref, mn_ref, qg_ref, att_ref, og_ref)


def back_body(part_ref, wkv_ref, s0, s1, s2, s3):
    cap = s0.shape[1]
    for o in range(3):
        rows = slice(o * 4 * cap, (o + 1) * 4 * cap)
        back = nt(part_ref[rows, :], wkv_ref[...]).astype(BF16)
        for k, piece in enumerate((s0, s1, s2, s3)):
            piece[o] = back[k * cap : (k + 1) * cap]


def mesh_body(att_ref, qg_ref, og_ref, wo_hbm, wq_hbm, mesh_hbm, gain_hbm, out_ref, grad_ref,
              wo_ref, wq_ref, mesh_ref, gain_ref, sems):
    copies = fetch(
        (wo_hbm, wq_hbm, mesh_hbm, gain_hbm), (wo_ref, wq_ref, mesh_ref, gain_ref), sems
    )
    for copy in copies:
        copy.wait()
    wide = mesh_ref[...].astype(F32)
    out_ref[...] = (wide + nn(att_ref[...], wo_ref[...])).astype(BF16)
    upstream = nt(qg_ref[...], wq_ref[...])
    back = norm_back(wide, inv_rms(wide), gain_ref[...], upstream)
    grad_ref[...] = (og_ref[...].astype(F32) + back).astype(BF16)


def pack_body(core_ref, p0, p1, p2, p3, near_ref, far_ref):
    cap = p0.shape[1]
    near = core_ref[0] * 2
    for k, piece in enumerate((p0, p1, p2, p3)):
        near_ref[k * cap : (k + 1) * cap, :] = piece[near]
        far_ref[k * cap : (k + 1) * cap, :] = piece[2 - near]


def mix_body(own, near, m1, m2, m3):
    cap = m1.shape[0] // 2
    for k, mixed in enumerate((m1, m2, m3), 1):
        mixed[0:cap] = own[k * cap : (k + 1) * cap]
        mixed[cap : 2 * cap] = near[k * cap : (k + 1) * cap]


def split_body(block, f1, f2, f3):
    cap = f1.shape[0]
    for k, piece in enumerate((f1, f2, f3), 1):
        piece[...] = block[k * cap : (k + 1) * cap]


def grid_body(sub_ref, core_ref, near, far, s0, s1, s2, s3, rows_hbm, gain_hbm, x_hbm, out_hbm,
              got, done_ref, done_sems, rows_ref, gain_ref, x_ref, sems):
    copies = fetch((rows_hbm, gain_hbm, x_hbm), (rows_ref, gain_ref, x_ref), sems)
    points = x_ref.shape[0]
    half = points // 2
    cap = rows_ref.shape[3]
    block = 4 * cap
    me = sub_ref[0]
    core = core_ref[0]
    got[pl.ds(pl.multiple_of((1 - core) * (2 * block), block), block), :] = near[...]
    got[pl.ds(pl.multiple_of(core * (2 * block), block), block), :] = far[...]
    for k, piece in enumerate((s0, s1, s2, s3)):
        got[block + k * cap : block + (k + 1) * cap] = piece[1]
    for copy in copies:
        copy.wait()
    gain = gain_ref[...]
    idx = []
    for o in range(3):
        for k in range(4):
            idx.append(rows_ref[0, o, pl.ds(lax.rem(me + k, 4), 1), :])
    idx = jnp.concatenate(idx, axis=1)
    tile = 256
    stores = []
    for t in range(points // tile):
        first = t * tile
        low = 0 if first < half else block
        ids = lax.broadcasted_iota(jnp.int32, (tile, 2 * block), 0) + first
        onehot = jnp.where(ids == idx[:, low : low + 2 * block], 1.0, 0.0).astype(BF16)
        upstream = nn(onehot, got[low : low + 2 * block, :])
        wide = x_ref[first : first + tile, :].astype(F32)
        part = slice(first, first + tile)
        done_ref[part, :] = norm_back(wide, inv_rms(wide), gain, upstream).astype(BF16)
        stores.append(
            pltpu.make_async_copy(done_ref.at[part], out_hbm.at[part], done_sems.at[t])
        )
        stores[-1].start()
    for store in stores:
        store.wait()


def widen_body(turn, core_ref, half_ref, *refs):
    out_hbm, wide, sems = refs[-3:]
    count, width, _ = wide.shape
    half = core_ref[0] ^ turn
    part = width // 2
    copies = []
    for i in range(2 * count):
        m, rows = i // 2, pl.ds((i % 2) * part, part)
        wide[m, rows, :] = half_ref[i * part : (i + 1) * part, :].astype(F32)
        copies.append(
            pltpu.make_async_copy(
                wide.at[m, rows], out_hbm.at[lax.select(half == 0, m, 3 - m), rows], sems.at[i]
            )
        )
        copies[-1].start()
    for copy in copies:
        copy.wait()


def pair_body(keep_ref, other_ref, out_hbm, sums, sems):
    part = sums.shape[0] // 4
    copies = []
    for i in range(4):
        at = slice(i * part, (i + 1) * part)
        sums[at, :] = (keep_ref[at, :].astype(F32) + other_ref[at, :].astype(F32)).astype(BF16)
        copies.append(pltpu.make_async_copy(sums.at[at], out_hbm.at[at], sems.at[i]))
        copies[-1].start()
    for copy in copies:
        copy.wait()


def spread_body(p0, p1, p2, p3, out_hbm, total, sems):
    even = p0[...].astype(F32) + p2[...].astype(F32)
    odd = p1[...].astype(F32) + p3[...].astype(F32)
    total[...] = (even + odd).astype(BF16)
    copies = []
    for i in range(out_hbm.shape[0]):
        copies.append(pltpu.make_async_copy(total, out_hbm.at[i], sems.at[i]))
        copies[-1].start()
    for copy in copies:
        copy.wait()


def shifted(block, axis, k):
    n = lax.axis_size(axis)
    return lax.ppermute(block, axis, [(i, (i + k) % n) for i in range(n)])


def swapped_far(block):
    n = lax.axis_size(SLAB)
    pairs = [(i, i + 1) for i in range(1, n - 1, 2)]
    return lax.ppermute(block, SLAB, pairs + [(j, i) for i, j in pairs])


def sds(shape, dtype=BF16):
    return jax.ShapeDtypeStruct(shape, dtype)


def shards(grid_x, mesh_h, gain_grid, gain_mesh, w_query, w_key, w_value, w_out, edge_bias,
           neighbours, valid, send_rows, out_grad):
    points, width = grid_x.shape
    nodes, fan = neighbours.shape
    cap = send_rows.shape[3]
    block = 4 * cap
    slots = 3 * block
    heads = edge_bias.shape[1] // fan
    sub1 = lax.axis_index("z").astype(jnp.int32).reshape(1)
    core1 = lax.axis_index("gc").astype(jnp.int32).reshape(1)
    gain_g, gain_m = gain_grid.reshape(1, width), gain_mesh.reshape(1, width)
    (grid_x, mesh_h, out_grad, send_rows, w_key, w_value, w_query, w_out, gain_g, gain_m, edge_bias,
     neighbours, valid) = (
        pltpu.with_memory_space_constraint(a, pltpu.HBM)
        for a in (grid_x, mesh_h, out_grad, send_rows, w_key, w_value, w_query, w_out, gain_g, gain_m,
                  edge_bias, neighbours, valid)
    )

    one, two, four = sds((cap, width)), sds((2 * cap, width)), sds((block, width))
    near, far, own = call(
        gather_body, [four] * 3, [SM, SM, HB, HB, HB],
        (sub1, core1, send_rows, gain_g, grid_x), 1 << 30, 4 << 20, "gather_rows",
        held(send_rows, gain_g, grid_x)[:-1] + [pltpu.SemaphoreType.DMA((4,))],
    )

    far = swapped_far(far)
    near = shifted(near, "gc", 1)
    mixed = call(mix_body, [two] * 3, [VM] * 2, (own, near), 0, 1 << 20, "mix")
    mixed = [shifted(m, "z", k) for k, m in enumerate(mixed, 1)]
    mesh_normed, queries, att_grad, og_near = call(
        mesh_in_body, [sds((nodes, width))] * 4, [HB] * 5, (mesh_h, gain_m, w_query, w_out, out_grad),
        1 << 28, 2 << 20, "mesh_in", held(mesh_h, gain_m, w_query, w_out)[:-1] + [pltpu.SemaphoreType.DMA((5,))],
    )
    far, mixed[0], queries = lax.optimization_barrier((far, mixed[0], queries))
    outer = call(split_body, [one] * 3, [VM], (far,), 0, 1 << 19, "split")
    outer = [shifted(f, "z", k) for k, f in enumerate(outer, 1)]
    received = near, far, own, *mixed, *outer
    sub2, far = lax.optimization_barrier((sub1, far))
    (dense,) = call(
        slots_body, [sds((heads, nodes, slots), F32)], [SM] + [HB] * 3,
        (sub2, neighbours, valid, edge_bias), 1 << 30, 8 << 20, "slots",
        [pltpu.VMEM((nodes * 8, 128), F32), pltpu.VMEM((heads, nodes, 128), F32)]
        + held(neighbours, valid, edge_bias),
    )
    send, part_grads, attended, query_grad, weights_near, rows = call(
        middle_body,
        [sds((2 * width, width)), sds((slots, 2 * width))] + [sds((nodes, width))] * 2
        + [sds((width, 2 * width)), sds((slots, width))],
        [SM] + [VM] * 14 + [HB] * 2,
        (core1, *received, queries, att_grad, mesh_normed, og_near, dense, w_key, w_value),
        3 << 30, 8 << 20, "middle",
        [pltpu.VMEM((slots, width), BF16)] * 2 + [pltpu.SemaphoreType.DMA((2,))],
    )

    other = shifted(send, "gc", 1)
    (keep,) = call(
        keep_body, [sds((2 * width, width))], [SM] + [VM] * 6,
        (core1, rows, part_grads, mesh_normed, query_grad, attended, og_near), 1 << 29, 3 << 20, "keep",
    )
    s0, s1, s2, s3 = call(
        back_body, [sds((3, cap, width))] * 4, [VM] * 2, (part_grads, weights_near),
        1 << 30, 3 << 20, "back",
    )
    other, s1, keep = lax.optimization_barrier((other, s1, keep))
    (own,) = call(
        pair_body, [sds((2 * width, width))], [VM] * 2, (keep, other), 1 << 20, 3 << 20, "pair",
        [pltpu.VMEM((2 * width, width), BF16), pltpu.SemaphoreType.DMA((4,))], [HB],
    )
    plane = lax.axis_size(PLANE)
    share = 2 * width // plane
    parts = lax.all_to_all(own.reshape(plane, share, width), PLANE, 0, 0, tiled=True)

    attended, own = lax.optimization_barrier((attended, own))
    mesh_out, mesh_grad = call(
        mesh_body, [sds((nodes, width))] * 2, [VM] * 3 + [HB] * 4,
        (attended, query_grad, og_near, w_out, w_query, mesh_h, gain_m), 1 << 28, 2 << 20, "mesh",
        held(w_out, w_query, mesh_h, gain_m),
    )
    s1, s2, s3 = (shifted(s, "z", -k) for k, s in ((1, s1), (2, s2), (3, s3)))
    s1, parts, mesh_out = lax.optimization_barrier((s1, parts, mesh_out))
    part = jnp.sum(parts.astype(F32), axis=0).astype(BF16)
    part, s0 = lax.optimization_barrier((part, s0))
    near, far = call(
        pack_body, [four] * 2, [SM] + [VM] * 4, (core1, s0, s1, s2, s3), 0, 1 << 20, "pack"
    )
    far = swapped_far(far)
    near = shifted(near, "gc", 1)
    p1, p2, p3 = (shifted(part, "z", k) for k in (1, 2, 3))
    p1, near, far = lax.optimization_barrier((p1, near, far))
    (spread,) = call(
        spread_body, [sds((plane, share, width))], [VM] * 4, (part, p1, p2, p3), 1 << 18, 1 << 20,
        "spread", [pltpu.VMEM((share, width), BF16), pltpu.SemaphoreType.DMA((plane,))], [HB],
    )
    mine = lax.all_to_all(spread, PLANE, 0, 0, tiled=True).reshape(2 * width, width)
    (grid_grad,) = call(
        grid_body, [sds((points, width))], [SM] * 2 + [VM] * 6 + [HB] * 3,
        (sub1, core1, near, far, s0, s1, s2, s3, send_rows, gain_g, grid_x),
        1 << 30, 5 << 20, "grid_grad",
        [pltpu.VMEM((slots, width), BF16), pltpu.VMEM((points, width), BF16),
         pltpu.SemaphoreType.DMA((points // 256,))] + held(send_rows, gain_g, grid_x),
        [HB],
    )
    mine, grid_grad = lax.optimization_barrier((mine, grid_grad))
    theirs = shifted(mine, "gc", 1)
    whole = sds((4, width, width), F32)
    wide = [pltpu.VMEM((2, width, width), F32), pltpu.SemaphoreType.DMA((4,))]
    (weight_grads,) = call(
        functools.partial(widen_body, 0), [whole], [SM, VM], (core1, mine), 1 << 20, 3 << 20, "widen_own",
        wide, [HB],
    )
    (weight_grads,) = call(
        functools.partial(widen_body, 1), [whole], [SM, VM, HB], (core1, theirs, weight_grads),
        1 << 20, 3 << 20, "widen_other", wide, [HB], {2: 0},
    )
    return mesh_out, mesh_grad, grid_grad, weight_grads


def solution(mesh):
    split = Mesh(mesh.devices.reshape(4, 4, 2, mesh.shape["sub"]), ALL)
    rows = P(ALL, None)
    return jax.shard_map(
        shards,
        mesh=split,
        in_specs=(rows, rows, P(), P(), P(), P(), P(), P(), rows, rows, rows,
                  P(ALL, None, None, None), rows),
        out_specs=(rows, rows, rows, P()),
        check_vma=False,
    )
```

```python
import functools

import jax
import jax.numpy as jnp
from jax import lax
from jax.experimental import pallas as pl
from jax.experimental.pallas import tpu as pltpu
from jax.sharding import Mesh
from jax.sharding import PartitionSpec as P

SLAB = ("gx", "gy", "gc")
PLANE = ("gx", "gy")
ALL = ("gx", "gy", "gc", "z")

EPSILON = 1e-06
ABSENT = -1e30
F32 = jnp.float32
BF16 = jnp.bfloat16

VM = pl.BlockSpec(memory_space=pltpu.VMEM)
SM = pl.BlockSpec(memory_space=pltpu.SMEM)
HB = pl.BlockSpec(memory_space=pltpu.HBM)


def nn(a, b):
    return lax.dot_general(a, b, (((1,), (0,)), ((), ())), preferred_element_type=F32)


def nt(a, b):
    return lax.dot_general(a, b, (((1,), (1,)), ((), ())), preferred_element_type=F32)


def tn(a, b):
    return lax.dot_general(a, b, (((0,), (0,)), ((), ())), preferred_element_type=F32)


def inv_rms(wide):
    return lax.rsqrt(jnp.mean(wide * wide, axis=-1, keepdims=True) + EPSILON)


def norm_back(wide, factor, gain_row, upstream):
    scaled = gain_row * upstream
    inner = jnp.mean(wide * scaled, axis=-1, keepdims=True)
    return factor * scaled - wide * (factor * factor * factor * inner)


def call(body, outs, in_specs, args, flops, nbytes, name, scratch=(), out_specs=None, aliases=None):
    return pl.pallas_call(
        body,
        out_shape=outs,
        in_specs=in_specs,
        out_specs=out_specs or [VM] * len(outs),
        scratch_shapes=list(scratch),
        input_output_aliases=aliases or {},
        compiler_params=pltpu.CompilerParams(vmem_limit_bytes=24 << 20),
        cost_estimate=pl.CostEstimate(flops=flops, bytes_accessed=nbytes, transcendentals=0),
        name=name,
    )(*args)


def fetch(sources, targets, sems):
    copies = []
    for i, (source, target) in enumerate(zip(sources, targets)):
        copies.append(pltpu.make_async_copy(source, target, sems.at[i]))
        copies[-1].start()
    return copies


def held(*args):
    return [pltpu.VMEM(a.shape, a.dtype) for a in args] + [pltpu.SemaphoreType.DMA((len(args),))]


def assemble(rows, near_first, near, own, m1, m2, m3, f0, f1, f2, f3):
    block = near.shape[0]
    cap = block // 4
    near_at = pl.multiple_of((1 - near_first) * (2 * block), block)
    far_at = pl.multiple_of(near_first * (2 * block), block)
    rows[block : block + cap] = own[0:cap]
    rows[pl.ds(near_at, cap), :] = near[0:cap]
    for k, mixed in enumerate((m1, m2, m3), 1):
        rows[block + k * cap : block + (k + 1) * cap] = mixed[0:cap]
        rows[pl.ds(near_at + k * cap, cap), :] = mixed[cap : 2 * cap]
    for k, far in enumerate((f0, f1, f2, f3)):
        rows[pl.ds(far_at + k * cap, cap), :] = far[...]


def gather_body(sub_ref, core_ref, rows_hbm, gain_hbm, x_hbm, near_ref, own_ref, f0, f1, f2, f3,
                rows_ref, gain_ref, x_ref, sems):
    half = x_ref.shape[0] // 2
    cap = rows_ref.shape[3]
    core = core_ref[0]
    firsts = [pl.multiple_of((1 - core) * half, half), pl.multiple_of(core * half, half)]
    parts = [pl.ds(first, half) for first in firsts]
    copies = fetch(
        [rows_hbm, gain_hbm] + [x_hbm.at[p] for p in parts],
        [rows_ref, gain_ref] + [x_ref.at[p] for p in parts],
        sems,
    )
    copies[0].wait()
    copies[1].wait()
    me = sub_ref[0]
    eye = lax.broadcasted_iota(jnp.int32, (cap, cap), 0) == lax.broadcasted_iota(
        jnp.int32, (cap, cap), 1
    )
    gain = gain_ref[...]
    steps = (
        (2 - 2 * core, firsts[0], half, (near_ref,)),
        (2 * core, firsts[1], half, (f0, f1, f2, f3)),
        (1, 0, 2 * half, (own_ref,)),
    )
    for step, (o, first, count, outs) in enumerate(steps):
        cols = []
        for k in range(4):
            s = lax.rem(me + k, 4)
            row = rows_ref[0, o, pl.ds(s, 1), :].astype(F32)
            cols.append(jnp.sum(jnp.where(eye, row, 0.0), axis=1, keepdims=True))
        col = jnp.concatenate(cols, axis=0).astype(jnp.int32) - first
        lanes = lax.broadcasted_iota(jnp.int32, (4 * cap, count), 1)
        onehot = jnp.where(lanes == col, 1.0, 0.0).astype(BF16)
        if step < 2:
            copies[2 + step].wait()
        wide = nn(onehot, x_ref[pl.ds(first, count), :])
        normed = (wide * inv_rms(wide) * gain).astype(BF16)
        for i, out_ref in enumerate(outs):
            size = out_ref.shape[0]
            out_ref[...] = normed[i * size : (i + 1) * size]


def mesh_in_body(mesh_hbm, gain_hbm, wq_hbm, wo_hbm, og_hbm, normed_ref, q_ref, ag_ref, og_ref,
                 mesh_ref, gain_ref, wq_ref, wo_ref, sems):
    copies = fetch(
        (mesh_hbm, gain_hbm, wq_hbm, wo_hbm, og_hbm), (mesh_ref, gain_ref, wq_ref, wo_ref, og_ref), sems
    )
    for copy in copies:
        copy.wait()
    wide = mesh_ref[...].astype(F32)
    normed = (wide * inv_rms(wide) * gain_ref[...]).astype(BF16)
    normed_ref[...] = normed
    q_ref[...] = (nn(normed, wq_ref[...]) * (128 ** -0.5)).astype(BF16)
    ag_ref[...] = nt(og_ref[...], wo_ref[...]).astype(BF16)


def slots_body(sub_ref, nbr_hbm, valid_hbm, bias_hbm, dense_ref, inv_ref, edge_ref,
               nbr_ref, valid_ref, bias_ref, sems):
    copies = fetch((nbr_hbm, valid_hbm, bias_hbm), (nbr_ref, valid_ref, bias_ref), sems)
    heads, nodes, slots = dense_ref.shape
    fan = nbr_ref.shape[1]
    for copy in copies:
        copy.wait()
    slot = nbr_ref[...]
    slot = (slot & ~192) | (((sub_ref[0] - (slot >> 6)) & 3) << 6)
    high, low = slot >> 7, slot & 127
    blocks = lax.broadcasted_iota(jnp.int32, (8, fan), 0)
    lanes = lax.broadcasted_iota(jnp.int32, (128, fan), 0)
    edge = lax.broadcasted_iota(jnp.int32, (8, fan), 1).astype(F32) + 1.0
    for m in range(nodes):
        named = jnp.where(high[m : m + 1, :] == blocks, edge, 0.0).astype(BF16)
        places = jnp.where(low[m : m + 1, :] == lanes, 1.0, 0.0).astype(BF16)
        inv_ref[m * 8 : (m + 1) * 8, :] = nt(named, places)
    live = valid_ref[...] == 1
    for h in range(heads):
        edge_ref[h, :, 0:fan] = jnp.where(live, bias_ref[:, h * fan : (h + 1) * fan], ABSENT)
    for b in range(slots // 128):
        at = inv_ref[pl.ds(b, nodes, stride=8), :].astype(jnp.int32) - 1
        here = at >= 0
        at = jnp.maximum(at, 0)
        for h in range(heads):
            got = jnp.take_along_axis(edge_ref[h], at, axis=1, mode="promise_in_bounds")
            dense_ref[h, :, b * 128 : (b + 1) * 128] = jnp.where(here, got, ABSENT)


def middle_body(core_ref, near, own, m1, m2, m3, f0, f1, f2, f3, q_ref, ag_ref, mn_ref, og_ref,
                bias_ref, wk_hbm, wv_hbm, send_ref, part_ref, att_ref, qg_ref, wkv_ref, rows,
                keys, vals, sems):
    width = q_ref.shape[1]
    copies = fetch(
        (wk_hbm, wv_hbm), (wkv_ref.at[:, pl.ds(0, width)], wkv_ref.at[:, pl.ds(width, width)]), sems
    )
    heads = bias_ref.shape[0]
    core = core_ref[0]
    assemble(rows, 1 - core, near, own, m1, m2, m3, f0, f1, f2, f3)
    copies[0].wait()
    keys[...] = nn(rows[...], wkv_ref[:, :width]).astype(BF16)
    copies[1].wait()
    vals[...] = nn(rows[...], wkv_ref[:, width:]).astype(BF16)
    for h in range(heads):
        at = slice(h * 128, (h + 1) * 128)
        q, ag = q_ref[:, at], ag_ref[:, at]
        kh, vh = keys[:, at], vals[:, at]
        scores = nt(q, kh) + bias_ref[h]
        peak = jnp.max(scores, axis=1, keepdims=True)
        terms = jnp.exp(scores - peak)
        probs = terms / jnp.sum(terms, axis=1, keepdims=True)
        probs_b = probs.astype(BF16)
        att_ref[:, at] = nn(probs_b, vh).astype(BF16)
        pg = nt(ag, vh)
        sg = (probs * (pg - jnp.sum(probs * pg, axis=1, keepdims=True))).astype(BF16)
        qg_ref[:, at] = (nn(sg, kh) * (128 ** -0.5)).astype(BF16)
        part_ref[:, at] = tn(sg, q).astype(BF16)
        part_ref[:, width + h * 128 : width + (h + 1) * 128] = tn(probs_b, ag).astype(BF16)
    half_grads(1 - core, send_ref, rows, part_ref, mn_ref, qg_ref, att_ref, og_ref)


def half_grads(half, out_ref, rows, part_ref, mn_ref, qg_ref, att_ref, og_ref):
    width = mn_ref.shape[1]
    first = half == 0
    left = jnp.where(first, mn_ref[...].astype(F32), att_ref[...].astype(F32)).astype(BF16)
    right = jnp.where(first, qg_ref[...].astype(F32), og_ref[...].astype(F32)).astype(BF16)
    columns = pl.ds(pl.multiple_of(half * width, width), width)
    out_ref[0:width] = tn(left, right).astype(BF16)
    out_ref[width : 2 * width] = tn(rows[...], part_ref[:, columns]).astype(BF16)


def keep_body(core_ref, rows, part_ref, mn_ref, qg_ref, att_ref, og_ref, keep_ref):
    half_grads(core_ref[0], keep_ref, rows, part_ref, mn_ref, qg_ref, att_ref, og_ref)


def back_body(core_ref, part_ref, wkv_ref, near_ref, own_ref, f0, f1, f2, f3):
    block = own_ref.shape[0]
    near_at = pl.multiple_of(core_ref[0] * (2 * block), block)
    far_at = pl.multiple_of((1 - core_ref[0]) * (2 * block), block)
    for first, outs in ((near_at, (near_ref,)), (far_at, (f0, f1, f2, f3)), (block, (own_ref,))):
        back = nt(part_ref[pl.ds(first, block), :], wkv_ref[...]).astype(BF16)
        for i, out_ref in enumerate(outs):
            size = out_ref.shape[0]
            out_ref[...] = back[i * size : (i + 1) * size]


def mesh_body(att_ref, qg_ref, og_ref, wo_hbm, wq_hbm, mesh_hbm, gain_hbm, out_ref, grad_ref,
              wo_ref, wq_ref, mesh_ref, gain_ref, sems):
    copies = fetch(
        (wo_hbm, wq_hbm, mesh_hbm, gain_hbm), (wo_ref, wq_ref, mesh_ref, gain_ref), sems
    )
    for copy in copies:
        copy.wait()
    wide = mesh_ref[...].astype(F32)
    out_ref[...] = (wide + nn(att_ref[...], wo_ref[...])).astype(BF16)
    upstream = nt(qg_ref[...], wq_ref[...])
    back = norm_back(wide, inv_rms(wide), gain_ref[...], upstream)
    grad_ref[...] = (og_ref[...].astype(F32) + back).astype(BF16)


def mix_body(own, near, m1, m2, m3):
    cap = m1.shape[0] // 2
    for k, mixed in enumerate((m1, m2, m3), 1):
        mixed[0:cap] = own[k * cap : (k + 1) * cap]
        mixed[cap : 2 * cap] = near[k * cap : (k + 1) * cap]


def grid_body(sub_ref, core_ref, near, own, m1, m2, m3, f0, f1, f2, f3, rows_hbm, gain_hbm, x_hbm, out_hbm,
              got, done_ref, done_sems, rows_ref, gain_ref, x_ref, sems):
    copies = fetch((rows_hbm, gain_hbm, x_hbm), (rows_ref, gain_ref, x_ref), sems)
    points = x_ref.shape[0]
    half = points // 2
    cap = rows_ref.shape[3]
    block = 4 * cap
    me = sub_ref[0]
    assemble(got, core_ref[0], near, own, m1, m2, m3, f0, f1, f2, f3)
    for copy in copies:
        copy.wait()
    gain = gain_ref[...]
    idx = []
    for o in range(3):
        for k in range(4):
            idx.append(rows_ref[0, o, pl.ds(lax.rem(me + k, 4), 1), :])
    idx = jnp.concatenate(idx, axis=1)
    tile = 256
    stores = []
    for t in range(points // tile):
        first = t * tile
        low = 0 if first < half else block
        ids = lax.broadcasted_iota(jnp.int32, (tile, 2 * block), 0) + first
        onehot = jnp.where(ids == idx[:, low : low + 2 * block], 1.0, 0.0).astype(BF16)
        upstream = nn(onehot, got[low : low + 2 * block, :])
        wide = x_ref[first : first + tile, :].astype(F32)
        part = slice(first, first + tile)
        done_ref[part, :] = norm_back(wide, inv_rms(wide), gain, upstream).astype(BF16)
        stores.append(
            pltpu.make_async_copy(done_ref.at[part], out_hbm.at[part], done_sems.at[t])
        )
        stores[-1].start()
    for store in stores:
        store.wait()


def widen_body(turn, core_ref, half_ref, *refs):
    out_hbm, wide, sems = refs[-3:]
    count, width, _ = wide.shape
    half = core_ref[0] ^ turn
    part = width // 2
    copies = []
    for i in range(2 * count):
        m, rows = i // 2, pl.ds((i % 2) * part, part)
        wide[m, rows, :] = half_ref[i * part : (i + 1) * part, :].astype(F32)
        copies.append(
            pltpu.make_async_copy(
                wide.at[m, rows], out_hbm.at[lax.select(half == 0, m, 3 - m), rows], sems.at[i]
            )
        )
        copies[-1].start()
    for copy in copies:
        copy.wait()


def pair_body(keep_ref, other_ref, out_hbm, sums, sems):
    part = sums.shape[0] // 4
    copies = []
    for i in range(4):
        at = slice(i * part, (i + 1) * part)
        sums[at, :] = (keep_ref[at, :].astype(F32) + other_ref[at, :].astype(F32)).astype(BF16)
        copies.append(pltpu.make_async_copy(sums.at[at], out_hbm.at[at], sems.at[i]))
        copies[-1].start()
    for copy in copies:
        copy.wait()


def spread_body(p0, p1, p2, p3, out_hbm, total, sems):
    even = p0[...].astype(F32) + p2[...].astype(F32)
    odd = p1[...].astype(F32) + p3[...].astype(F32)
    total[...] = (even + odd).astype(BF16)
    copies = []
    for i in range(out_hbm.shape[0]):
        copies.append(pltpu.make_async_copy(total, out_hbm.at[i], sems.at[i]))
        copies[-1].start()
    for copy in copies:
        copy.wait()


def shifted(block, axis, k):
    n = lax.axis_size(axis)
    return lax.ppermute(block, axis, [(i, (i + k) % n) for i in range(n)])


def to_far(block, k):
    slabs, subs = lax.axis_size(SLAB), lax.axis_size("z")
    pairs = [(i, i + 1) for i in range(1, slabs - 1, 2)]
    pairs += [(j, i) for i, j in pairs]
    route = [(i * subs + c, j * subs + (c + k) % subs) for i, j in pairs for c in range(subs)]
    return lax.ppermute(block, ALL, route)


def sds(shape, dtype=BF16):
    return jax.ShapeDtypeStruct(shape, dtype)


def shards(grid_x, mesh_h, gain_grid, gain_mesh, w_query, w_key, w_value, w_out, edge_bias,
           neighbours, valid, send_rows, out_grad):
    points, width = grid_x.shape
    nodes, fan = neighbours.shape
    cap = send_rows.shape[3]
    block = 4 * cap
    slots = 3 * block
    heads = edge_bias.shape[1] // fan
    sub1 = lax.axis_index("z").astype(jnp.int32).reshape(1)
    core1 = lax.axis_index("gc").astype(jnp.int32).reshape(1)
    gain_g, gain_m = gain_grid.reshape(1, width), gain_mesh.reshape(1, width)
    (grid_x, mesh_h, out_grad, send_rows, w_key, w_value, w_query, w_out, gain_g, gain_m, edge_bias,
     neighbours, valid) = (
        pltpu.with_memory_space_constraint(a, pltpu.HBM)
        for a in (grid_x, mesh_h, out_grad, send_rows, w_key, w_value, w_query, w_out, gain_g, gain_m,
                  edge_bias, neighbours, valid)
    )

    one, two, four = sds((cap, width)), sds((2 * cap, width)), sds((block, width))

    def exchange(near, own, far, sign):
        near = shifted(near, "gc", 1)
        far = [to_far(f, sign * k) for k, f in enumerate(far)]
        mixed = call(mix_body, [two] * 3, [VM] * 2, (own, near), 0, 1 << 20, "mix")
        mixed = [shifted(m, "z", sign * k) for k, m in enumerate(mixed, 1)]
        return near, own, *mixed, *far

    near, own, *far = call(
        gather_body, [four] * 2 + [one] * 4, [SM, SM, HB, HB, HB],
        (sub1, core1, send_rows, gain_g, grid_x), 1 << 30, 4 << 20, "gather_rows",
        held(send_rows, gain_g, grid_x)[:-1] + [pltpu.SemaphoreType.DMA((4,))],
    )
    received = exchange(near, own, far, 1)
    mesh_normed, queries, att_grad, og_near = call(
        mesh_in_body, [sds((nodes, width))] * 4, [HB] * 5, (mesh_h, gain_m, w_query, w_out, out_grad),
        1 << 28, 2 << 20, "mesh_in", held(mesh_h, gain_m, w_query, w_out)[:-1] + [pltpu.SemaphoreType.DMA((5,))],
    )
    sub2, near = lax.optimization_barrier((sub1, received[0]))
    (dense,) = call(
        slots_body, [sds((heads, nodes, slots), F32)], [SM] + [HB] * 3,
        (sub2, neighbours, valid, edge_bias), 1 << 30, 8 << 20, "slots",
        [pltpu.VMEM((nodes * 8, 128), F32), pltpu.VMEM((heads, nodes, 128), F32)]
        + held(neighbours, valid, edge_bias),
    )
    send, part_grads, attended, query_grad, weights_near, rows = call(
        middle_body,
        [sds((2 * width, width)), sds((slots, 2 * width))] + [sds((nodes, width))] * 2
        + [sds((width, 2 * width)), sds((slots, width))],
        [SM] + [VM] * 14 + [HB] * 2,
        (core1, *received, queries, att_grad, mesh_normed, og_near, dense, w_key, w_value),
        3 << 30, 8 << 20, "middle",
        [pltpu.VMEM((slots, width), BF16)] * 2 + [pltpu.SemaphoreType.DMA((2,))],
    )

    other = shifted(send, "gc", 1)
    (keep,) = call(
        keep_body, [sds((2 * width, width))], [SM] + [VM] * 6,
        (core1, rows, part_grads, mesh_normed, query_grad, attended, og_near), 1 << 29, 3 << 20, "keep",
    )
    near, own, *far = call(
        back_body, [four] * 2 + [one] * 4, [SM] + [VM] * 2, (core1, part_grads, weights_near),
        1 << 30, 3 << 20, "back",
    )
    other, near, keep = lax.optimization_barrier((other, near, keep))
    returned = exchange(near, own, far, -1)
    (sums,) = call(
        pair_body, [sds((2 * width, width))], [VM] * 2, (keep, other), 1 << 20, 3 << 20, "pair",
        [pltpu.VMEM((2 * width, width), BF16), pltpu.SemaphoreType.DMA((4,))], [HB],
    )
    plane = lax.axis_size(PLANE)
    share = 2 * width // plane
    parts = lax.all_to_all(sums.reshape(plane, share, width), PLANE, 0, 0, tiled=True)

    attended, sums = lax.optimization_barrier((attended, sums))
    mesh_out, mesh_grad = call(
        mesh_body, [sds((nodes, width))] * 2, [VM] * 3 + [HB] * 4,
        (attended, query_grad, og_near, w_out, w_query, mesh_h, gain_m), 1 << 28, 2 << 20, "mesh",
        held(w_out, w_query, mesh_h, gain_m),
    )
    parts, mesh_out, *returned = lax.optimization_barrier((parts, mesh_out, *returned))
    part = jnp.sum(parts.astype(F32), axis=0).astype(BF16)
    p1, p2, p3 = (shifted(part, "z", k) for k in (1, 2, 3))
    (spread,) = call(
        spread_body, [sds((plane, share, width))], [VM] * 4, (part, p1, p2, p3), 1 << 18, 1 << 20,
        "spread", [pltpu.VMEM((share, width), BF16), pltpu.SemaphoreType.DMA((plane,))], [HB],
    )
    mine = lax.all_to_all(spread, PLANE, 0, 0, tiled=True).reshape(2 * width, width)
    (grid_grad,) = call(
        grid_body, [sds((points, width))], [SM] * 2 + [VM] * 9 + [HB] * 3,
        (sub1, core1, *returned, send_rows, gain_g, grid_x),
        1 << 30, 5 << 20, "grid_grad",
        [pltpu.VMEM((slots, width), BF16), pltpu.VMEM((points, width), BF16),
         pltpu.SemaphoreType.DMA((points // 256,))] + held(send_rows, gain_g, grid_x),
        [HB],
    )
    mine, grid_grad = lax.optimization_barrier((mine, grid_grad))
    theirs = shifted(mine, "gc", 1)
    whole = sds((4, width, width), F32)
    wide = [pltpu.VMEM((2, width, width), F32), pltpu.SemaphoreType.DMA((4,))]
    (weight_grads,) = call(
        functools.partial(widen_body, 0), [whole], [SM, VM], (core1, mine), 1 << 20, 3 << 20, "widen_own",
        wide, [HB],
    )
    (weight_grads,) = call(
        functools.partial(widen_body, 1), [whole], [SM, VM, HB], (core1, theirs, weight_grads),
        1 << 20, 3 << 20, "widen_other", wide, [HB], {2: 0},
    )
    return mesh_out, mesh_grad, grid_grad, weight_grads


def solution(mesh):
    split = Mesh(mesh.devices.reshape(4, 4, 2, mesh.shape["sub"]), ALL)
    rows = P(ALL, None)
    return jax.shard_map(
        shards,
        mesh=split,
        in_specs=(rows, rows, P(), P(), P(), P(), P(), P(), rows, rows, rows,
                  P(ALL, None, None, None), rows),
        out_specs=(rows, rows, rows, P()),
        check_vma=False,
    )
```

```python
import functools

import jax
import jax.numpy as jnp
from jax import lax
from jax.experimental import pallas as pl
from jax.experimental.pallas import tpu as pltpu
from jax.sharding import Mesh
from jax.sharding import PartitionSpec as P

SLAB = ("gx", "gy", "gc")
PLANE = ("gx", "gy")
ALL = ("gx", "gy", "gc", "z")

EPSILON = 1e-06
ABSENT = -1e30
F32 = jnp.float32
BF16 = jnp.bfloat16

VM = pl.BlockSpec(memory_space=pltpu.VMEM)
SM = pl.BlockSpec(memory_space=pltpu.SMEM)
HB = pl.BlockSpec(memory_space=pltpu.HBM)


def nn(a, b):
    return lax.dot_general(a, b, (((1,), (0,)), ((), ())), preferred_element_type=F32)


def nt(a, b):
    return lax.dot_general(a, b, (((1,), (1,)), ((), ())), preferred_element_type=F32)


def tn(a, b):
    return lax.dot_general(a, b, (((0,), (0,)), ((), ())), preferred_element_type=F32)


def inv_rms(wide):
    return lax.rsqrt(jnp.mean(wide * wide, axis=-1, keepdims=True) + EPSILON)


def norm_back(wide, factor, gain_row, upstream):
    scaled = gain_row * upstream
    inner = jnp.mean(wide * scaled, axis=-1, keepdims=True)
    return factor * scaled - wide * (factor * factor * factor * inner)


def call(body, outs, in_specs, args, flops, nbytes, name, scratch=(), out_specs=None, aliases=None):
    return pl.pallas_call(
        body,
        out_shape=outs,
        in_specs=in_specs,
        out_specs=out_specs or [VM] * len(outs),
        scratch_shapes=list(scratch),
        input_output_aliases=aliases or {},
        compiler_params=pltpu.CompilerParams(vmem_limit_bytes=24 << 20),
        cost_estimate=pl.CostEstimate(flops=flops, bytes_accessed=nbytes, transcendentals=0),
        name=name,
    )(*args)


def fetch(sources, targets, sems):
    copies = []
    for i, (source, target) in enumerate(zip(sources, targets)):
        copies.append(pltpu.make_async_copy(source, target, sems.at[i]))
        copies[-1].start()
    return copies


def held(*args):
    return [pltpu.VMEM(a.shape, a.dtype) for a in args] + [pltpu.SemaphoreType.DMA((len(args),))]


def assemble(rows, near_first, near, far, own, *pieces):
    block = near.shape[0]
    cap = block // 4
    near_at = pl.multiple_of((1 - near_first) * (2 * block), block)
    far_at = pl.multiple_of(near_first * (2 * block), block)
    rows[block : block + cap] = own[0:cap]
    rows[pl.ds(near_at, cap), :] = near[0:cap]
    rows[pl.ds(far_at, cap), :] = far[0:cap]
    for k in range(1, 4):
        mixed, last = pieces[k - 1], pieces[len(pieces) - 4 + k]
        rows[block + k * cap : block + (k + 1) * cap] = mixed[0:cap]
        rows[pl.ds(near_at + k * cap, cap), :] = mixed[cap : 2 * cap]
        rows[pl.ds(far_at + k * cap, cap), :] = last[last.shape[0] - cap :]


def gather_body(sub_ref, core_ref, rows_hbm, gain_hbm, x_hbm, near_ref, far_ref, own_ref,
                rows_ref, gain_ref, x_ref, sems):
    half = x_ref.shape[0] // 2
    cap = rows_ref.shape[3]
    core = core_ref[0]
    firsts = [pl.multiple_of((1 - core) * half, half), pl.multiple_of(core * half, half)]
    parts = [pl.ds(first, half) for first in firsts]
    copies = fetch(
        [rows_hbm, gain_hbm] + [x_hbm.at[p] for p in parts],
        [rows_ref, gain_ref] + [x_ref.at[p] for p in parts],
        sems,
    )
    copies[0].wait()
    copies[1].wait()
    me = sub_ref[0]
    eye = lax.broadcasted_iota(jnp.int32, (cap, cap), 0) == lax.broadcasted_iota(
        jnp.int32, (cap, cap), 1
    )
    gain = gain_ref[...]
    steps = (
        (2 - 2 * core, firsts[0], half, near_ref),
        (2 * core, firsts[1], half, far_ref),
        (1, 0, 2 * half, own_ref),
    )
    for step, (o, first, count, out_ref) in enumerate(steps):
        cols = []
        for k in range(4):
            s = lax.rem(me + k, 4)
            row = rows_ref[0, o, pl.ds(s, 1), :].astype(F32)
            cols.append(jnp.sum(jnp.where(eye, row, 0.0), axis=1, keepdims=True))
        col = jnp.concatenate(cols, axis=0).astype(jnp.int32) - first
        lanes = lax.broadcasted_iota(jnp.int32, (4 * cap, count), 1)
        onehot = jnp.where(lanes == col, 1.0, 0.0).astype(BF16)
        if step < 2:
            copies[2 + step].wait()
        wide = nn(onehot, x_ref[pl.ds(first, count), :])
        out_ref[...] = (wide * inv_rms(wide) * gain).astype(BF16)


def mesh_in_body(mesh_hbm, gain_hbm, wq_hbm, wo_hbm, og_hbm, normed_ref, q_ref, ag_ref, og_ref,
                 mesh_ref, gain_ref, wq_ref, wo_ref, sems):
    copies = fetch(
        (mesh_hbm, gain_hbm, wq_hbm, wo_hbm, og_hbm), (mesh_ref, gain_ref, wq_ref, wo_ref, og_ref), sems
    )
    for copy in copies:
        copy.wait()
    wide = mesh_ref[...].astype(F32)
    normed = (wide * inv_rms(wide) * gain_ref[...]).astype(BF16)
    normed_ref[...] = normed
    q_ref[...] = (nn(normed, wq_ref[...]) * (128 ** -0.5)).astype(BF16)
    ag_ref[...] = nt(og_ref[...], wo_ref[...]).astype(BF16)


def slots_body(sub_ref, nbr_hbm, valid_hbm, bias_hbm, dense_ref, inv_ref, edge_ref,
               nbr_ref, valid_ref, bias_ref, sems):
    copies = fetch((nbr_hbm, valid_hbm, bias_hbm), (nbr_ref, valid_ref, bias_ref), sems)
    heads, nodes, slots = dense_ref.shape
    fan = nbr_ref.shape[1]
    for copy in copies:
        copy.wait()
    slot = nbr_ref[...]
    slot = (slot & ~192) | (((sub_ref[0] - (slot >> 6)) & 3) << 6)
    high, low = slot >> 7, slot & 127
    blocks = lax.broadcasted_iota(jnp.int32, (8, fan), 0)
    lanes = lax.broadcasted_iota(jnp.int32, (128, fan), 0)
    edge = lax.broadcasted_iota(jnp.int32, (8, fan), 1).astype(F32) + 1.0
    for m in range(nodes):
        named = jnp.where(high[m : m + 1, :] == blocks, edge, 0.0).astype(BF16)
        places = jnp.where(low[m : m + 1, :] == lanes, 1.0, 0.0).astype(BF16)
        inv_ref[m * 8 : (m + 1) * 8, :] = nt(named, places)
    live = valid_ref[...] == 1
    for h in range(heads):
        edge_ref[h, :, 0:fan] = jnp.where(live, bias_ref[:, h * fan : (h + 1) * fan], ABSENT)
    for b in range(slots // 128):
        at = inv_ref[pl.ds(b, nodes, stride=8), :].astype(jnp.int32) - 1
        here = at >= 0
        at = jnp.maximum(at, 0)
        for h in range(heads):
            got = jnp.take_along_axis(edge_ref[h], at, axis=1, mode="promise_in_bounds")
            dense_ref[h, :, b * 128 : (b + 1) * 128] = jnp.where(here, got, ABSENT)


def middle_body(core_ref, near, far, own, m1, m2, m3, f1, f2, f3, q_ref, ag_ref, mn_ref, og_ref,
                bias_ref, wk_hbm, wv_hbm, send_ref, part_ref, att_ref, qg_ref, wkv_ref, rows,
                keys, vals, sems):
    width = q_ref.shape[1]
    copies = fetch(
        (wk_hbm, wv_hbm), (wkv_ref.at[:, pl.ds(0, width)], wkv_ref.at[:, pl.ds(width, width)]), sems
    )
    heads = bias_ref.shape[0]
    core = core_ref[0]
    assemble(rows, 1 - core, near, far, own, m1, m2, m3, f1, f2, f3)
    copies[0].wait()
    keys[...] = nn(rows[...], wkv_ref[:, :width]).astype(BF16)
    copies[1].wait()
    vals[...] = nn(rows[...], wkv_ref[:, width:]).astype(BF16)
    for h in range(heads):
        at = slice(h * 128, (h + 1) * 128)
        q, ag = q_ref[:, at], ag_ref[:, at]
        kh, vh = keys[:, at], vals[:, at]
        scores = nt(q, kh) + bias_ref[h]
        peak = jnp.max(scores, axis=1, keepdims=True)
        terms = jnp.exp(scores - peak)
        probs = terms / jnp.sum(terms, axis=1, keepdims=True)
        probs_b = probs.astype(BF16)
        att_ref[:, at] = nn(probs_b, vh).astype(BF16)
        pg = nt(ag, vh)
        sg = (probs * (pg - jnp.sum(probs * pg, axis=1, keepdims=True))).astype(BF16)
        qg_ref[:, at] = (nn(sg, kh) * (128 ** -0.5)).astype(BF16)
        part_ref[:, at] = tn(sg, q).astype(BF16)
        part_ref[:, width + h * 128 : width + (h + 1) * 128] = tn(probs_b, ag).astype(BF16)
    half_grads(1 - core, send_ref, rows, part_ref, mn_ref, qg_ref, att_ref, og_ref)


def half_grads(half, out_ref, rows, part_ref, mn_ref, qg_ref, att_ref, og_ref):
    width = mn_ref.shape[1]
    first = half == 0
    left = jnp.where(first, mn_ref[...].astype(F32), att_ref[...].astype(F32)).astype(BF16)
    right = jnp.where(first, qg_ref[...].astype(F32), og_ref[...].astype(F32)).astype(BF16)
    columns = pl.ds(pl.multiple_of(half * width, width), width)
    out_ref[0:width] = tn(left, right).astype(BF16)
    out_ref[width : 2 * width] = tn(rows[...], part_ref[:, columns]).astype(BF16)


def keep_body(core_ref, rows, part_ref, mn_ref, qg_ref, att_ref, og_ref, keep_ref):
    half_grads(core_ref[0], keep_ref, rows, part_ref, mn_ref, qg_ref, att_ref, og_ref)


def back_body(part_ref, wkv_ref, s0, s1, s2, s3):
    cap = s0.shape[1]
    for o in range(3):
        rows = slice(o * 4 * cap, (o + 1) * 4 * cap)
        back = nt(part_ref[rows, :], wkv_ref[...]).astype(BF16)
        for k, piece in enumerate((s0, s1, s2, s3)):
            piece[o] = back[k * cap : (k + 1) * cap]


def mesh_body(att_ref, qg_ref, og_ref, wo_hbm, wq_hbm, mesh_hbm, gain_hbm, out_ref, grad_ref,
              wo_ref, wq_ref, mesh_ref, gain_ref, sems):
    copies = fetch(
        (wo_hbm, wq_hbm, mesh_hbm, gain_hbm), (wo_ref, wq_ref, mesh_ref, gain_ref), sems
    )
    for copy in copies:
        copy.wait()
    wide = mesh_ref[...].astype(F32)
    out_ref[...] = (wide + nn(att_ref[...], wo_ref[...])).astype(BF16)
    upstream = nt(qg_ref[...], wq_ref[...])
    back = norm_back(wide, inv_rms(wide), gain_ref[...], upstream)
    grad_ref[...] = (og_ref[...].astype(F32) + back).astype(BF16)


def pack_body(core_ref, p0, p1, p2, p3, near_ref, far_ref):
    cap = p0.shape[1]
    near = core_ref[0] * 2
    for k, piece in enumerate((p0, p1, p2, p3)):
        near_ref[k * cap : (k + 1) * cap, :] = piece[near]
        far_ref[k * cap : (k + 1) * cap, :] = piece[2 - near]


def mix_body(own, near, m1, m2, m3):
    cap = m1.shape[0] // 2
    for k, mixed in enumerate((m1, m2, m3), 1):
        mixed[0:cap] = own[k * cap : (k + 1) * cap]
        mixed[cap : 2 * cap] = near[k * cap : (k + 1) * cap]


def split_body(block, f1, f2, f3):
    cap = f1.shape[0]
    for k, piece in enumerate((f1, f2, f3), 1):
        piece[...] = block[k * cap : (k + 1) * cap]


def grid_body(turn, sub_ref, core_ref, outer, s0, s1, s2, s3, rows_hbm, gain_hbm, x_hbm, *refs):
    out_hbm, got, done_ref, done_sems, rows_ref, gain_ref, x_ref, sems = refs[-8:]
    half = x_ref.shape[0]
    upper = (1 - core_ref[0]) if turn == 0 else core_ref[0]
    base = pl.multiple_of(upper * half, half)
    copies = fetch((rows_hbm, gain_hbm, x_hbm.at[pl.ds(base, half)]), (rows_ref, gain_ref, x_ref), sems)
    cap = rows_ref.shape[3]
    block = 4 * cap
    me = sub_ref[0]
    got[0:block] = outer[...]
    for k, piece in enumerate((s0, s1, s2, s3)):
        got[block + k * cap : block + (k + 1) * cap] = piece[1]
    for copy in copies:
        copy.wait()
    gain = gain_ref[...]
    idx = []
    for o in (2 * upper, 1):
        for k in range(4):
            idx.append(rows_ref[0, o, pl.ds(lax.rem(me + k, 4), 1), :])
    idx = jnp.concatenate(idx, axis=1) - base
    tile = 256
    stores = []
    for t in range(half // tile):
        part = slice(t * tile, (t + 1) * tile)
        ids = lax.broadcasted_iota(jnp.int32, (tile, 2 * block), 0) + t * tile
        onehot = jnp.where(ids == idx, 1.0, 0.0).astype(BF16)
        upstream = nn(onehot, got[...])
        wide = x_ref[part, :].astype(F32)
        done_ref[part, :] = norm_back(wide, inv_rms(wide), gain, upstream).astype(BF16)
        stores.append(
            pltpu.make_async_copy(
                done_ref.at[part], out_hbm.at[pl.ds(base + t * tile, tile)], done_sems.at[t]
            )
        )
        stores[-1].start()
    for store in stores:
        store.wait()


def widen_body(turn, core_ref, half_ref, *refs):
    out_hbm, wide, sems = refs[-3:]
    count, width, _ = wide.shape
    half = core_ref[0] ^ turn
    part = width // 2
    copies = []
    for i in range(2 * count):
        m, rows = i // 2, pl.ds((i % 2) * part, part)
        wide[m, rows, :] = half_ref[i * part : (i + 1) * part, :].astype(F32)
        copies.append(
            pltpu.make_async_copy(
                wide.at[m, rows], out_hbm.at[lax.select(half == 0, m, 3 - m), rows], sems.at[i]
            )
        )
        copies[-1].start()
    for copy in copies:
        copy.wait()


def pair_body(keep_ref, other_ref, out_hbm, sums, sems):
    part = sums.shape[0] // 4
    copies = []
    for i in range(4):
        at = slice(i * part, (i + 1) * part)
        sums[at, :] = (keep_ref[at, :].astype(F32) + other_ref[at, :].astype(F32)).astype(BF16)
        copies.append(pltpu.make_async_copy(sums.at[at], out_hbm.at[at], sems.at[i]))
        copies[-1].start()
    for copy in copies:
        copy.wait()


def spread_body(p0, p1, p2, p3, out_hbm, total, sems):
    even = p0[...].astype(F32) + p2[...].astype(F32)
    odd = p1[...].astype(F32) + p3[...].astype(F32)
    total[...] = (even + odd).astype(BF16)
    copies = []
    for i in range(out_hbm.shape[0]):
        copies.append(pltpu.make_async_copy(total, out_hbm.at[i], sems.at[i]))
        copies[-1].start()
    for copy in copies:
        copy.wait()


def shifted(block, axis, k):
    n = lax.axis_size(axis)
    return lax.ppermute(block, axis, [(i, (i + k) % n) for i in range(n)])


def swapped_far(block):
    n = lax.axis_size(SLAB)
    pairs = [(i, i + 1) for i in range(1, n - 1, 2)]
    return lax.ppermute(block, SLAB, pairs + [(j, i) for i, j in pairs])


def sds(shape, dtype=BF16):
    return jax.ShapeDtypeStruct(shape, dtype)


def shards(grid_x, mesh_h, gain_grid, gain_mesh, w_query, w_key, w_value, w_out, edge_bias,
           neighbours, valid, send_rows, out_grad):
    points, width = grid_x.shape
    nodes, fan = neighbours.shape
    cap = send_rows.shape[3]
    block = 4 * cap
    slots = 3 * block
    heads = edge_bias.shape[1] // fan
    sub1 = lax.axis_index("z").astype(jnp.int32).reshape(1)
    core1 = lax.axis_index("gc").astype(jnp.int32).reshape(1)
    gain_g, gain_m = gain_grid.reshape(1, width), gain_mesh.reshape(1, width)
    (grid_x, mesh_h, out_grad, send_rows, w_key, w_value, w_query, w_out, gain_g, gain_m, edge_bias,
     neighbours, valid) = (
        pltpu.with_memory_space_constraint(a, pltpu.HBM)
        for a in (grid_x, mesh_h, out_grad, send_rows, w_key, w_value, w_query, w_out, gain_g, gain_m,
                  edge_bias, neighbours, valid)
    )

    one, two, four = sds((cap, width)), sds((2 * cap, width)), sds((block, width))
    near, far, own = call(
        gather_body, [four] * 3, [SM, SM, HB, HB, HB],
        (sub1, core1, send_rows, gain_g, grid_x), 1 << 30, 4 << 20, "gather_rows",
        held(send_rows, gain_g, grid_x)[:-1] + [pltpu.SemaphoreType.DMA((4,))],
    )

    far = swapped_far(far)
    near = shifted(near, "gc", 1)
    mixed = call(mix_body, [two] * 3, [VM] * 2, (own, near), 0, 1 << 20, "mix")
    mixed = [shifted(m, "z", k) for k, m in enumerate(mixed, 1)]
    mesh_normed, queries, att_grad, og_near = call(
        mesh_in_body, [sds((nodes, width))] * 4, [HB] * 5, (mesh_h, gain_m, w_query, w_out, out_grad),
        1 << 28, 2 << 20, "mesh_in", held(mesh_h, gain_m, w_query, w_out)[:-1] + [pltpu.SemaphoreType.DMA((5,))],
    )
    far, mixed[0], queries = lax.optimization_barrier((far, mixed[0], queries))
    outer = call(split_body, [one] * 3, [VM], (far,), 0, 1 << 19, "split")
    outer = [shifted(f, "z", k) for k, f in enumerate(outer, 1)]
    received = near, far, own, *mixed, *outer
    sub2, far = lax.optimization_barrier((sub1, far))
    (dense,) = call(
        slots_body, [sds((heads, nodes, slots), F32)], [SM] + [HB] * 3,
        (sub2, neighbours, valid, edge_bias), 1 << 30, 8 << 20, "slots",
        [pltpu.VMEM((nodes * 8, 128), F32), pltpu.VMEM((heads, nodes, 128), F32)]
        + held(neighbours, valid, edge_bias),
    )
    send, part_grads, attended, query_grad, weights_near, rows = call(
        middle_body,
        [sds((2 * width, width)), sds((slots, 2 * width))] + [sds((nodes, width))] * 2
        + [sds((width, 2 * width)), sds((slots, width))],
        [SM] + [VM] * 14 + [HB] * 2,
        (core1, *received, queries, att_grad, mesh_normed, og_near, dense, w_key, w_value),
        3 << 30, 8 << 20, "middle",
        [pltpu.VMEM((slots, width), BF16)] * 2 + [pltpu.SemaphoreType.DMA((2,))],
    )

    other = shifted(send, "gc", 1)
    (keep,) = call(
        keep_body, [sds((2 * width, width))], [SM] + [VM] * 6,
        (core1, rows, part_grads, mesh_normed, query_grad, attended, og_near), 1 << 29, 3 << 20, "keep",
    )
    s0, s1, s2, s3 = call(
        back_body, [sds((3, cap, width))] * 4, [VM] * 2, (part_grads, weights_near),
        1 << 30, 3 << 20, "back",
    )
    other, s1, keep = lax.optimization_barrier((other, s1, keep))
    (own,) = call(
        pair_body, [sds((2 * width, width))], [VM] * 2, (keep, other), 1 << 20, 3 << 20, "pair",
        [pltpu.VMEM((2 * width, width), BF16), pltpu.SemaphoreType.DMA((4,))], [HB],
    )
    plane = lax.axis_size(PLANE)
    share = 2 * width // plane
    parts = lax.all_to_all(own.reshape(plane, share, width), PLANE, 0, 0, tiled=True)

    attended, own = lax.optimization_barrier((attended, own))
    mesh_out, mesh_grad = call(
        mesh_body, [sds((nodes, width))] * 2, [VM] * 3 + [HB] * 4,
        (attended, query_grad, og_near, w_out, w_query, mesh_h, gain_m), 1 << 28, 2 << 20, "mesh",
        held(w_out, w_query, mesh_h, gain_m),
    )
    s1, s2, s3 = (shifted(s, "z", -k) for k, s in ((1, s1), (2, s2), (3, s3)))
    s1, s2, s3, parts, mesh_out = lax.optimization_barrier((s1, s2, s3, parts, mesh_out))
    part = jnp.sum(parts.astype(F32), axis=0).astype(BF16)
    part, s0 = lax.optimization_barrier((part, s0))
    near, far = call(
        pack_body, [four] * 2, [SM] + [VM] * 4, (core1, s0, s1, s2, s3), 0, 1 << 20, "pack"
    )
    far = swapped_far(far)
    near = shifted(near, "gc", 1)
    p1, p2, p3 = (shifted(part, "z", k) for k in (1, 2, 3))
    (spread,) = call(
        spread_body, [sds((plane, share, width))], [VM] * 4, (part, p1, p2, p3), 1 << 18, 1 << 20,
        "spread", [pltpu.VMEM((share, width), BF16), pltpu.SemaphoreType.DMA((plane,))], [HB],
    )
    mine = lax.all_to_all(spread, PLANE, 0, 0, tiled=True).reshape(2 * width, width)
    half = points // 2
    grid_scratch = [
        pltpu.VMEM((2 * block, width), BF16), pltpu.VMEM((half, width), BF16),
        pltpu.SemaphoreType.DMA((half // 256,)), pltpu.VMEM(send_rows.shape, send_rows.dtype),
        pltpu.VMEM(gain_g.shape, F32), pltpu.VMEM((half, width), BF16), pltpu.SemaphoreType.DMA((3,)),
    ]
    grid_specs = [SM] * 2 + [VM] * 5 + [HB] * 3
    (grid_grad,) = call(
        functools.partial(grid_body, 0), [sds((points, width))], grid_specs,
        (sub1, core1, near, s0, s1, s2, s3, send_rows, gain_g, grid_x),
        1 << 29, 3 << 20, "grid_near", grid_scratch, [HB],
    )
    (grid_grad,) = call(
        functools.partial(grid_body, 1), [sds((points, width))], grid_specs + [HB],
        (sub1, core1, far, s0, s1, s2, s3, send_rows, gain_g, grid_x, grid_grad),
        1 << 29, 3 << 20, "grid_far", grid_scratch, [HB], {10: 0},
    )
    mine, grid_grad = lax.optimization_barrier((mine, grid_grad))
    theirs = shifted(mine, "gc", 1)
    whole = sds((4, width, width), F32)
    wide = [pltpu.VMEM((2, width, width), F32), pltpu.SemaphoreType.DMA((4,))]
    (weight_grads,) = call(
        functools.partial(widen_body, 0), [whole], [SM, VM], (core1, mine), 1 << 20, 3 << 20, "widen_own",
        wide, [HB],
    )
    (weight_grads,) = call(
        functools.partial(widen_body, 1), [whole], [SM, VM, HB], (core1, theirs, weight_grads),
        1 << 20, 3 << 20, "widen_other", wide, [HB], {2: 0},
    )
    return mesh_out, mesh_grad, grid_grad, weight_grads


def solution(mesh):
    split = Mesh(mesh.devices.reshape(4, 4, 2, mesh.shape["sub"]), ALL)
    rows = P(ALL, None)
    return jax.shard_map(
        shards,
        mesh=split,
        in_specs=(rows, rows, P(), P(), P(), P(), P(), P(), rows, rows, rows,
                  P(ALL, None, None, None), rows),
        out_specs=(rows, rows, rows, P()),
        check_vma=False,
    )
```

```python
import functools

import jax
import jax.numpy as jnp
from jax import lax
from jax.experimental import pallas as pl
from jax.experimental.pallas import tpu as pltpu
from jax.sharding import Mesh
from jax.sharding import PartitionSpec as P

SLAB = ("gx", "gy", "gc")
PLANE = ("gx", "gy")
ALL = ("gx", "gy", "gc", "z")

EPSILON = 1e-06
ABSENT = -1e30
F32 = jnp.float32
BF16 = jnp.bfloat16

VM = pl.BlockSpec(memory_space=pltpu.VMEM)
SM = pl.BlockSpec(memory_space=pltpu.SMEM)
HB = pl.BlockSpec(memory_space=pltpu.HBM)


def nn(a, b):
    return lax.dot_general(a, b, (((1,), (0,)), ((), ())), preferred_element_type=F32)


def nt(a, b):
    return lax.dot_general(a, b, (((1,), (1,)), ((), ())), preferred_element_type=F32)


def tn(a, b):
    return lax.dot_general(a, b, (((0,), (0,)), ((), ())), preferred_element_type=F32)


def inv_rms(wide):
    return lax.rsqrt(jnp.mean(wide * wide, axis=-1, keepdims=True) + EPSILON)


def norm_back(wide, factor, gain_row, upstream):
    scaled = gain_row * upstream
    inner = jnp.mean(wide * scaled, axis=-1, keepdims=True)
    return factor * scaled - wide * (factor * factor * factor * inner)


def call(body, outs, in_specs, args, flops, nbytes, name, scratch=(), out_specs=None, aliases=None):
    return pl.pallas_call(
        body,
        out_shape=outs,
        in_specs=in_specs,
        out_specs=out_specs or [VM] * len(outs),
        scratch_shapes=list(scratch),
        input_output_aliases=aliases or {},
        compiler_params=pltpu.CompilerParams(vmem_limit_bytes=24 << 20),
        cost_estimate=pl.CostEstimate(flops=flops, bytes_accessed=nbytes, transcendentals=0),
        name=name,
    )(*args)


def fetch(sources, targets, sems):
    copies = []
    for i, (source, target) in enumerate(zip(sources, targets)):
        copies.append(pltpu.make_async_copy(source, target, sems.at[i]))
        copies[-1].start()
    return copies


def held(*args):
    return [pltpu.VMEM(a.shape, a.dtype) for a in args] + [pltpu.SemaphoreType.DMA((len(args),))]


def assemble(rows, near_first, near, far, own, *pieces):
    block = near.shape[0]
    cap = block // 4
    near_at = pl.multiple_of((1 - near_first) * (2 * block), block)
    far_at = pl.multiple_of(near_first * (2 * block), block)
    rows[block : block + cap] = own[0:cap]
    rows[pl.ds(near_at, cap), :] = near[0:cap]
    rows[pl.ds(far_at, cap), :] = far[0:cap]
    for k in range(1, 4):
        mixed, last = pieces[k - 1], pieces[len(pieces) - 4 + k]
        rows[block + k * cap : block + (k + 1) * cap] = mixed[0:cap]
        rows[pl.ds(near_at + k * cap, cap), :] = mixed[cap : 2 * cap]
        rows[pl.ds(far_at + k * cap, cap), :] = last[last.shape[0] - cap :]


def gather_body(sub_ref, core_ref, rows_hbm, gain_hbm, x_hbm, near_ref, far_ref, own_ref,
                rows_ref, gain_ref, x_ref, sems):
    half = x_ref.shape[0] // 2
    cap = rows_ref.shape[3]
    core = core_ref[0]
    firsts = [pl.multiple_of((1 - core) * half, half), pl.multiple_of(core * half, half)]
    parts = [pl.ds(first, half) for first in firsts]
    copies = fetch(
        [rows_hbm, gain_hbm] + [x_hbm.at[p] for p in parts],
        [rows_ref, gain_ref] + [x_ref.at[p] for p in parts],
        sems,
    )
    copies[0].wait()
    copies[1].wait()
    me = sub_ref[0]
    eye = lax.broadcasted_iota(jnp.int32, (cap, cap), 0) == lax.broadcasted_iota(
        jnp.int32, (cap, cap), 1
    )
    gain = gain_ref[...]
    steps = (
        (2 - 2 * core, firsts[0], half, near_ref),
        (2 * core, firsts[1], half, far_ref),
        (1, 0, 2 * half, own_ref),
    )
    for step, (o, first, count, out_ref) in enumerate(steps):
        cols = []
        for k in range(4):
            s = lax.rem(me + k, 4)
            row = rows_ref[0, o, pl.ds(s, 1), :].astype(F32)
            cols.append(jnp.sum(jnp.where(eye, row, 0.0), axis=1, keepdims=True))
        col = jnp.concatenate(cols, axis=0).astype(jnp.int32) - first
        lanes = lax.broadcasted_iota(jnp.int32, (4 * cap, count), 1)
        onehot = jnp.where(lanes == col, 1.0, 0.0).astype(BF16)
        if step < 2:
            copies[2 + step].wait()
        wide = nn(onehot, x_ref[pl.ds(first, count), :])
        out_ref[...] = (wide * inv_rms(wide) * gain).astype(BF16)


def mesh_in_body(mesh_hbm, gain_hbm, wq_hbm, wo_hbm, og_hbm, normed_ref, q_ref, ag_ref, og_ref,
                 mesh_ref, gain_ref, wq_ref, wo_ref, sems):
    copies = fetch(
        (mesh_hbm, gain_hbm, wq_hbm, wo_hbm, og_hbm), (mesh_ref, gain_ref, wq_ref, wo_ref, og_ref), sems
    )
    for copy in copies:
        copy.wait()
    wide = mesh_ref[...].astype(F32)
    normed = (wide * inv_rms(wide) * gain_ref[...]).astype(BF16)
    normed_ref[...] = normed
    q_ref[...] = (nn(normed, wq_ref[...]) * (128 ** -0.5)).astype(BF16)
    ag_ref[...] = nt(og_ref[...], wo_ref[...]).astype(BF16)


def slots_body(sub_ref, nbr_hbm, valid_hbm, bias_hbm, dense_ref, inv_ref, edge_ref,
               nbr_ref, valid_ref, bias_ref, sems):
    copies = fetch((nbr_hbm, valid_hbm, bias_hbm), (nbr_ref, valid_ref, bias_ref), sems)
    heads, nodes, slots = dense_ref.shape
    fan = nbr_ref.shape[1]
    for copy in copies:
        copy.wait()
    slot = nbr_ref[...]
    slot = (slot & ~192) | (((sub_ref[0] - (slot >> 6)) & 3) << 6)
    high, low = slot >> 7, slot & 127
    blocks = lax.broadcasted_iota(jnp.int32, (8, fan), 0)
    lanes = lax.broadcasted_iota(jnp.int32, (128, fan), 0)
    edge = lax.broadcasted_iota(jnp.int32, (8, fan), 1).astype(F32) + 1.0
    for m in range(nodes):
        named = jnp.where(high[m : m + 1, :] == blocks, edge, 0.0).astype(BF16)
        places = jnp.where(low[m : m + 1, :] == lanes, 1.0, 0.0).astype(BF16)
        inv_ref[m * 8 : (m + 1) * 8, :] = nt(named, places)
    live = valid_ref[...] == 1
    for h in range(heads):
        edge_ref[h, :, 0:fan] = jnp.where(live, bias_ref[:, h * fan : (h + 1) * fan], ABSENT)
    for b in range(slots // 128):
        at = inv_ref[pl.ds(b, nodes, stride=8), :].astype(jnp.int32) - 1
        here = at >= 0
        at = jnp.maximum(at, 0)
        for h in range(heads):
            got = jnp.take_along_axis(edge_ref[h], at, axis=1, mode="promise_in_bounds")
            dense_ref[h, :, b * 128 : (b + 1) * 128] = jnp.where(here, got, ABSENT)


def middle_body(core_ref, near, far, own, m1, m2, m3, f1, f2, f3, q_ref, ag_ref, mn_ref, og_ref,
                bias_ref, wk_hbm, wv_hbm, send_ref, part_ref, att_ref, qg_ref, wkv_ref, rows,
                keys, vals, sems):
    width = q_ref.shape[1]
    copies = fetch(
        (wk_hbm, wv_hbm), (wkv_ref.at[:, pl.ds(0, width)], wkv_ref.at[:, pl.ds(width, width)]), sems
    )
    heads = bias_ref.shape[0]
    core = core_ref[0]
    assemble(rows, 1 - core, near, far, own, m1, m2, m3, f1, f2, f3)
    copies[0].wait()
    keys[...] = nn(rows[...], wkv_ref[:, :width]).astype(BF16)
    copies[1].wait()
    vals[...] = nn(rows[...], wkv_ref[:, width:]).astype(BF16)
    for h in range(heads):
        at = slice(h * 128, (h + 1) * 128)
        q, ag = q_ref[:, at], ag_ref[:, at]
        kh, vh = keys[:, at], vals[:, at]
        scores = nt(q, kh) + bias_ref[h]
        peak = jnp.max(scores, axis=1, keepdims=True)
        terms = jnp.exp(scores - peak)
        probs = terms / jnp.sum(terms, axis=1, keepdims=True)
        probs_b = probs.astype(BF16)
        att_ref[:, at] = nn(probs_b, vh).astype(BF16)
        pg = nt(ag, vh)
        sg = (probs * (pg - jnp.sum(probs * pg, axis=1, keepdims=True))).astype(BF16)
        qg_ref[:, at] = (nn(sg, kh) * (128 ** -0.5)).astype(BF16)
        part_ref[:, at] = tn(sg, q).astype(BF16)
        part_ref[:, width + h * 128 : width + (h + 1) * 128] = tn(probs_b, ag).astype(BF16)
    half_grads(1 - core, send_ref, rows, part_ref, mn_ref, qg_ref, att_ref, og_ref)


def half_grads(half, out_ref, rows, part_ref, mn_ref, qg_ref, att_ref, og_ref):
    width = mn_ref.shape[1]
    first = half == 0
    left = jnp.where(first, mn_ref[...].astype(F32), att_ref[...].astype(F32)).astype(BF16)
    right = jnp.where(first, qg_ref[...].astype(F32), og_ref[...].astype(F32)).astype(BF16)
    columns = pl.ds(pl.multiple_of(half * width, width), width)
    out_ref[0:width] = tn(left, right).astype(BF16)
    out_ref[width : 2 * width] = tn(rows[...], part_ref[:, columns]).astype(BF16)


def keep_body(core_ref, rows, part_ref, mn_ref, qg_ref, att_ref, og_ref, keep_ref):
    half_grads(core_ref[0], keep_ref, rows, part_ref, mn_ref, qg_ref, att_ref, og_ref)


def back_body(part_ref, wkv_ref, s0, s1, s2, s3):
    cap = s0.shape[1]
    for o in range(3):
        rows = slice(o * 4 * cap, (o + 1) * 4 * cap)
        back = nt(part_ref[rows, :], wkv_ref[...]).astype(BF16)
        for k, piece in enumerate((s0, s1, s2, s3)):
            piece[o] = back[k * cap : (k + 1) * cap]


def mesh_body(att_ref, qg_ref, og_ref, wo_hbm, wq_hbm, mesh_hbm, gain_hbm, out_ref, grad_ref,
              wo_ref, wq_ref, mesh_ref, gain_ref, sems):
    copies = fetch(
        (wo_hbm, wq_hbm, mesh_hbm, gain_hbm), (wo_ref, wq_ref, mesh_ref, gain_ref), sems
    )
    for copy in copies:
        copy.wait()
    wide = mesh_ref[...].astype(F32)
    out_ref[...] = (wide + nn(att_ref[...], wo_ref[...])).astype(BF16)
    upstream = nt(qg_ref[...], wq_ref[...])
    back = norm_back(wide, inv_rms(wide), gain_ref[...], upstream)
    grad_ref[...] = (og_ref[...].astype(F32) + back).astype(BF16)


def pack_body(core_ref, p0, p1, p2, p3, near_ref, far_ref):
    cap = p0.shape[1]
    near = core_ref[0] * 2
    for k, piece in enumerate((p0, p1, p2, p3)):
        near_ref[k * cap : (k + 1) * cap, :] = piece[near]
        far_ref[k * cap : (k + 1) * cap, :] = piece[2 - near]


def mix_body(own, near, m1, m2, m3):
    cap = m1.shape[0] // 2
    for k, mixed in enumerate((m1, m2, m3), 1):
        mixed[0:cap] = own[k * cap : (k + 1) * cap]
        mixed[cap : 2 * cap] = near[k * cap : (k + 1) * cap]


def split_body(block, f1, f2, f3):
    cap = f1.shape[0]
    for k, piece in enumerate((f1, f2, f3), 1):
        piece[...] = block[k * cap : (k + 1) * cap]


def grid_body(turn, sub_ref, core_ref, outer, s0, s1, s2, s3, rows_hbm, gain_hbm, x_hbm, *refs):
    out_hbm, got, done_ref, done_sems, rows_ref, gain_ref, x_ref, sems = refs[-8:]
    half = x_ref.shape[0]
    upper = (1 - core_ref[0]) if turn == 0 else core_ref[0]
    base = pl.multiple_of(upper * half, half)
    tile = 256
    tiles = half // tile
    spans = [pl.ds(t * tile, tile) for t in range(tiles)]
    copies = fetch(
        [rows_hbm, gain_hbm] + [x_hbm.at[pl.ds(base + t * tile, tile)] for t in range(tiles)],
        [rows_ref, gain_ref] + [x_ref.at[span] for span in spans],
        sems,
    )
    cap = rows_ref.shape[3]
    block = 4 * cap
    me = sub_ref[0]
    got[0:block] = outer[...]
    for k, piece in enumerate((s0, s1, s2, s3)):
        got[block + k * cap : block + (k + 1) * cap] = piece[1]
    copies[0].wait()
    copies[1].wait()
    gain = gain_ref[...]
    idx = []
    for o in (2 * upper, 1):
        for k in range(4):
            idx.append(rows_ref[0, o, pl.ds(lax.rem(me + k, 4), 1), :])
    idx = jnp.concatenate(idx, axis=1) - base
    stores = []
    for t in range(tiles):
        part = slice(t * tile, (t + 1) * tile)
        ids = lax.broadcasted_iota(jnp.int32, (tile, 2 * block), 0) + t * tile
        onehot = jnp.where(ids == idx, 1.0, 0.0).astype(BF16)
        upstream = nn(onehot, got[...])
        copies[2 + t].wait()
        wide = x_ref[part, :].astype(F32)
        done_ref[part, :] = norm_back(wide, inv_rms(wide), gain, upstream).astype(BF16)
        stores.append(
            pltpu.make_async_copy(
                done_ref.at[part], out_hbm.at[pl.ds(base + t * tile, tile)], done_sems.at[t]
            )
        )
        stores[-1].start()
    for store in stores:
        store.wait()


def widen_body(turn, core_ref, half_ref, *refs):
    out_hbm, wide, sems = refs[-3:]
    count, width, _ = wide.shape
    half = core_ref[0] ^ turn
    part = width // 4
    copies = []
    for i in range(4 * count):
        m, rows = i // 4, pl.ds((i % 4) * part, part)
        wide[m, rows, :] = half_ref[i * part : (i + 1) * part, :].astype(F32)
        copies.append(
            pltpu.make_async_copy(
                wide.at[m, rows], out_hbm.at[lax.select(half == 0, m, 3 - m), rows], sems.at[i]
            )
        )
        copies[-1].start()
    for copy in copies:
        copy.wait()


def pair_body(keep_ref, other_ref, out_hbm, sums, sems):
    part = sums.shape[0] // 4
    copies = []
    for i in range(4):
        at = slice(i * part, (i + 1) * part)
        sums[at, :] = (keep_ref[at, :].astype(F32) + other_ref[at, :].astype(F32)).astype(BF16)
        copies.append(pltpu.make_async_copy(sums.at[at], out_hbm.at[at], sems.at[i]))
        copies[-1].start()
    for copy in copies:
        copy.wait()


def spread_body(p0, p1, p2, p3, out_hbm, total, sems):
    even = p0[...].astype(F32) + p2[...].astype(F32)
    odd = p1[...].astype(F32) + p3[...].astype(F32)
    total[...] = (even + odd).astype(BF16)
    copies = []
    for i in range(out_hbm.shape[0]):
        copies.append(pltpu.make_async_copy(total, out_hbm.at[i], sems.at[i]))
        copies[-1].start()
    for copy in copies:
        copy.wait()


def shifted(block, axis, k):
    n = lax.axis_size(axis)
    return lax.ppermute(block, axis, [(i, (i + k) % n) for i in range(n)])


def swapped_far(block):
    n = lax.axis_size(SLAB)
    pairs = [(i, i + 1) for i in range(1, n - 1, 2)]
    return lax.ppermute(block, SLAB, pairs + [(j, i) for i, j in pairs])


def sds(shape, dtype=BF16):
    return jax.ShapeDtypeStruct(shape, dtype)


def shards(grid_x, mesh_h, gain_grid, gain_mesh, w_query, w_key, w_value, w_out, edge_bias,
           neighbours, valid, send_rows, out_grad):
    points, width = grid_x.shape
    nodes, fan = neighbours.shape
    cap = send_rows.shape[3]
    block = 4 * cap
    slots = 3 * block
    heads = edge_bias.shape[1] // fan
    sub1 = lax.axis_index("z").astype(jnp.int32).reshape(1)
    core1 = lax.axis_index("gc").astype(jnp.int32).reshape(1)
    gain_g, gain_m = gain_grid.reshape(1, width), gain_mesh.reshape(1, width)
    (grid_x, mesh_h, out_grad, send_rows, w_key, w_value, w_query, w_out, gain_g, gain_m, edge_bias,
     neighbours, valid) = (
        pltpu.with_memory_space_constraint(a, pltpu.HBM)
        for a in (grid_x, mesh_h, out_grad, send_rows, w_key, w_value, w_query, w_out, gain_g, gain_m,
                  edge_bias, neighbours, valid)
    )

    one, two, four = sds((cap, width)), sds((2 * cap, width)), sds((block, width))
    near, far, own = call(
        gather_body, [four] * 3, [SM, SM, HB, HB, HB],
        (sub1, core1, send_rows, gain_g, grid_x), 1 << 30, 4 << 20, "gather_rows",
        held(send_rows, gain_g, grid_x)[:-1] + [pltpu.SemaphoreType.DMA((4,))],
    )

    far = swapped_far(far)
    near = shifted(near, "gc", 1)
    mixed = call(mix_body, [two] * 3, [VM] * 2, (own, near), 0, 1 << 20, "mix")
    mixed = [shifted(m, "z", k) for k, m in enumerate(mixed, 1)]
    mesh_normed, queries, att_grad, og_near = call(
        mesh_in_body, [sds((nodes, width))] * 4, [HB] * 5, (mesh_h, gain_m, w_query, w_out, out_grad),
        1 << 28, 2 << 20, "mesh_in", held(mesh_h, gain_m, w_query, w_out)[:-1] + [pltpu.SemaphoreType.DMA((5,))],
    )
    far, mixed[0], queries = lax.optimization_barrier((far, mixed[0], queries))
    outer = call(split_body, [one] * 3, [VM], (far,), 0, 1 << 19, "split")
    outer = [shifted(f, "z", k) for k, f in enumerate(outer, 1)]
    received = near, far, own, *mixed, *outer
    sub2, far = lax.optimization_barrier((sub1, far))
    (dense,) = call(
        slots_body, [sds((heads, nodes, slots), F32)], [SM] + [HB] * 3,
        (sub2, neighbours, valid, edge_bias), 1 << 30, 8 << 20, "slots",
        [pltpu.VMEM((nodes * 8, 128), F32), pltpu.VMEM((heads, nodes, 128), F32)]
        + held(neighbours, valid, edge_bias),
    )
    send, part_grads, attended, query_grad, weights_near, rows = call(
        middle_body,
        [sds((2 * width, width)), sds((slots, 2 * width))] + [sds((nodes, width))] * 2
        + [sds((width, 2 * width)), sds((slots, width))],
        [SM] + [VM] * 14 + [HB] * 2,
        (core1, *received, queries, att_grad, mesh_normed, og_near, dense, w_key, w_value),
        3 << 30, 8 << 20, "middle",
        [pltpu.VMEM((slots, width), BF16)] * 2 + [pltpu.SemaphoreType.DMA((2,))],
    )

    other = shifted(send, "gc", 1)
    (keep,) = call(
        keep_body, [sds((2 * width, width))], [SM] + [VM] * 6,
        (core1, rows, part_grads, mesh_normed, query_grad, attended, og_near), 1 << 29, 3 << 20, "keep",
    )
    s0, s1, s2, s3 = call(
        back_body, [sds((3, cap, width))] * 4, [VM] * 2, (part_grads, weights_near),
        1 << 30, 3 << 20, "back",
    )
    other, s1, keep = lax.optimization_barrier((other, s1, keep))
    (own,) = call(
        pair_body, [sds((2 * width, width))], [VM] * 2, (keep, other), 1 << 20, 3 << 20, "pair",
        [pltpu.VMEM((2 * width, width), BF16), pltpu.SemaphoreType.DMA((4,))], [HB],
    )
    plane = lax.axis_size(PLANE)
    share = 2 * width // plane
    parts = lax.all_to_all(own.reshape(plane, share, width), PLANE, 0, 0, tiled=True)

    attended, own = lax.optimization_barrier((attended, own))
    mesh_out, mesh_grad = call(
        mesh_body, [sds((nodes, width))] * 2, [VM] * 3 + [HB] * 4,
        (attended, query_grad, og_near, w_out, w_query, mesh_h, gain_m), 1 << 28, 2 << 20, "mesh",
        held(w_out, w_query, mesh_h, gain_m),
    )
    s1, s2, s3 = (shifted(s, "z", -k) for k, s in ((1, s1), (2, s2), (3, s3)))
    s1, s2, s3, parts, mesh_out = lax.optimization_barrier((s1, s2, s3, parts, mesh_out))
    part = jnp.sum(parts.astype(F32), axis=0).astype(BF16)
    part, s0 = lax.optimization_barrier((part, s0))
    near, far = call(
        pack_body, [four] * 2, [SM] + [VM] * 4, (core1, s0, s1, s2, s3), 0, 1 << 20, "pack"
    )
    far = swapped_far(far)
    near = shifted(near, "gc", 1)
    p1, p2, p3 = (shifted(part, "z", k) for k in (1, 2, 3))
    (spread,) = call(
        spread_body, [sds((plane, share, width))], [VM] * 4, (part, p1, p2, p3), 1 << 18, 1 << 20,
        "spread", [pltpu.VMEM((share, width), BF16), pltpu.SemaphoreType.DMA((plane,))], [HB],
    )
    mine = lax.all_to_all(spread, PLANE, 0, 0, tiled=True).reshape(2 * width, width)
    half = points // 2
    grid_scratch = [
        pltpu.VMEM((2 * block, width), BF16), pltpu.VMEM((half, width), BF16),
        pltpu.SemaphoreType.DMA((half // 256,)), pltpu.VMEM(send_rows.shape, send_rows.dtype),
        pltpu.VMEM(gain_g.shape, F32), pltpu.VMEM((half, width), BF16), pltpu.SemaphoreType.DMA((2 + half // 256,)),
    ]
    grid_specs = [SM] * 2 + [VM] * 5 + [HB] * 3
    (grid_grad,) = call(
        functools.partial(grid_body, 0), [sds((points, width))], grid_specs,
        (sub1, core1, near, s0, s1, s2, s3, send_rows, gain_g, grid_x),
        1 << 29, 3 << 20, "grid_near", grid_scratch, [HB],
    )
    mine, far, grid_grad = lax.optimization_barrier((mine, far, grid_grad))
    theirs = shifted(mine, "gc", 1)
    (grid_grad,) = call(
        functools.partial(grid_body, 1), [sds((points, width))], grid_specs + [HB],
        (sub1, core1, far, s0, s1, s2, s3, send_rows, gain_g, grid_x, grid_grad),
        1 << 29, 3 << 20, "grid_far", grid_scratch, [HB], {10: 0},
    )
    whole = sds((4, width, width), F32)
    wide = [pltpu.VMEM((2, width, width), F32), pltpu.SemaphoreType.DMA((8,))]
    (weight_grads,) = call(
        functools.partial(widen_body, 0), [whole], [SM, VM], (core1, mine), 1 << 20, 3 << 20, "widen_own",
        wide, [HB],
    )
    (weight_grads,) = call(
        functools.partial(widen_body, 1), [whole], [SM, VM, HB], (core1, theirs, weight_grads),
        1 << 20, 3 << 20, "widen_other", wide, [HB], {2: 0},
    )
    return mesh_out, mesh_grad, grid_grad, weight_grads


def solution(mesh):
    split = Mesh(mesh.devices.reshape(4, 4, 2, mesh.shape["sub"]), ALL)
    rows = P(ALL, None)
    return jax.shard_map(
        shards,
        mesh=split,
        in_specs=(rows, rows, P(), P(), P(), P(), P(), P(), rows, rows, rows,
                  P(ALL, None, None, None), rows),
        out_specs=(rows, rows, rows, P()),
        check_vma=False,
    )
```

```python
import functools

import jax
import jax.numpy as jnp
from jax import lax
from jax.experimental import pallas as pl
from jax.experimental.pallas import tpu as pltpu
from jax.sharding import Mesh
from jax.sharding import PartitionSpec as P

SLAB = ("gx", "gy", "gc")
PLANE = ("gx", "gy")
ALL = ("gx", "gy", "gc", "z")

EPSILON = 1e-06
ABSENT = -1e30
F32 = jnp.float32
BF16 = jnp.bfloat16

VM = pl.BlockSpec(memory_space=pltpu.VMEM)
SM = pl.BlockSpec(memory_space=pltpu.SMEM)
HB = pl.BlockSpec(memory_space=pltpu.HBM)


def nn(a, b):
    return lax.dot_general(a, b, (((1,), (0,)), ((), ())), preferred_element_type=F32)


def nt(a, b):
    return lax.dot_general(a, b, (((1,), (1,)), ((), ())), preferred_element_type=F32)


def tn(a, b):
    return lax.dot_general(a, b, (((0,), (0,)), ((), ())), preferred_element_type=F32)


def inv_rms(wide):
    return lax.rsqrt(jnp.mean(wide * wide, axis=-1, keepdims=True) + EPSILON)


def norm_back(wide, factor, gain_row, upstream):
    scaled = gain_row * upstream
    inner = jnp.mean(wide * scaled, axis=-1, keepdims=True)
    return factor * scaled - wide * (factor * factor * factor * inner)


def call(body, outs, in_specs, args, flops, nbytes, name, scratch=(), out_specs=None, aliases=None):
    return pl.pallas_call(
        body,
        out_shape=outs,
        in_specs=in_specs,
        out_specs=out_specs or [VM] * len(outs),
        scratch_shapes=list(scratch),
        input_output_aliases=aliases or {},
        compiler_params=pltpu.CompilerParams(vmem_limit_bytes=16 << 20),
        cost_estimate=pl.CostEstimate(flops=flops, bytes_accessed=nbytes, transcendentals=0),
        name=name,
    )(*args)


def fetch(sources, targets, sems):
    copies = []
    for i, (source, target) in enumerate(zip(sources, targets)):
        copies.append(pltpu.make_async_copy(source, target, sems.at[i]))
        copies[-1].start()
    return copies


def held(*args):
    return [pltpu.VMEM(a.shape, a.dtype) for a in args] + [pltpu.SemaphoreType.DMA((len(args),))]


def assemble(rows, near_first, near, far, own, *pieces):
    block = near.shape[0]
    cap = block // 4
    near_at = pl.multiple_of((1 - near_first) * (2 * block), block)
    far_at = pl.multiple_of(near_first * (2 * block), block)
    rows[block : block + cap] = own[0:cap]
    rows[pl.ds(near_at, cap), :] = near[0:cap]
    rows[pl.ds(far_at, cap), :] = far[0:cap]
    for k in range(1, 4):
        mixed, last = pieces[k - 1], pieces[len(pieces) - 4 + k]
        rows[block + k * cap : block + (k + 1) * cap] = mixed[0:cap]
        rows[pl.ds(near_at + k * cap, cap), :] = mixed[cap : 2 * cap]
        rows[pl.ds(far_at + k * cap, cap), :] = last[last.shape[0] - cap :]


def gather_body(sub_ref, core_ref, rows_hbm, gain_hbm, x_hbm, *refs):
    later = (len(refs) - 7) // 2
    later_hbm, refs = refs[:later], refs[later:]
    near_ref, far_ref, own_ref = refs[:3]
    later_refs = refs[3 : 3 + later - 1]
    rows_ref, gain_ref, x_ref, sems, later_sems = refs[-5:]
    half = x_ref.shape[0] // 2
    cap = rows_ref.shape[3]
    core = core_ref[0]
    firsts = [pl.multiple_of((1 - core) * half, half), pl.multiple_of(core * half, half)]
    parts = [pl.ds(first, half) for first in firsts]
    copies = fetch(
        [rows_hbm, gain_hbm] + [x_hbm.at[p] for p in parts],
        [rows_ref, gain_ref] + [x_ref.at[p] for p in parts],
        sems,
    )
    wkv_ref = later_refs[-1]
    width = x_ref.shape[1]
    later_refs = (*later_refs[:-1], wkv_ref.at[:, pl.ds(0, width)], wkv_ref.at[:, pl.ds(width, width)])
    later_copies = fetch(later_hbm, later_refs, later_sems)
    copies[0].wait()
    copies[1].wait()
    me = sub_ref[0]
    eye = lax.broadcasted_iota(jnp.int32, (cap, cap), 0) == lax.broadcasted_iota(
        jnp.int32, (cap, cap), 1
    )
    gain = gain_ref[...]
    steps = (
        (2 - 2 * core, firsts[0], half, near_ref),
        (2 * core, firsts[1], half, far_ref),
        (1, 0, 2 * half, own_ref),
    )
    for step, (o, first, count, out_ref) in enumerate(steps):
        cols = []
        for k in range(4):
            s = lax.rem(me + k, 4)
            row = rows_ref[0, o, pl.ds(s, 1), :].astype(F32)
            cols.append(jnp.sum(jnp.where(eye, row, 0.0), axis=1, keepdims=True))
        col = jnp.concatenate(cols, axis=0).astype(jnp.int32) - first
        lanes = lax.broadcasted_iota(jnp.int32, (4 * cap, count), 1)
        onehot = jnp.where(lanes == col, 1.0, 0.0).astype(BF16)
        if step < 2:
            copies[2 + step].wait()
        wide = nn(onehot, x_ref[pl.ds(first, count), :])
        out_ref[...] = (wide * inv_rms(wide) * gain).astype(BF16)
    for copy in later_copies:
        copy.wait()


def mesh_in_body(mesh_ref, gain_ref, wq_ref, wo_ref, og_ref, normed_ref, q_ref, ag_ref):
    wide = mesh_ref[...].astype(F32)
    normed = (wide * inv_rms(wide) * gain_ref[...]).astype(BF16)
    normed_ref[...] = normed
    q_ref[...] = (nn(normed, wq_ref[...]) * (128 ** -0.5)).astype(BF16)
    ag_ref[...] = nt(og_ref[...], wo_ref[...]).astype(BF16)


def slots_body(sub_ref, nbr_ref, valid_ref, bias_ref, dense_ref, inv_ref, edge_ref):
    heads, nodes, slots = dense_ref.shape
    fan = nbr_ref.shape[1]
    slot = nbr_ref[...]
    slot = (slot & ~192) | (((sub_ref[0] - (slot >> 6)) & 3) << 6)
    high, low = slot >> 7, slot & 127
    blocks = lax.broadcasted_iota(jnp.int32, (8, fan), 0)
    lanes = lax.broadcasted_iota(jnp.int32, (128, fan), 0)
    edge = lax.broadcasted_iota(jnp.int32, (8, fan), 1).astype(F32) + 1.0
    for m in range(nodes):
        named = jnp.where(high[m : m + 1, :] == blocks, edge, 0.0).astype(BF16)
        places = jnp.where(low[m : m + 1, :] == lanes, 1.0, 0.0).astype(BF16)
        inv_ref[m * 8 : (m + 1) * 8, :] = nt(named, places)
    live = valid_ref[...] == 1
    for h in range(heads):
        edge_ref[h, :, 0:fan] = jnp.where(live, bias_ref[:, h * fan : (h + 1) * fan], ABSENT)
    for b in range(slots // 128):
        at = inv_ref[pl.ds(b, nodes, stride=8), :].astype(jnp.int32) - 1
        here = at >= 0
        at = jnp.maximum(at, 0)
        for h in range(heads):
            got = jnp.take_along_axis(edge_ref[h], at, axis=1, mode="promise_in_bounds")
            dense_ref[h, :, b * 128 : (b + 1) * 128] = jnp.where(here, got, ABSENT)


def middle_body(core_ref, near, far, own, m1, m2, m3, f1, f2, f3, q_ref, ag_ref, mn_ref, og_ref,
                bias_ref, wkv_ref, send_ref, part_ref, att_ref, qg_ref, rows, keys, vals):
    width = q_ref.shape[1]
    heads = bias_ref.shape[0]
    core = core_ref[0]
    assemble(rows, 1 - core, near, far, own, m1, m2, m3, f1, f2, f3)
    keys[...] = nn(rows[...], wkv_ref[:, :width]).astype(BF16)
    vals[...] = nn(rows[...], wkv_ref[:, width:]).astype(BF16)
    for h in range(heads):
        at = slice(h * 128, (h + 1) * 128)
        q, ag = q_ref[:, at], ag_ref[:, at]
        kh, vh = keys[:, at], vals[:, at]
        scores = nt(q, kh) + bias_ref[h]
        peak = jnp.max(scores, axis=1, keepdims=True)
        terms = jnp.exp(scores - peak)
        probs = terms / jnp.sum(terms, axis=1, keepdims=True)
        probs_b = probs.astype(BF16)
        att_ref[:, at] = nn(probs_b, vh).astype(BF16)
        pg = nt(ag, vh)
        sg = (probs * (pg - jnp.sum(probs * pg, axis=1, keepdims=True))).astype(BF16)
        qg_ref[:, at] = (nn(sg, kh) * (128 ** -0.5)).astype(BF16)
        part_ref[:, at] = tn(sg, q).astype(BF16)
        part_ref[:, width + h * 128 : width + (h + 1) * 128] = tn(probs_b, ag).astype(BF16)
    half_grads(1 - core, send_ref, rows, part_ref, mn_ref, qg_ref, att_ref, og_ref)


def half_grads(half, out_ref, rows, part_ref, mn_ref, qg_ref, att_ref, og_ref):
    width = mn_ref.shape[1]
    first = half == 0
    left = jnp.where(first, mn_ref[...].astype(F32), att_ref[...].astype(F32)).astype(BF16)
    right = jnp.where(first, qg_ref[...].astype(F32), og_ref[...].astype(F32)).astype(BF16)
    columns = pl.ds(pl.multiple_of(half * width, width), width)
    out_ref[0:width] = tn(left, right).astype(BF16)
    out_ref[width : 2 * width] = tn(rows[...], part_ref[:, columns]).astype(BF16)


def keep_body(core_ref, rows, part_ref, mn_ref, qg_ref, att_ref, og_ref, keep_ref):
    half_grads(core_ref[0], keep_ref, rows, part_ref, mn_ref, qg_ref, att_ref, og_ref)


def back_body(part_ref, wkv_ref, s0, s1, s2, s3):
    cap = s0.shape[1]
    for o in range(3):
        rows = slice(o * 4 * cap, (o + 1) * 4 * cap)
        back = nt(part_ref[rows, :], wkv_ref[...]).astype(BF16)
        for k, piece in enumerate((s0, s1, s2, s3)):
            piece[o] = back[k * cap : (k + 1) * cap]


def mesh_body(att_ref, qg_ref, og_ref, wo_ref, wq_ref, mesh_ref, gain_ref, out_ref, grad_ref):
    wide = mesh_ref[...].astype(F32)
    out_ref[...] = (wide + nn(att_ref[...], wo_ref[...])).astype(BF16)
    upstream = nt(qg_ref[...], wq_ref[...])
    back = norm_back(wide, inv_rms(wide), gain_ref[...], upstream)
    grad_ref[...] = (og_ref[...].astype(F32) + back).astype(BF16)


def pack_body(core_ref, p0, p1, p2, p3, near_ref, far_ref):
    cap = p0.shape[1]
    near = core_ref[0] * 2
    for k, piece in enumerate((p0, p1, p2, p3)):
        near_ref[k * cap : (k + 1) * cap, :] = piece[near]
        far_ref[k * cap : (k + 1) * cap, :] = piece[2 - near]


def mix_body(own, near, m1, m2, m3):
    cap = m1.shape[0] // 2
    for k, mixed in enumerate((m1, m2, m3), 1):
        mixed[0:cap] = own[k * cap : (k + 1) * cap]
        mixed[cap : 2 * cap] = near[k * cap : (k + 1) * cap]


def split_body(block, f1, f2, f3):
    cap = f1.shape[0]
    for k, piece in enumerate((f1, f2, f3), 1):
        piece[...] = block[k * cap : (k + 1) * cap]


def grid_body(turn, sub_ref, core_ref, outer, s0, s1, s2, s3, rows_hbm, gain_hbm, x_hbm, *refs):
    out_hbm, got, done_ref, done_sems, rows_ref, gain_ref, x_ref, sems = refs[-8:]
    half = x_ref.shape[0]
    upper = (1 - core_ref[0]) if turn == 0 else core_ref[0]
    base = pl.multiple_of(upper * half, half)
    tile = 256
    tiles = half // tile
    spans = [pl.ds(t * tile, tile) for t in range(tiles)]
    copies = fetch(
        [rows_hbm, gain_hbm] + [x_hbm.at[pl.ds(base + t * tile, tile)] for t in range(tiles)],
        [rows_ref, gain_ref] + [x_ref.at[span] for span in spans],
        sems,
    )
    cap = rows_ref.shape[3]
    block = 4 * cap
    me = sub_ref[0]
    got[0:block] = outer[...]
    for k, piece in enumerate((s0, s1, s2, s3)):
        got[block + k * cap : block + (k + 1) * cap] = piece[1]
    copies[0].wait()
    copies[1].wait()
    gain = gain_ref[...]
    idx = []
    for o in (2 * upper, 1):
        for k in range(4):
            idx.append(rows_ref[0, o, pl.ds(lax.rem(me + k, 4), 1), :])
    idx = jnp.concatenate(idx, axis=1) - base
    stores = []
    for t in range(tiles):
        part = slice(t * tile, (t + 1) * tile)
        ids = lax.broadcasted_iota(jnp.int32, (tile, 2 * block), 0) + t * tile
        onehot = jnp.where(ids == idx, 1.0, 0.0).astype(BF16)
        upstream = nn(onehot, got[...])
        copies[2 + t].wait()
        wide = x_ref[part, :].astype(F32)
        done_ref[part, :] = norm_back(wide, inv_rms(wide), gain, upstream).astype(BF16)
        stores.append(
            pltpu.make_async_copy(
                done_ref.at[part], out_hbm.at[pl.ds(base + t * tile, tile)], done_sems.at[t]
            )
        )
        stores[-1].start()
    for store in stores:
        store.wait()


def widen_body(turn, core_ref, half_ref, *refs):
    out_hbm, wide, sems = refs[-3:]
    count, width, _ = wide.shape
    half = core_ref[0] ^ turn
    part = width // 4
    copies = []
    for i in range(4 * count):
        m, rows = i // 4, pl.ds((i % 4) * part, part)
        wide[m, rows, :] = half_ref[i * part : (i + 1) * part, :].astype(F32)
        copies.append(
            pltpu.make_async_copy(
                wide.at[m, rows], out_hbm.at[lax.select(half == 0, m, 3 - m), rows], sems.at[i]
            )
        )
        copies[-1].start()
    for copy in copies:
        copy.wait()


def pair_body(keep_ref, other_ref, out_hbm, sums, sems):
    part = sums.shape[0] // 4
    copies = []
    for i in range(4):
        at = slice(i * part, (i + 1) * part)
        sums[at, :] = (keep_ref[at, :].astype(F32) + other_ref[at, :].astype(F32)).astype(BF16)
        copies.append(pltpu.make_async_copy(sums.at[at], out_hbm.at[at], sems.at[i]))
        copies[-1].start()
    for copy in copies:
        copy.wait()


def spread_body(p0, p1, p2, p3, out_hbm, total, sems):
    even = p0[...].astype(F32) + p2[...].astype(F32)
    odd = p1[...].astype(F32) + p3[...].astype(F32)
    total[...] = (even + odd).astype(BF16)
    copies = []
    for i in range(out_hbm.shape[0]):
        copies.append(pltpu.make_async_copy(total, out_hbm.at[i], sems.at[i]))
        copies[-1].start()
    for copy in copies:
        copy.wait()


def shifted(block, axis, k):
    n = lax.axis_size(axis)
    return lax.ppermute(block, axis, [(i, (i + k) % n) for i in range(n)])


def swapped_far(block):
    n = lax.axis_size(SLAB)
    pairs = [(i, i + 1) for i in range(1, n - 1, 2)]
    return lax.ppermute(block, SLAB, pairs + [(j, i) for i, j in pairs])


def sds(shape, dtype=BF16):
    return jax.ShapeDtypeStruct(shape, dtype)


def shards(grid_x, mesh_h, gain_grid, gain_mesh, w_query, w_key, w_value, w_out, edge_bias,
           neighbours, valid, send_rows, out_grad):
    points, width = grid_x.shape
    nodes, fan = neighbours.shape
    cap = send_rows.shape[3]
    block = 4 * cap
    slots = 3 * block
    heads = edge_bias.shape[1] // fan
    sub1 = lax.axis_index("z").astype(jnp.int32).reshape(1)
    core1 = lax.axis_index("gc").astype(jnp.int32).reshape(1)
    gain_g, gain_m = gain_grid.reshape(1, width), gain_mesh.reshape(1, width)
    (grid_x, mesh_h, out_grad, send_rows, w_key, w_value, w_query, w_out, gain_g, gain_m, edge_bias,
     neighbours, valid) = (
        pltpu.with_memory_space_constraint(a, pltpu.HBM)
        for a in (grid_x, mesh_h, out_grad, send_rows, w_key, w_value, w_query, w_out, gain_g, gain_m,
                  edge_bias, neighbours, valid)
    )

    one, two, four = sds((cap, width)), sds((2 * cap, width)), sds((block, width))
    later = (mesh_h, gain_m, w_query, w_out, out_grad, neighbours, valid, edge_bias)
    weights = sds((width, 2 * width))
    near, far, own, *later, weights_near = call(
        gather_body, [four] * 3 + [sds(a.shape, a.dtype) for a in later] + [weights],
        [SM, SM] + [HB] * (5 + len(later)),
        (sub1, core1, send_rows, gain_g, grid_x, *later, w_key, w_value), 1 << 30, 6 << 20, "gather_rows",
        held(send_rows, gain_g, grid_x)[:-1]
        + [pltpu.SemaphoreType.DMA((4,)), pltpu.SemaphoreType.DMA((len(later) + 2,))],
    )
    mesh_near, gain_near, wq_near, wo_near, og_near, nbr_near, valid_near, bias_near = later
    far = swapped_far(far)
    near = shifted(near, "gc", 1)
    mixed = call(mix_body, [two] * 3, [VM] * 2, (own, near), 0, 1 << 20, "mix")
    mixed = [shifted(m, "z", k) for k, m in enumerate(mixed, 1)]
    mesh_normed, queries, att_grad = call(
        mesh_in_body, [sds((nodes, width))] * 3, [VM] * 5,
        (mesh_near, gain_near, wq_near, wo_near, og_near), 1 << 28, 2 << 20, "mesh_in",
    )
    far, mixed[0], queries = lax.optimization_barrier((far, mixed[0], queries))
    outer = call(split_body, [one] * 3, [VM], (far,), 0, 1 << 19, "split")
    outer = [shifted(f, "z", k) for k, f in enumerate(outer, 1)]
    received = near, far, own, *mixed, *outer
    sub2, far = lax.optimization_barrier((sub1, far))
    (dense,) = call(
        slots_body, [sds((heads, nodes, slots), F32)], [SM] + [VM] * 3,
        (sub2, nbr_near, valid_near, bias_near), 1 << 30, 8 << 20, "slots",
        [pltpu.VMEM((nodes * 8, 128), F32), pltpu.VMEM((heads, nodes, 128), F32)],
    )
    send, part_grads, attended, query_grad, rows = call(
        middle_body,
        [sds((2 * width, width)), sds((slots, 2 * width))] + [sds((nodes, width))] * 2
        + [sds((slots, width))],
        [SM] + [VM] * 15,
        (core1, *received, queries, att_grad, mesh_normed, og_near, dense, weights_near),
        3 << 30, 8 << 20, "middle", [pltpu.VMEM((slots, width), BF16)] * 2,
    )

    other = shifted(send, "gc", 1)
    (keep,) = call(
        keep_body, [sds((2 * width, width))], [SM] + [VM] * 6,
        (core1, rows, part_grads, mesh_normed, query_grad, attended, og_near), 1 << 29, 3 << 20, "keep",
    )
    s0, s1, s2, s3 = call(
        back_body, [sds((3, cap, width))] * 4, [VM] * 2, (part_grads, weights_near),
        1 << 30, 3 << 20, "back",
    )
    other, s1, keep = lax.optimization_barrier((other, s1, keep))
    (own,) = call(
        pair_body, [sds((2 * width, width))], [VM] * 2, (keep, other), 1 << 20, 3 << 20, "pair",
        [pltpu.VMEM((2 * width, width), BF16), pltpu.SemaphoreType.DMA((4,))], [HB],
    )
    plane = lax.axis_size(PLANE)
    share = 2 * width // plane
    parts = lax.all_to_all(own.reshape(plane, share, width), PLANE, 0, 0, tiled=True)

    attended, own = lax.optimization_barrier((attended, own))
    mesh_out, mesh_grad = call(
        mesh_body, [sds((nodes, width))] * 2, [VM] * 7,
        (attended, query_grad, og_near, wo_near, wq_near, mesh_near, gain_near), 1 << 28, 2 << 20, "mesh",
    )
    s1, s2, s3 = (shifted(s, "z", -k) for k, s in ((1, s1), (2, s2), (3, s3)))
    s1, s2, s3, parts, mesh_out = lax.optimization_barrier((s1, s2, s3, parts, mesh_out))
    part = jnp.sum(parts.astype(F32), axis=0).astype(BF16)
    part, s0 = lax.optimization_barrier((part, s0))
    near, far = call(
        pack_body, [four] * 2, [SM] + [VM] * 4, (core1, s0, s1, s2, s3), 0, 1 << 20, "pack"
    )
    far = swapped_far(far)
    near = shifted(near, "gc", 1)
    p1, p2, p3 = (shifted(part, "z", k) for k in (1, 2, 3))
    (spread,) = call(
        spread_body, [sds((plane, share, width))], [VM] * 4, (part, p1, p2, p3), 1 << 18, 1 << 20,
        "spread", [pltpu.VMEM((share, width), BF16), pltpu.SemaphoreType.DMA((plane,))], [HB],
    )
    mine = lax.all_to_all(spread, PLANE, 0, 0, tiled=True).reshape(2 * width, width)
    half = points // 2
    grid_scratch = [
        pltpu.VMEM((2 * block, width), BF16), pltpu.VMEM((half, width), BF16),
        pltpu.SemaphoreType.DMA((half // 256,)), pltpu.VMEM(send_rows.shape, send_rows.dtype),
        pltpu.VMEM(gain_g.shape, F32), pltpu.VMEM((half, width), BF16), pltpu.SemaphoreType.DMA((2 + half // 256,)),
    ]
    grid_specs = [SM] * 2 + [VM] * 5 + [HB] * 3
    (grid_grad,) = call(
        functools.partial(grid_body, 0), [sds((points, width))], grid_specs,
        (sub1, core1, near, s0, s1, s2, s3, send_rows, gain_g, grid_x),
        1 << 29, 3 << 20, "grid_near", grid_scratch, [HB],
    )
    mine, far, grid_grad = lax.optimization_barrier((mine, far, grid_grad))
    theirs = shifted(mine, "gc", 1)
    (grid_grad,) = call(
        functools.partial(grid_body, 1), [sds((points, width))], grid_specs + [HB],
        (sub1, core1, far, s0, s1, s2, s3, send_rows, gain_g, grid_x, grid_grad),
        1 << 29, 3 << 20, "grid_far", grid_scratch, [HB], {10: 0},
    )
    whole = sds((4, width, width), F32)
    wide = [pltpu.VMEM((2, width, width), F32), pltpu.SemaphoreType.DMA((8,))]
    (weight_grads,) = call(
        functools.partial(widen_body, 0), [whole], [SM, VM], (core1, mine), 1 << 20, 3 << 20, "widen_own",
        wide, [HB],
    )
    (weight_grads,) = call(
        functools.partial(widen_body, 1), [whole], [SM, VM, HB], (core1, theirs, weight_grads),
        1 << 20, 3 << 20, "widen_other", wide, [HB], {2: 0},
    )
    return mesh_out, mesh_grad, grid_grad, weight_grads


def solution(mesh):
    split = Mesh(mesh.devices.reshape(4, 4, 2, mesh.shape["sub"]), ALL)
    rows = P(ALL, None)
    return jax.shard_map(
        shards,
        mesh=split,
        in_specs=(rows, rows, P(), P(), P(), P(), P(), P(), rows, rows, rows,
                  P(ALL, None, None, None), rows),
        out_specs=(rows, rows, rows, P()),
        check_vma=False,
    )
```

```python
import functools

import jax
import jax.numpy as jnp
from jax import lax
from jax.experimental import pallas as pl
from jax.experimental.pallas import tpu as pltpu
from jax.sharding import Mesh
from jax.sharding import PartitionSpec as P

SLAB = ("gx", "gy", "gc")
PLANE = ("gx", "gy")
ALL = ("gx", "gy", "gc", "z")

EPSILON = 1e-06
ABSENT = -1e30
F32 = jnp.float32
BF16 = jnp.bfloat16

VM = pl.BlockSpec(memory_space=pltpu.VMEM)
SM = pl.BlockSpec(memory_space=pltpu.SMEM)
HB = pl.BlockSpec(memory_space=pltpu.HBM)


def nn(a, b):
    return lax.dot_general(a, b, (((1,), (0,)), ((), ())), preferred_element_type=F32)


def nt(a, b):
    return lax.dot_general(a, b, (((1,), (1,)), ((), ())), preferred_element_type=F32)


def tn(a, b):
    return lax.dot_general(a, b, (((0,), (0,)), ((), ())), preferred_element_type=F32)


def inv_rms(wide):
    return lax.rsqrt(jnp.mean(wide * wide, axis=-1, keepdims=True) + EPSILON)


def norm_back(wide, factor, gain_row, upstream):
    scaled = gain_row * upstream
    inner = jnp.mean(wide * scaled, axis=-1, keepdims=True)
    return factor * scaled - wide * (factor * factor * factor * inner)


def call(body, outs, in_specs, args, flops, nbytes, name, scratch=(), out_specs=None, aliases=None):
    return pl.pallas_call(
        body,
        out_shape=outs,
        in_specs=in_specs,
        out_specs=out_specs or [VM] * len(outs),
        scratch_shapes=list(scratch),
        input_output_aliases=aliases or {},
        compiler_params=pltpu.CompilerParams(vmem_limit_bytes=16 << 20),
        cost_estimate=pl.CostEstimate(flops=flops, bytes_accessed=nbytes, transcendentals=0),
        name=name,
    )(*args)


def fetch(sources, targets, sems):
    copies = []
    for i, (source, target) in enumerate(zip(sources, targets)):
        copies.append(pltpu.make_async_copy(source, target, sems.at[i]))
        copies[-1].start()
    return copies


def held(*args):
    return [pltpu.VMEM(a.shape, a.dtype) for a in args] + [pltpu.SemaphoreType.DMA((len(args),))]


def assemble(rows, near_first, near, far, own, *pieces):
    block = near.shape[0]
    cap = block // 4
    near_at = pl.multiple_of((1 - near_first) * (2 * block), block)
    far_at = pl.multiple_of(near_first * (2 * block), block)
    rows[block : block + cap] = own[0:cap]
    rows[pl.ds(near_at, cap), :] = near[0:cap]
    rows[pl.ds(far_at, cap), :] = far[0:cap]
    for k in range(1, 4):
        mixed, last = pieces[k - 1], pieces[len(pieces) - 4 + k]
        rows[block + k * cap : block + (k + 1) * cap] = mixed[0:cap]
        rows[pl.ds(near_at + k * cap, cap), :] = mixed[cap : 2 * cap]
        rows[pl.ds(far_at + k * cap, cap), :] = last[last.shape[0] - cap :]


def gather_body(sub_ref, core_ref, rows_hbm, gain_hbm, x_hbm, *refs):
    later = (len(refs) - 8) // 2
    later_hbm, refs = refs[:later], refs[later:]
    near_ref, far_ref, own_ref, rows_ref, gain_ref = refs[:5]
    later_refs = refs[5 : 5 + later]
    x_ref, sems, later_sems = refs[-3:]
    half = x_ref.shape[0] // 2
    cap = rows_ref.shape[3]
    core = core_ref[0]
    firsts = [pl.multiple_of((1 - core) * half, half), pl.multiple_of(core * half, half)]
    parts = [pl.ds(first, half) for first in firsts]
    copies = fetch(
        [rows_hbm, gain_hbm] + [x_hbm.at[p] for p in parts],
        [rows_ref, gain_ref] + [x_ref.at[p] for p in parts],
        sems,
    )
    later_copies = fetch(later_hbm, later_refs, later_sems)
    copies[0].wait()
    copies[1].wait()
    me = sub_ref[0]
    eye = lax.broadcasted_iota(jnp.int32, (cap, cap), 0) == lax.broadcasted_iota(
        jnp.int32, (cap, cap), 1
    )
    gain = gain_ref[...]
    steps = (
        (2 - 2 * core, firsts[0], half, near_ref),
        (2 * core, firsts[1], half, far_ref),
        (1, 0, 2 * half, own_ref),
    )
    for step, (o, first, count, out_ref) in enumerate(steps):
        cols = []
        for k in range(4):
            s = lax.rem(me + k, 4)
            row = rows_ref[0, o, pl.ds(s, 1), :].astype(F32)
            cols.append(jnp.sum(jnp.where(eye, row, 0.0), axis=1, keepdims=True))
        col = jnp.concatenate(cols, axis=0).astype(jnp.int32) - first
        lanes = lax.broadcasted_iota(jnp.int32, (4 * cap, count), 1)
        onehot = jnp.where(lanes == col, 1.0, 0.0).astype(BF16)
        if step < 2:
            copies[2 + step].wait()
        wide = nn(onehot, x_ref[pl.ds(first, count), :])
        out_ref[...] = (wide * inv_rms(wide) * gain).astype(BF16)
    for copy in later_copies:
        copy.wait()


def mesh_in_body(mesh_ref, gain_ref, wq_ref, wo_ref, og_ref, normed_ref, q_ref, ag_ref):
    wide = mesh_ref[...].astype(F32)
    normed = (wide * inv_rms(wide) * gain_ref[...]).astype(BF16)
    normed_ref[...] = normed
    q_ref[...] = (nn(normed, wq_ref[...]) * (128 ** -0.5)).astype(BF16)
    ag_ref[...] = nt(og_ref[...], wo_ref[...]).astype(BF16)


def slots_body(sub_ref, nbr_ref, valid_ref, bias_ref, wk_hbm, wv_hbm, dense_ref, wkv_ref,
               inv_ref, edge_ref, sems):
    width = wk_hbm.shape[0]
    copies = fetch(
        (wk_hbm, wv_hbm), (wkv_ref.at[:, pl.ds(0, width)], wkv_ref.at[:, pl.ds(width, width)]), sems
    )
    heads, nodes, slots = dense_ref.shape
    fan = nbr_ref.shape[1]
    slot = nbr_ref[...]
    slot = (slot & ~192) | (((sub_ref[0] - (slot >> 6)) & 3) << 6)
    high, low = slot >> 7, slot & 127
    blocks = lax.broadcasted_iota(jnp.int32, (8, fan), 0)
    lanes = lax.broadcasted_iota(jnp.int32, (128, fan), 0)
    edge = lax.broadcasted_iota(jnp.int32, (8, fan), 1).astype(F32) + 1.0
    for m in range(nodes):
        named = jnp.where(high[m : m + 1, :] == blocks, edge, 0.0).astype(BF16)
        places = jnp.where(low[m : m + 1, :] == lanes, 1.0, 0.0).astype(BF16)
        inv_ref[m * 8 : (m + 1) * 8, :] = nt(named, places)
    live = valid_ref[...] == 1
    for h in range(heads):
        edge_ref[h, :, 0:fan] = jnp.where(live, bias_ref[:, h * fan : (h + 1) * fan], ABSENT)
    for b in range(slots // 128):
        at = inv_ref[pl.ds(b, nodes, stride=8), :].astype(jnp.int32) - 1
        here = at >= 0
        at = jnp.maximum(at, 0)
        for h in range(heads):
            got = jnp.take_along_axis(edge_ref[h], at, axis=1, mode="promise_in_bounds")
            dense_ref[h, :, b * 128 : (b + 1) * 128] = jnp.where(here, got, ABSENT)
    for copy in copies:
        copy.wait()


def middle_body(core_ref, near, far, own, m1, m2, m3, f1, f2, f3, q_ref, ag_ref, mn_ref, og_ref,
                bias_ref, wkv_ref, send_ref, part_ref, att_ref, qg_ref, rows, keys, vals):
    width = q_ref.shape[1]
    heads = bias_ref.shape[0]
    core = core_ref[0]
    assemble(rows, 1 - core, near, far, own, m1, m2, m3, f1, f2, f3)
    keys[...] = nn(rows[...], wkv_ref[:, :width]).astype(BF16)
    vals[...] = nn(rows[...], wkv_ref[:, width:]).astype(BF16)
    for h in range(heads):
        at = slice(h * 128, (h + 1) * 128)
        q, ag = q_ref[:, at], ag_ref[:, at]
        kh, vh = keys[:, at], vals[:, at]
        scores = nt(q, kh) + bias_ref[h]
        peak = jnp.max(scores, axis=1, keepdims=True)
        terms = jnp.exp(scores - peak)
        probs = terms / jnp.sum(terms, axis=1, keepdims=True)
        probs_b = probs.astype(BF16)
        att_ref[:, at] = nn(probs_b, vh).astype(BF16)
        pg = nt(ag, vh)
        sg = (probs * (pg - jnp.sum(probs * pg, axis=1, keepdims=True))).astype(BF16)
        qg_ref[:, at] = (nn(sg, kh) * (128 ** -0.5)).astype(BF16)
        part_ref[:, at] = tn(sg, q).astype(BF16)
        part_ref[:, width + h * 128 : width + (h + 1) * 128] = tn(probs_b, ag).astype(BF16)
    half_grads(1 - core, send_ref, rows, part_ref, mn_ref, qg_ref, att_ref, og_ref)


def half_grads(half, out_ref, rows, part_ref, mn_ref, qg_ref, att_ref, og_ref):
    width = mn_ref.shape[1]
    first = half == 0
    left = jnp.where(first, mn_ref[...].astype(F32), att_ref[...].astype(F32)).astype(BF16)
    right = jnp.where(first, qg_ref[...].astype(F32), og_ref[...].astype(F32)).astype(BF16)
    columns = pl.ds(pl.multiple_of(half * width, width), width)
    out_ref[0:width] = tn(left, right).astype(BF16)
    out_ref[width : 2 * width] = tn(rows[...], part_ref[:, columns]).astype(BF16)


def keep_body(core_ref, rows, part_ref, mn_ref, qg_ref, att_ref, og_ref, keep_ref):
    half_grads(core_ref[0], keep_ref, rows, part_ref, mn_ref, qg_ref, att_ref, og_ref)


def back_body(part_ref, wkv_ref, s0, s1, s2, s3):
    cap = s0.shape[1]
    for o in range(3):
        rows = slice(o * 4 * cap, (o + 1) * 4 * cap)
        back = nt(part_ref[rows, :], wkv_ref[...]).astype(BF16)
        for k, piece in enumerate((s0, s1, s2, s3)):
            piece[o] = back[k * cap : (k + 1) * cap]


def mesh_body(att_ref, qg_ref, og_ref, wo_ref, wq_ref, mesh_ref, gain_ref, out_ref, grad_ref):
    wide = mesh_ref[...].astype(F32)
    out_ref[...] = (wide + nn(att_ref[...], wo_ref[...])).astype(BF16)
    upstream = nt(qg_ref[...], wq_ref[...])
    back = norm_back(wide, inv_rms(wide), gain_ref[...], upstream)
    grad_ref[...] = (og_ref[...].astype(F32) + back).astype(BF16)


def pack_body(core_ref, p0, p1, p2, p3, near_ref, far_ref):
    cap = p0.shape[1]
    near = core_ref[0] * 2
    for k, piece in enumerate((p0, p1, p2, p3)):
        near_ref[k * cap : (k + 1) * cap, :] = piece[near]
        far_ref[k * cap : (k + 1) * cap, :] = piece[2 - near]


def mix_body(own, near, m1, m2, m3):
    cap = m1.shape[0] // 2
    for k, mixed in enumerate((m1, m2, m3), 1):
        mixed[0:cap] = own[k * cap : (k + 1) * cap]
        mixed[cap : 2 * cap] = near[k * cap : (k + 1) * cap]


def split_body(block, f1, f2, f3):
    cap = f1.shape[0]
    for k, piece in enumerate((f1, f2, f3), 1):
        piece[...] = block[k * cap : (k + 1) * cap]


def grid_half(upper, sub_ref, outer, s0, s1, s2, s3, rows_ref, gain_ref, x_ref, out_hbm, got, done_ref,
              sems, ready):
    half = x_ref.shape[0]
    base = pl.multiple_of(upper * half, half)
    cap = rows_ref.shape[3]
    block = 4 * cap
    me = sub_ref[0]
    got[0:block] = outer[...]
    for k, piece in enumerate((s0, s1, s2, s3)):
        got[block + k * cap : block + (k + 1) * cap] = piece[1]
    gain = gain_ref[...]
    idx = []
    for o in (2 * upper, 1):
        for k in range(4):
            idx.append(rows_ref[0, o, pl.ds(lax.rem(me + k, 4), 1), :])
    idx = jnp.concatenate(idx, axis=1) - base
    tile = 256
    stores = []
    for t in range(half // tile):
        part = slice(t * tile, (t + 1) * tile)
        ids = lax.broadcasted_iota(jnp.int32, (tile, 2 * block), 0) + t * tile
        onehot = jnp.where(ids == idx, 1.0, 0.0).astype(BF16)
        upstream = nn(onehot, got[...])
        if t == 0:
            ready()
        wide = x_ref[part, :].astype(F32)
        done_ref[part, :] = norm_back(wide, inv_rms(wide), gain, upstream).astype(BF16)
        stores.append(
            pltpu.make_async_copy(
                done_ref.at[part], out_hbm.at[pl.ds(base + t * tile, tile)], sems.at[t]
            )
        )
        stores[-1].start()
    for store in stores:
        store.wait()


def grid_near_body(sub_ref, core_ref, near, s0, s1, s2, s3, rows_ref, gain_ref, x_hbm,
                   out_hbm, far_x_ref, got, done_ref, done_sems, x_ref, sems):
    half = x_ref.shape[0]
    upper = 1 - core_ref[0]
    copies = fetch(
        [x_hbm.at[pl.ds(pl.multiple_of(u * half, half), half)] for u in (upper, core_ref[0])],
        [x_ref, far_x_ref],
        sems,
    )
    grid_half(upper, sub_ref, near, s0, s1, s2, s3, rows_ref, gain_ref, x_ref, out_hbm, got, done_ref,
              done_sems, copies[0].wait)
    copies[1].wait()


def grid_far_body(sub_ref, core_ref, far, s0, s1, s2, s3, rows_ref, gain_ref, x_ref, prior_hbm,
                  out_hbm, got, done_ref, done_sems):
    grid_half(core_ref[0], sub_ref, far, s0, s1, s2, s3, rows_ref, gain_ref, x_ref, out_hbm, got,
              done_ref, done_sems, lambda: None)


def widen_body(turn, core_ref, half_ref, *refs):
    out_hbm, wide, sems = refs[-3:]
    count, width, _ = wide.shape
    half = core_ref[0] ^ turn
    part = width // 4
    copies = []
    for i in range(4 * count):
        m, rows = i // 4, pl.ds((i % 4) * part, part)
        wide[m, rows, :] = half_ref[i * part : (i + 1) * part, :].astype(F32)
        copies.append(
            pltpu.make_async_copy(
                wide.at[m, rows], out_hbm.at[lax.select(half == 0, m, 3 - m), rows], sems.at[i]
            )
        )
        copies[-1].start()
    for copy in copies:
        copy.wait()


def pair_body(keep_ref, other_ref, out_hbm, sums, sems):
    part = sums.shape[0] // 4
    copies = []
    for i in range(4):
        at = slice(i * part, (i + 1) * part)
        sums[at, :] = (keep_ref[at, :].astype(F32) + other_ref[at, :].astype(F32)).astype(BF16)
        copies.append(pltpu.make_async_copy(sums.at[at], out_hbm.at[at], sems.at[i]))
        copies[-1].start()
    for copy in copies:
        copy.wait()


def plane_body(parts_ref, out_ref):
    total = parts_ref[0].astype(F32)
    for i in range(1, parts_ref.shape[0]):
        total = total + parts_ref[i].astype(F32)
    out_ref[...] = total.astype(BF16)


def spread_body(p0, p1, p2, p3, out_hbm, total, sems):
    even = p0[...].astype(F32) + p2[...].astype(F32)
    odd = p1[...].astype(F32) + p3[...].astype(F32)
    total[...] = (even + odd).astype(BF16)
    copies = []
    for i in range(out_hbm.shape[0]):
        copies.append(pltpu.make_async_copy(total, out_hbm.at[i], sems.at[i]))
        copies[-1].start()
    for copy in copies:
        copy.wait()


def shifted(block, axis, k):
    n = lax.axis_size(axis)
    return lax.ppermute(block, axis, [(i, (i + k) % n) for i in range(n)])


def swapped_far(block):
    n = lax.axis_size(SLAB)
    pairs = [(i, i + 1) for i in range(1, n - 1, 2)]
    return lax.ppermute(block, SLAB, pairs + [(j, i) for i, j in pairs])


def sds(shape, dtype=BF16):
    return jax.ShapeDtypeStruct(shape, dtype)


def shards(grid_x, mesh_h, gain_grid, gain_mesh, w_query, w_key, w_value, w_out, edge_bias,
           neighbours, valid, send_rows, out_grad):
    points, width = grid_x.shape
    nodes, fan = neighbours.shape
    cap = send_rows.shape[3]
    block = 4 * cap
    slots = 3 * block
    heads = edge_bias.shape[1] // fan
    sub1 = lax.axis_index("z").astype(jnp.int32).reshape(1)
    core1 = lax.axis_index("gc").astype(jnp.int32).reshape(1)
    gain_g, gain_m = gain_grid.reshape(1, width), gain_mesh.reshape(1, width)
    (grid_x, mesh_h, out_grad, send_rows, w_key, w_value, w_query, w_out, gain_g, gain_m, edge_bias,
     neighbours, valid) = (
        pltpu.with_memory_space_constraint(a, pltpu.HBM)
        for a in (grid_x, mesh_h, out_grad, send_rows, w_key, w_value, w_query, w_out, gain_g, gain_m,
                  edge_bias, neighbours, valid)
    )

    one, two, four = sds((cap, width)), sds((2 * cap, width)), sds((block, width))
    later = (mesh_h, gain_m, w_query, w_out, out_grad, neighbours, valid, edge_bias)
    near, far, own, rows_near, gain_g_near, *later = call(
        gather_body,
        [four] * 3 + [sds(a.shape, a.dtype) for a in (send_rows, gain_g, *later)],
        [SM, SM] + [HB] * (3 + len(later)),
        (sub1, core1, send_rows, gain_g, grid_x, *later), 1 << 30, 5 << 20, "gather_rows",
        [pltpu.VMEM((points, width), BF16), pltpu.SemaphoreType.DMA((4,)),
         pltpu.SemaphoreType.DMA((len(later),))],
    )
    mesh_near, gain_near, wq_near, wo_near, og_near, nbr_near, valid_near, bias_near = later
    far = swapped_far(far)
    near = shifted(near, "gc", 1)
    mixed = call(mix_body, [two] * 3, [VM] * 2, (own, near), 0, 1 << 20, "mix")
    mixed = [shifted(m, "z", k) for k, m in enumerate(mixed, 1)]
    mesh_normed, queries, att_grad = call(
        mesh_in_body, [sds((nodes, width))] * 3, [VM] * 5,
        (mesh_near, gain_near, wq_near, wo_near, og_near), 1 << 28, 2 << 20, "mesh_in",
    )
    far, mixed[0], queries = lax.optimization_barrier((far, mixed[0], queries))
    outer = call(split_body, [one] * 3, [VM], (far,), 0, 1 << 19, "split")
    outer = [shifted(f, "z", k) for k, f in enumerate(outer, 1)]
    received = near, far, own, *mixed, *outer
    sub2, far = lax.optimization_barrier((sub1, far))
    dense, weights_near = call(
        slots_body, [sds((heads, nodes, slots), F32), sds((width, 2 * width))],
        [SM] + [VM] * 3 + [HB] * 2,
        (sub2, nbr_near, valid_near, bias_near, w_key, w_value), 1 << 30, 8 << 20, "slots",
        [pltpu.VMEM((nodes * 8, 128), F32), pltpu.VMEM((heads, nodes, 128), F32),
         pltpu.SemaphoreType.DMA((2,))],
    )
    send, part_grads, attended, query_grad, rows = call(
        middle_body,
        [sds((2 * width, width)), sds((slots, 2 * width))] + [sds((nodes, width))] * 2
        + [sds((slots, width))],
        [SM] + [VM] * 15,
        (core1, *received, queries, att_grad, mesh_normed, og_near, dense, weights_near),
        3 << 30, 8 << 20, "middle", [pltpu.VMEM((slots, width), BF16)] * 2,
    )

    other = shifted(send, "gc", 1)
    (keep,) = call(
        keep_body, [sds((2 * width, width))], [SM] + [VM] * 6,
        (core1, rows, part_grads, mesh_normed, query_grad, attended, og_near), 1 << 29, 3 << 20, "keep",
    )
    s0, s1, s2, s3 = call(
        back_body, [sds((3, cap, width))] * 4, [VM] * 2, (part_grads, weights_near),
        1 << 30, 3 << 20, "back",
    )
    other, s1, keep = lax.optimization_barrier((other, s1, keep))
    (own,) = call(
        pair_body, [sds((2 * width, width))], [VM] * 2, (keep, other), 1 << 20, 3 << 20, "pair",
        [pltpu.VMEM((2 * width, width), BF16), pltpu.SemaphoreType.DMA((4,))], [HB],
    )
    plane = lax.axis_size(PLANE)
    share = 2 * width // plane
    parts = lax.all_to_all(own.reshape(plane, share, width), PLANE, 0, 0, tiled=True)

    attended, own = lax.optimization_barrier((attended, own))
    mesh_out, mesh_grad = call(
        mesh_body, [sds((nodes, width))] * 2, [VM] * 7,
        (attended, query_grad, og_near, wo_near, wq_near, mesh_near, gain_near), 1 << 28, 2 << 20, "mesh",
    )
    s1, s2, s3 = (shifted(s, "z", -k) for k, s in ((1, s1), (2, s2), (3, s3)))
    s1, s2, s3, parts, mesh_out = lax.optimization_barrier((s1, s2, s3, parts, mesh_out))
    (part,) = call(plane_body, [sds((share, width))], [VM], (parts,), 1 << 20, 1 << 20, "plane")
    part, s0 = lax.optimization_barrier((part, s0))
    near, far = call(
        pack_body, [four] * 2, [SM] + [VM] * 4, (core1, s0, s1, s2, s3), 0, 1 << 20, "pack"
    )
    far = swapped_far(far)
    near = shifted(near, "gc", 1)
    p1, p2, p3 = (shifted(part, "z", k) for k in (1, 2, 3))
    (spread,) = call(
        spread_body, [sds((plane, share, width))], [VM] * 4, (part, p1, p2, p3), 1 << 18, 1 << 20,
        "spread", [pltpu.VMEM((share, width), BF16), pltpu.SemaphoreType.DMA((plane,))], [HB],
    )
    mine = lax.all_to_all(spread, PLANE, 0, 0, tiled=True).reshape(2 * width, width)
    half = points // 2
    grid_scratch = [
        pltpu.VMEM((2 * block, width), BF16), pltpu.VMEM((half, width), BF16),
        pltpu.SemaphoreType.DMA((half // 256,)),
    ]
    grid_grad, far_x = call(
        grid_near_body, [sds((points, width)), sds((half, width))], [SM] * 2 + [VM] * 7 + [HB],
        (sub1, core1, near, s0, s1, s2, s3, rows_near, gain_g_near, grid_x),
        1 << 29, 3 << 20, "grid_near",
        grid_scratch + [pltpu.VMEM((half, width), BF16), pltpu.SemaphoreType.DMA((2,))], [HB, VM],
    )
    mine, far, grid_grad = lax.optimization_barrier((mine, far, grid_grad))
    theirs = shifted(mine, "gc", 1)
    (grid_grad,) = call(
        grid_far_body, [sds((points, width))], [SM] * 2 + [VM] * 8 + [HB],
        (sub1, core1, far, s0, s1, s2, s3, rows_near, gain_g_near, far_x, grid_grad),
        1 << 29, 3 << 20, "grid_far", grid_scratch, [HB], {10: 0},
    )
    whole = sds((4, width, width), F32)
    wide = [pltpu.VMEM((2, width, width), F32), pltpu.SemaphoreType.DMA((8,))]
    (weight_grads,) = call(
        functools.partial(widen_body, 0), [whole], [SM, VM], (core1, mine), 1 << 20, 3 << 20, "widen_own",
        wide, [HB],
    )
    (weight_grads,) = call(
        functools.partial(widen_body, 1), [whole], [SM, VM, HB], (core1, theirs, weight_grads),
        1 << 20, 3 << 20, "widen_other", wide, [HB], {2: 0},
    )
    return mesh_out, mesh_grad, grid_grad, weight_grads


def solution(mesh):
    split = Mesh(mesh.devices.reshape(4, 4, 2, mesh.shape["sub"]), ALL)
    rows = P(ALL, None)
    return jax.shard_map(
        shards,
        mesh=split,
        in_specs=(rows, rows, P(), P(), P(), P(), P(), P(), rows, rows, rows,
                  P(ALL, None, None, None), rows),
        out_specs=(rows, rows, rows, P()),
        check_vma=False,
    )
```

```python
import functools

import jax
import jax.numpy as jnp
from jax import lax
from jax.experimental import pallas as pl
from jax.experimental.pallas import tpu as pltpu
from jax.sharding import Mesh
from jax.sharding import PartitionSpec as P

SLAB = ("gx", "gy", "gc")
PLANE = ("gx", "gy")
ALL = ("gx", "gy", "gc", "z")

EPSILON = 1e-06
ABSENT = -1e30
F32 = jnp.float32
BF16 = jnp.bfloat16

VM = pl.BlockSpec(memory_space=pltpu.VMEM)
SM = pl.BlockSpec(memory_space=pltpu.SMEM)
HB = pl.BlockSpec(memory_space=pltpu.HBM)


def nn(a, b):
    return lax.dot_general(a, b, (((1,), (0,)), ((), ())), preferred_element_type=F32)


def nt(a, b):
    return lax.dot_general(a, b, (((1,), (1,)), ((), ())), preferred_element_type=F32)


def tn(a, b):
    return lax.dot_general(a, b, (((0,), (0,)), ((), ())), preferred_element_type=F32)


def inv_rms(wide):
    return lax.rsqrt(jnp.mean(wide * wide, axis=-1, keepdims=True) + EPSILON)


def norm_back(wide, factor, gain_row, upstream):
    scaled = gain_row * upstream
    inner = jnp.mean(wide * scaled, axis=-1, keepdims=True)
    return factor * scaled - wide * (factor * factor * factor * inner)


def call(body, outs, in_specs, args, flops, nbytes, name, scratch=(), out_specs=None, aliases=None):
    return pl.pallas_call(
        body,
        out_shape=outs,
        in_specs=in_specs,
        out_specs=out_specs or [VM] * len(outs),
        scratch_shapes=list(scratch),
        input_output_aliases=aliases or {},
        compiler_params=pltpu.CompilerParams(vmem_limit_bytes=16 << 20),
        cost_estimate=pl.CostEstimate(flops=flops, bytes_accessed=nbytes, transcendentals=0),
        name=name,
    )(*args)


def fetch(sources, targets, sems):
    copies = []
    for i, (source, target) in enumerate(zip(sources, targets)):
        copies.append(pltpu.make_async_copy(source, target, sems.at[i]))
        copies[-1].start()
    return copies


def held(*args):
    return [pltpu.VMEM(a.shape, a.dtype) for a in args] + [pltpu.SemaphoreType.DMA((len(args),))]


def assemble(rows, near_first, near, far, own, *pieces):
    block = near.shape[0]
    cap = block // 4
    near_at = pl.multiple_of((1 - near_first) * (2 * block), block)
    far_at = pl.multiple_of(near_first * (2 * block), block)
    rows[block : block + cap] = own[0:cap]
    rows[pl.ds(near_at, cap), :] = near[0:cap]
    rows[pl.ds(far_at, cap), :] = far[0:cap]
    for k in range(1, 4):
        mixed, last = pieces[k - 1], pieces[len(pieces) - 4 + k]
        rows[block + k * cap : block + (k + 1) * cap] = mixed[0:cap]
        rows[pl.ds(near_at + k * cap, cap), :] = mixed[cap : 2 * cap]
        rows[pl.ds(far_at + k * cap, cap), :] = last[last.shape[0] - cap :]


def gather_body(sub_ref, core_ref, rows_hbm, gain_hbm, x_hbm, near_ref, far_ref, rows_ref, gain_ref,
                x_ref, sems):
    half = x_ref.shape[0] // 2
    core = core_ref[0]
    firsts = [pl.multiple_of((1 - core) * half, half), pl.multiple_of(core * half, half)]
    parts = [pl.ds(first, half) for first in firsts]
    copies = fetch(
        [rows_hbm, gain_hbm] + [x_hbm.at[p] for p in parts],
        [rows_ref, gain_ref] + [x_ref.at[p] for p in parts],
        sems,
    )
    copies[0].wait()
    copies[1].wait()
    steps = ((2 - 2 * core, firsts[0], near_ref), (2 * core, firsts[1], far_ref))
    for step, (o, first, out_ref) in enumerate(steps):
        onehot = picks(sub_ref, rows_ref, o, first, half)
        copies[2 + step].wait()
        out_ref[...] = normed_rows(onehot, x_ref[pl.ds(first, half), :], gain_ref)


def own_body(sub_ref, rows_ref, gain_ref, x_ref, *refs):
    later = (len(refs) - 2) // 2
    own_ref = refs[later]
    copies = fetch(refs[:later], refs[later + 1 : -1], refs[-1])
    onehot = picks(sub_ref, rows_ref, 1, 0, x_ref.shape[0])
    own_ref[...] = normed_rows(onehot, x_ref[...], gain_ref)
    for copy in copies:
        copy.wait()


def picks(sub_ref, rows_ref, o, first, count):
    cap = rows_ref.shape[3]
    eye = lax.broadcasted_iota(jnp.int32, (cap, cap), 0) == lax.broadcasted_iota(
        jnp.int32, (cap, cap), 1
    )
    cols = []
    for k in range(4):
        row = rows_ref[0, o, pl.ds(lax.rem(sub_ref[0] + k, 4), 1), :].astype(F32)
        cols.append(jnp.sum(jnp.where(eye, row, 0.0), axis=1, keepdims=True))
    col = jnp.concatenate(cols, axis=0).astype(jnp.int32) - first
    lanes = lax.broadcasted_iota(jnp.int32, (4 * cap, count), 1)
    return jnp.where(lanes == col, 1.0, 0.0).astype(BF16)


def normed_rows(onehot, points, gain_ref):
    wide = nn(onehot, points)
    return (wide * inv_rms(wide) * gain_ref[...]).astype(BF16)


def mesh_in_body(mesh_ref, gain_ref, wq_ref, wo_ref, og_ref, normed_ref, q_ref, ag_ref):
    wide = mesh_ref[...].astype(F32)
    normed = (wide * inv_rms(wide) * gain_ref[...]).astype(BF16)
    normed_ref[...] = normed
    q_ref[...] = (nn(normed, wq_ref[...]) * (128 ** -0.5)).astype(BF16)
    ag_ref[...] = nt(og_ref[...], wo_ref[...]).astype(BF16)


def slots_body(sub_ref, nbr_ref, valid_ref, bias_ref, wk_hbm, wv_hbm, dense_ref, wkv_ref,
               inv_ref, edge_ref, sems):
    width = wk_hbm.shape[0]
    copies = fetch(
        (wk_hbm, wv_hbm), (wkv_ref.at[:, pl.ds(0, width)], wkv_ref.at[:, pl.ds(width, width)]), sems
    )
    heads, nodes, slots = dense_ref.shape
    fan = nbr_ref.shape[1]
    slot = nbr_ref[...]
    slot = (slot & ~192) | (((sub_ref[0] - (slot >> 6)) & 3) << 6)
    high, low = slot >> 7, slot & 127
    blocks = lax.broadcasted_iota(jnp.int32, (8, fan), 0)
    lanes = lax.broadcasted_iota(jnp.int32, (128, fan), 0)
    edge = lax.broadcasted_iota(jnp.int32, (8, fan), 1).astype(F32) + 1.0
    for m in range(nodes):
        named = jnp.where(high[m : m + 1, :] == blocks, edge, 0.0).astype(BF16)
        places = jnp.where(low[m : m + 1, :] == lanes, 1.0, 0.0).astype(BF16)
        inv_ref[m * 8 : (m + 1) * 8, :] = nt(named, places)
    live = valid_ref[...] == 1
    for h in range(heads):
        edge_ref[h, :, 0:fan] = jnp.where(live, bias_ref[:, h * fan : (h + 1) * fan], ABSENT)
    for b in range(slots // 128):
        at = inv_ref[pl.ds(b, nodes, stride=8), :].astype(jnp.int32) - 1
        here = at >= 0
        at = jnp.maximum(at, 0)
        for h in range(heads):
            got = jnp.take_along_axis(edge_ref[h], at, axis=1, mode="promise_in_bounds")
            dense_ref[h, :, b * 128 : (b + 1) * 128] = jnp.where(here, got, ABSENT)
    for copy in copies:
        copy.wait()


def middle_body(core_ref, near, far, own, m1, m2, m3, f1, f2, f3, q_ref, ag_ref, mn_ref, og_ref,
                bias_ref, wkv_ref, send_ref, part_ref, att_ref, qg_ref, rows, keys, vals):
    width = q_ref.shape[1]
    heads = bias_ref.shape[0]
    core = core_ref[0]
    assemble(rows, 1 - core, near, far, own, m1, m2, m3, f1, f2, f3)
    keys[...] = nn(rows[...], wkv_ref[:, :width]).astype(BF16)
    vals[...] = nn(rows[...], wkv_ref[:, width:]).astype(BF16)
    for h in range(heads):
        at = slice(h * 128, (h + 1) * 128)
        q, ag = q_ref[:, at], ag_ref[:, at]
        kh, vh = keys[:, at], vals[:, at]
        scores = nt(q, kh) + bias_ref[h]
        peak = jnp.max(scores, axis=1, keepdims=True)
        terms = jnp.exp(scores - peak)
        probs = terms * (1.0 / jnp.sum(terms, axis=1, keepdims=True))
        probs_b = probs.astype(BF16)
        att_ref[:, at] = nn(probs_b, vh).astype(BF16)
        pg = nt(ag, vh)
        sg = (probs * (pg - jnp.sum(probs * pg, axis=1, keepdims=True))).astype(BF16)
        qg_ref[:, at] = (nn(sg, kh) * (128 ** -0.5)).astype(BF16)
        part_ref[:, at] = tn(sg, q).astype(BF16)
        part_ref[:, width + h * 128 : width + (h + 1) * 128] = tn(probs_b, ag).astype(BF16)
    half_grads(1 - core, send_ref, rows, part_ref, mn_ref, qg_ref, att_ref, og_ref)


def half_grads(half, out_ref, rows, part_ref, mn_ref, qg_ref, att_ref, og_ref):
    width = mn_ref.shape[1]
    first = half == 0
    left = jnp.where(first, mn_ref[...].astype(F32), att_ref[...].astype(F32)).astype(BF16)
    right = jnp.where(first, qg_ref[...].astype(F32), og_ref[...].astype(F32)).astype(BF16)
    columns = pl.ds(pl.multiple_of(half * width, width), width)
    out_ref[0:width] = tn(left, right).astype(BF16)
    out_ref[width : 2 * width] = tn(rows[...], part_ref[:, columns]).astype(BF16)


def keep_body(core_ref, rows, part_ref, mn_ref, qg_ref, att_ref, og_ref, keep_ref):
    half_grads(core_ref[0], keep_ref, rows, part_ref, mn_ref, qg_ref, att_ref, og_ref)


def back_body(part_ref, wkv_ref, s0, s1, s2, s3):
    cap = s0.shape[1]
    for o in range(3):
        rows = slice(o * 4 * cap, (o + 1) * 4 * cap)
        back = nt(part_ref[rows, :], wkv_ref[...]).astype(BF16)
        for k, piece in enumerate((s0, s1, s2, s3)):
            piece[o] = back[k * cap : (k + 1) * cap]


def mesh_body(att_ref, qg_ref, og_ref, wo_ref, wq_ref, mesh_ref, gain_ref, out_ref, grad_ref):
    wide = mesh_ref[...].astype(F32)
    out_ref[...] = (wide + nn(att_ref[...], wo_ref[...])).astype(BF16)
    upstream = nt(qg_ref[...], wq_ref[...])
    back = norm_back(wide, inv_rms(wide), gain_ref[...], upstream)
    grad_ref[...] = (og_ref[...].astype(F32) + back).astype(BF16)


def pack_body(core_ref, p0, p1, p2, p3, near_ref, far_ref):
    cap = p0.shape[1]
    near = core_ref[0] * 2
    for k, piece in enumerate((p0, p1, p2, p3)):
        near_ref[k * cap : (k + 1) * cap, :] = piece[near]
        far_ref[k * cap : (k + 1) * cap, :] = piece[2 - near]


def mix_body(own, near, m1, m2, m3):
    cap = m1.shape[0] // 2
    for k, mixed in enumerate((m1, m2, m3), 1):
        mixed[0:cap] = own[k * cap : (k + 1) * cap]
        mixed[cap : 2 * cap] = near[k * cap : (k + 1) * cap]


def split_body(block, f1, f2, f3):
    cap = f1.shape[0]
    for k, piece in enumerate((f1, f2, f3), 1):
        piece[...] = block[k * cap : (k + 1) * cap]


def grid_half(upper, sub_ref, outer, s0, s1, s2, s3, rows_ref, gain_ref, x_ref, out_hbm, got, done_ref,
              sems, ready):
    half = x_ref.shape[0]
    base = pl.multiple_of(upper * half, half)
    cap = rows_ref.shape[3]
    block = 4 * cap
    me = sub_ref[0]
    got[0:block] = outer[...]
    for k, piece in enumerate((s0, s1, s2, s3)):
        got[block + k * cap : block + (k + 1) * cap] = piece[1]
    gain = gain_ref[...]
    idx = []
    for o in (2 * upper, 1):
        for k in range(4):
            idx.append(rows_ref[0, o, pl.ds(lax.rem(me + k, 4), 1), :])
    idx = jnp.concatenate(idx, axis=1) - base
    tile = 256
    stores = []
    for t in range(half // tile):
        part = slice(t * tile, (t + 1) * tile)
        ids = lax.broadcasted_iota(jnp.int32, (tile, 2 * block), 0) + t * tile
        onehot = jnp.where(ids == idx, 1.0, 0.0).astype(BF16)
        upstream = nn(onehot, got[...])
        if t == 0:
            ready()
        wide = x_ref[part, :].astype(F32)
        done_ref[part, :] = norm_back(wide, inv_rms(wide), gain, upstream).astype(BF16)
        stores.append(
            pltpu.make_async_copy(
                done_ref.at[part], out_hbm.at[pl.ds(base + t * tile, tile)], sems.at[t]
            )
        )
        stores[-1].start()
    for store in stores:
        store.wait()


def grid_near_body(sub_ref, core_ref, near, s0, s1, s2, s3, rows_ref, gain_ref, x_hbm,
                   out_hbm, far_x_ref, got, done_ref, done_sems, x_ref, sems):
    half = x_ref.shape[0]
    upper = 1 - core_ref[0]
    copies = fetch(
        [x_hbm.at[pl.ds(pl.multiple_of(u * half, half), half)] for u in (upper, core_ref[0])],
        [x_ref, far_x_ref],
        sems,
    )
    grid_half(upper, sub_ref, near, s0, s1, s2, s3, rows_ref, gain_ref, x_ref, out_hbm, got, done_ref,
              done_sems, copies[0].wait)
    copies[1].wait()


def grid_far_body(sub_ref, core_ref, far, s0, s1, s2, s3, rows_ref, gain_ref, x_ref, mine_ref, prior_hbm,
                  out_hbm, weights_hbm, got, done_ref, done_sems, wide, wide_sems):
    copies = widen(core_ref[0], mine_ref, weights_hbm, wide, wide_sems)
    grid_half(core_ref[0], sub_ref, far, s0, s1, s2, s3, rows_ref, gain_ref, x_ref, out_hbm, got,
              done_ref, done_sems, lambda: None)
    for copy in copies:
        copy.wait()


def widen(half, half_ref, out_hbm, wide, sems):
    count, width, _ = wide.shape
    part = width // 4
    copies = []
    for i in range(4 * count):
        m, rows = i // 4, pl.ds((i % 4) * part, part)
        wide[m, rows, :] = half_ref[i * part : (i + 1) * part, :].astype(F32)
        copies.append(
            pltpu.make_async_copy(
                wide.at[m, rows], out_hbm.at[lax.select(half == 0, m, 3 - m), rows], sems.at[i]
            )
        )
        copies[-1].start()
    return copies


def widen_body(core_ref, half_ref, prior_hbm, out_hbm, wide, sems):
    for copy in widen(1 - core_ref[0], half_ref, out_hbm, wide, sems):
        copy.wait()


def pair_body(keep_ref, other_ref, out_hbm, sums, sems):
    part = sums.shape[0] // 4
    copies = []
    for i in range(4):
        at = slice(i * part, (i + 1) * part)
        sums[at, :] = (keep_ref[at, :].astype(F32) + other_ref[at, :].astype(F32)).astype(BF16)
        copies.append(pltpu.make_async_copy(sums.at[at], out_hbm.at[at], sems.at[i]))
        copies[-1].start()
    for copy in copies:
        copy.wait()


def plane_body(parts_ref, out_ref):
    total = parts_ref[0].astype(F32)
    for i in range(1, parts_ref.shape[0]):
        total = total + parts_ref[i].astype(F32)
    out_ref[...] = total.astype(BF16)


def spread_body(p0, p1, p2, p3, out_hbm, total, sems):
    even = p0[...].astype(F32) + p2[...].astype(F32)
    odd = p1[...].astype(F32) + p3[...].astype(F32)
    total[...] = (even + odd).astype(BF16)
    copies = []
    for i in range(out_hbm.shape[0]):
        copies.append(pltpu.make_async_copy(total, out_hbm.at[i], sems.at[i]))
        copies[-1].start()
    for copy in copies:
        copy.wait()


def shifted(block, axis, k):
    n = lax.axis_size(axis)
    return lax.ppermute(block, axis, [(i, (i + k) % n) for i in range(n)])


def swapped_far(block):
    n = lax.axis_size(SLAB)
    pairs = [(i, i + 1) for i in range(1, n - 1, 2)]
    return lax.ppermute(block, SLAB, pairs + [(j, i) for i, j in pairs])


def sds(shape, dtype=BF16):
    return jax.ShapeDtypeStruct(shape, dtype)


def shards(grid_x, mesh_h, gain_grid, gain_mesh, w_query, w_key, w_value, w_out, edge_bias,
           neighbours, valid, send_rows, out_grad):
    points, width = grid_x.shape
    nodes, fan = neighbours.shape
    cap = send_rows.shape[3]
    block = 4 * cap
    slots = 3 * block
    heads = edge_bias.shape[1] // fan
    sub1 = lax.axis_index("z").astype(jnp.int32).reshape(1)
    core1 = lax.axis_index("gc").astype(jnp.int32).reshape(1)
    gain_g, gain_m = gain_grid.reshape(1, width), gain_mesh.reshape(1, width)
    (grid_x, mesh_h, out_grad, send_rows, w_key, w_value, w_query, w_out, gain_g, gain_m, edge_bias,
     neighbours, valid) = (
        pltpu.with_memory_space_constraint(a, pltpu.HBM)
        for a in (grid_x, mesh_h, out_grad, send_rows, w_key, w_value, w_query, w_out, gain_g, gain_m,
                  edge_bias, neighbours, valid)
    )

    one, two, four = sds((cap, width)), sds((2 * cap, width)), sds((block, width))
    later = (mesh_h, gain_m, w_query, w_out, out_grad, neighbours, valid, edge_bias)
    near, far, rows_near, gain_g_near, x_near = call(
        gather_body,
        [four] * 2 + [sds(a.shape, a.dtype) for a in (send_rows, gain_g, grid_x)],
        [SM, SM] + [HB] * 3, (sub1, core1, send_rows, gain_g, grid_x), 1 << 30, 3 << 20, "gather_rows",
        [pltpu.SemaphoreType.DMA((4,))],
    )
    own, *later = call(
        own_body, [four] + [sds(a.shape, a.dtype) for a in later], [SM] + [VM] * 3 + [HB] * len(later),
        (sub1, rows_near, gain_g_near, x_near, *later), 1 << 29, 4 << 20, "own_rows",
        [pltpu.SemaphoreType.DMA((len(later),))],
    )
    mesh_near, gain_near, wq_near, wo_near, og_near, nbr_near, valid_near, bias_near = later
    far = swapped_far(far)
    near = shifted(near, "gc", 1)
    mixed = call(mix_body, [two] * 3, [VM] * 2, (own, near), 0, 1 << 20, "mix")
    mixed = [shifted(m, "z", k) for k, m in enumerate(mixed, 1)]
    mesh_normed, queries, att_grad = call(
        mesh_in_body, [sds((nodes, width))] * 3, [VM] * 5,
        (mesh_near, gain_near, wq_near, wo_near, og_near), 1 << 28, 2 << 20, "mesh_in",
    )
    far, mixed[0], queries = lax.optimization_barrier((far, mixed[0], queries))
    outer = call(split_body, [one] * 3, [VM], (far,), 0, 1 << 19, "split")
    outer = [shifted(f, "z", k) for k, f in enumerate(outer, 1)]
    received = near, far, own, *mixed, *outer
    sub2, far = lax.optimization_barrier((sub1, far))
    dense, weights_near = call(
        slots_body, [sds((heads, nodes, slots), F32), sds((width, 2 * width))],
        [SM] + [VM] * 3 + [HB] * 2,
        (sub2, nbr_near, valid_near, bias_near, w_key, w_value), 1 << 30, 8 << 20, "slots",
        [pltpu.VMEM((nodes * 8, 128), F32), pltpu.VMEM((heads, nodes, 128), F32),
         pltpu.SemaphoreType.DMA((2,))],
    )
    send, part_grads, attended, query_grad, rows = call(
        middle_body,
        [sds((2 * width, width)), sds((slots, 2 * width))] + [sds((nodes, width))] * 2
        + [sds((slots, width))],
        [SM] + [VM] * 15,
        (core1, *received, queries, att_grad, mesh_normed, og_near, dense, weights_near),
        3 << 30, 8 << 20, "middle", [pltpu.VMEM((slots, width), BF16)] * 2,
    )

    other = shifted(send, "gc", 1)
    (keep,) = call(
        keep_body, [sds((2 * width, width))], [SM] + [VM] * 6,
        (core1, rows, part_grads, mesh_normed, query_grad, attended, og_near), 1 << 29, 3 << 20, "keep",
    )
    s0, s1, s2, s3 = call(
        back_body, [sds((3, cap, width))] * 4, [VM] * 2, (part_grads, weights_near),
        1 << 30, 3 << 20, "back",
    )
    other, s1, keep = lax.optimization_barrier((other, s1, keep))
    (own,) = call(
        pair_body, [sds((2 * width, width))], [VM] * 2, (keep, other), 1 << 20, 3 << 20, "pair",
        [pltpu.VMEM((2 * width, width), BF16), pltpu.SemaphoreType.DMA((4,))], [HB],
    )
    plane = lax.axis_size(PLANE)
    share = 2 * width // plane
    parts = lax.all_to_all(own.reshape(plane, share, width), PLANE, 0, 0, tiled=True)

    attended, own = lax.optimization_barrier((attended, own))
    mesh_out, mesh_grad = call(
        mesh_body, [sds((nodes, width))] * 2, [VM] * 7,
        (attended, query_grad, og_near, wo_near, wq_near, mesh_near, gain_near), 1 << 28, 2 << 20, "mesh",
    )
    s1, s2, s3 = (shifted(s, "z", -k) for k, s in ((1, s1), (2, s2), (3, s3)))
    s1, s2, s3, parts, mesh_out = lax.optimization_barrier((s1, s2, s3, parts, mesh_out))
    (part,) = call(plane_body, [sds((share, width))], [VM], (parts,), 1 << 20, 1 << 20, "plane")
    part, s0 = lax.optimization_barrier((part, s0))
    near, far = call(
        pack_body, [four] * 2, [SM] + [VM] * 4, (core1, s0, s1, s2, s3), 0, 1 << 20, "pack"
    )
    far = swapped_far(far)
    near = shifted(near, "gc", 1)
    p1, p2, p3 = (shifted(part, "z", k) for k in (1, 2, 3))
    (spread,) = call(
        spread_body, [sds((plane, share, width))], [VM] * 4, (part, p1, p2, p3), 1 << 18, 1 << 20,
        "spread", [pltpu.VMEM((share, width), BF16), pltpu.SemaphoreType.DMA((plane,))], [HB],
    )
    mine = lax.all_to_all(spread, PLANE, 0, 0, tiled=True).reshape(2 * width, width)
    half = points // 2
    grid_scratch = [
        pltpu.VMEM((2 * block, width), BF16), pltpu.VMEM((half, width), BF16),
        pltpu.SemaphoreType.DMA((half // 256,)),
    ]
    grid_grad, far_x = call(
        grid_near_body, [sds((points, width)), sds((half, width))], [SM] * 2 + [VM] * 7 + [HB],
        (sub1, core1, near, s0, s1, s2, s3, rows_near, gain_g_near, grid_x),
        1 << 29, 3 << 20, "grid_near",
        grid_scratch + [pltpu.VMEM((half, width), BF16), pltpu.SemaphoreType.DMA((2,))], [HB, VM],
    )
    mine, far, grid_grad = lax.optimization_barrier((mine, far, grid_grad))
    theirs = shifted(mine, "gc", 1)
    whole = sds((4, width, width), F32)
    wide = [pltpu.VMEM((2, width, width), F32), pltpu.SemaphoreType.DMA((8,))]
    grid_grad, weight_grads = call(
        grid_far_body, [sds((points, width)), whole], [SM] * 2 + [VM] * 9 + [HB],
        (sub1, core1, far, s0, s1, s2, s3, rows_near, gain_g_near, far_x, mine, grid_grad),
        1 << 29, 5 << 20, "grid_far", grid_scratch + wide, [HB, HB], {11: 0},
    )
    (weight_grads,) = call(
        widen_body, [whole], [SM, VM, HB], (core1, theirs, weight_grads), 1 << 20, 3 << 20, "widen", wide,
        [HB], {2: 0},
    )
    return mesh_out, mesh_grad, grid_grad, weight_grads


def solution(mesh):
    split = Mesh(mesh.devices.reshape(4, 4, 2, mesh.shape["sub"]), ALL)
    rows = P(ALL, None)
    return jax.shard_map(
        shards,
        mesh=split,
        in_specs=(rows, rows, P(), P(), P(), P(), P(), P(), rows, rows, rows,
                  P(ALL, None, None, None), rows),
        out_specs=(rows, rows, rows, P()),
        check_vma=False,
    )
```

```python
import functools

import jax
import jax.numpy as jnp
from jax import lax
from jax.experimental import pallas as pl
from jax.experimental.pallas import tpu as pltpu
from jax.sharding import Mesh
from jax.sharding import PartitionSpec as P

SLAB = ("gx", "gy", "gc")
PLANE = ("gx", "gy")
ALL = ("gx", "gy", "gc", "z")

EPSILON = 1e-06
ABSENT = -1e30
F32 = jnp.float32
BF16 = jnp.bfloat16

VM = pl.BlockSpec(memory_space=pltpu.VMEM)
SM = pl.BlockSpec(memory_space=pltpu.SMEM)
HB = pl.BlockSpec(memory_space=pltpu.HBM)


def nn(a, b):
    return lax.dot_general(a, b, (((1,), (0,)), ((), ())), preferred_element_type=F32)


def nt(a, b):
    return lax.dot_general(a, b, (((1,), (1,)), ((), ())), preferred_element_type=F32)


def tn(a, b):
    return lax.dot_general(a, b, (((0,), (0,)), ((), ())), preferred_element_type=F32)


def inv_rms(wide):
    return lax.rsqrt(jnp.mean(wide * wide, axis=-1, keepdims=True) + EPSILON)


def norm_back(wide, factor, gain_row, upstream):
    scaled = gain_row * upstream
    inner = jnp.mean(wide * scaled, axis=-1, keepdims=True)
    return factor * scaled - wide * (factor * factor * factor * inner)


def call(body, outs, in_specs, args, flops, nbytes, name, scratch=(), out_specs=None, aliases=None):
    return pl.pallas_call(
        body,
        out_shape=outs,
        in_specs=in_specs,
        out_specs=out_specs or [VM] * len(outs),
        scratch_shapes=list(scratch),
        input_output_aliases=aliases or {},
        compiler_params=pltpu.CompilerParams(vmem_limit_bytes=16 << 20),
        cost_estimate=pl.CostEstimate(flops=flops, bytes_accessed=nbytes, transcendentals=0),
        name=name,
    )(*args)


def fetch(sources, targets, sems):
    copies = []
    for i, (source, target) in enumerate(zip(sources, targets)):
        copies.append(pltpu.make_async_copy(source, target, sems.at[i]))
        copies[-1].start()
    return copies


def held(*args):
    return [pltpu.VMEM(a.shape, a.dtype) for a in args] + [pltpu.SemaphoreType.DMA((len(args),))]


def assemble(rows, near_first, near, far, own, *pieces):
    block = near.shape[0]
    cap = block // 4
    near_at = pl.multiple_of((1 - near_first) * (2 * block), block)
    far_at = pl.multiple_of(near_first * (2 * block), block)
    rows[block : block + cap] = own[0:cap]
    rows[pl.ds(near_at, cap), :] = near[0:cap]
    rows[pl.ds(far_at, cap), :] = far[0:cap]
    for k in range(1, 4):
        mixed, last = pieces[k - 1], pieces[len(pieces) - 4 + k]
        rows[block + k * cap : block + (k + 1) * cap] = mixed[0:cap]
        rows[pl.ds(near_at + k * cap, cap), :] = mixed[cap : 2 * cap]
        rows[pl.ds(far_at + k * cap, cap), :] = last[last.shape[0] - cap :]


def gather_body(sub_ref, core_ref, rows_hbm, gain_hbm, x_hbm, *refs):
    later = (len(refs) - 8) // 2
    later_hbm, refs = refs[:later], refs[later:]
    near_ref, far_ref, own_ref, rows_ref, gain_ref = refs[:5]
    later_refs = refs[5 : 5 + later]
    x_ref, sems, later_sems = refs[-3:]
    half = x_ref.shape[0] // 2
    cap = rows_ref.shape[3]
    core = core_ref[0]
    firsts = [pl.multiple_of((1 - core) * half, half), pl.multiple_of(core * half, half)]
    parts = [pl.ds(first, half) for first in firsts]
    copies = fetch(
        [rows_hbm, gain_hbm] + [x_hbm.at[p] for p in parts],
        [rows_ref, gain_ref] + [x_ref.at[p] for p in parts],
        sems,
    )
    copies[0].wait()
    copies[1].wait()
    me = sub_ref[0]
    eye = lax.broadcasted_iota(jnp.int32, (cap, cap), 0) == lax.broadcasted_iota(
        jnp.int32, (cap, cap), 1
    )
    gain = gain_ref[...]
    steps = (
        (2 - 2 * core, firsts[0], half, near_ref),
        (2 * core, firsts[1], half, far_ref),
        (1, 0, 2 * half, own_ref),
    )
    for step, (o, first, count, out_ref) in enumerate(steps):
        cols = []
        for k in range(4):
            s = lax.rem(me + k, 4)
            row = rows_ref[0, o, pl.ds(s, 1), :].astype(F32)
            cols.append(jnp.sum(jnp.where(eye, row, 0.0), axis=1, keepdims=True))
        col = jnp.concatenate(cols, axis=0).astype(jnp.int32) - first
        lanes = lax.broadcasted_iota(jnp.int32, (4 * cap, count), 1)
        onehot = jnp.where(lanes == col, 1.0, 0.0).astype(BF16)
        if step < 2:
            copies[2 + step].wait()
        if step == 1:
            later_copies = fetch(later_hbm, later_refs, later_sems)
        wide = nn(onehot, x_ref[pl.ds(first, count), :])
        out_ref[...] = (wide * inv_rms(wide) * gain).astype(BF16)
    for copy in later_copies:
        copy.wait()


def mesh_in_body(mesh_ref, gain_ref, wq_ref, wo_ref, og_ref, normed_ref, q_ref, ag_ref):
    wide = mesh_ref[...].astype(F32)
    normed = (wide * inv_rms(wide) * gain_ref[...]).astype(BF16)
    normed_ref[...] = normed
    q_ref[...] = (nn(normed, wq_ref[...]) * (128 ** -0.5)).astype(BF16)
    ag_ref[...] = nt(og_ref[...], wo_ref[...]).astype(BF16)


def slots_body(sub_ref, nbr_ref, valid_ref, bias_ref, wk_hbm, wv_hbm, dense_ref, wkv_ref,
               inv_ref, edge_ref, sems):
    width = wk_hbm.shape[0]
    copies = fetch(
        (wk_hbm, wv_hbm), (wkv_ref.at[:, pl.ds(0, width)], wkv_ref.at[:, pl.ds(width, width)]), sems
    )
    heads, nodes, slots = dense_ref.shape
    fan = nbr_ref.shape[1]
    slot = nbr_ref[...]
    slot = (slot & ~192) | (((sub_ref[0] - (slot >> 6)) & 3) << 6)
    high, low = slot >> 7, slot & 127
    blocks = lax.broadcasted_iota(jnp.int32, (8, fan), 0)
    lanes = lax.broadcasted_iota(jnp.int32, (128, fan), 0)
    edge = lax.broadcasted_iota(jnp.int32, (8, fan), 1).astype(F32) + 1.0
    for m in range(nodes):
        named = jnp.where(high[m : m + 1, :] == blocks, edge, 0.0).astype(BF16)
        places = jnp.where(low[m : m + 1, :] == lanes, 1.0, 0.0).astype(BF16)
        inv_ref[m * 8 : (m + 1) * 8, :] = nt(named, places)
    live = valid_ref[...] == 1
    for h in range(heads):
        edge_ref[h, :, 0:fan] = jnp.where(live, bias_ref[:, h * fan : (h + 1) * fan], ABSENT)
    for b in range(slots // 128):
        at = inv_ref[pl.ds(b, nodes, stride=8), :].astype(jnp.int32) - 1
        here = at >= 0
        at = jnp.maximum(at, 0)
        for h in range(heads):
            got = jnp.take_along_axis(edge_ref[h], at, axis=1, mode="promise_in_bounds")
            dense_ref[h, :, b * 128 : (b + 1) * 128] = jnp.where(here, got, ABSENT)
    for copy in copies:
        copy.wait()


def middle_body(core_ref, near, far, own, m1, m2, m3, f1, f2, f3, q_ref, ag_ref, mn_ref, og_ref,
                bias_ref, wkv_ref, send_ref, part_ref, att_ref, qg_ref, rows, keys, vals):
    width = q_ref.shape[1]
    heads = bias_ref.shape[0]
    core = core_ref[0]
    assemble(rows, 1 - core, near, far, own, m1, m2, m3, f1, f2, f3)
    keys[...] = nn(rows[...], wkv_ref[:, :width]).astype(BF16)
    vals[...] = nn(rows[...], wkv_ref[:, width:]).astype(BF16)
    for h in range(heads):
        at = slice(h * 128, (h + 1) * 128)
        q, ag = q_ref[:, at], ag_ref[:, at]
        kh, vh = keys[:, at], vals[:, at]
        scores = nt(q, kh) + bias_ref[h]
        peak = jnp.max(scores, axis=1, keepdims=True)
        terms = jnp.exp(scores - peak)
        probs = terms * (1.0 / jnp.sum(terms, axis=1, keepdims=True))
        probs_b = probs.astype(BF16)
        att_ref[:, at] = nn(probs_b, vh).astype(BF16)
        pg = nt(ag, vh)
        sg = (probs * (pg - jnp.sum(probs * pg, axis=1, keepdims=True))).astype(BF16)
        qg_ref[:, at] = (nn(sg, kh) * (128 ** -0.5)).astype(BF16)
        part_ref[:, at] = tn(sg, q).astype(BF16)
        part_ref[:, width + h * 128 : width + (h + 1) * 128] = tn(probs_b, ag).astype(BF16)
    half_grads(1 - core, send_ref, rows, part_ref, mn_ref, qg_ref, att_ref, og_ref)


def half_grads(half, out_ref, rows, part_ref, mn_ref, qg_ref, att_ref, og_ref):
    width = mn_ref.shape[1]
    first = half == 0
    left = jnp.where(first, mn_ref[...].astype(F32), att_ref[...].astype(F32)).astype(BF16)
    right = jnp.where(first, qg_ref[...].astype(F32), og_ref[...].astype(F32)).astype(BF16)
    columns = pl.ds(pl.multiple_of(half * width, width), width)
    out_ref[0:width] = tn(left, right).astype(BF16)
    out_ref[width : 2 * width] = tn(rows[...], part_ref[:, columns]).astype(BF16)


def keep_body(core_ref, rows, part_ref, mn_ref, qg_ref, att_ref, og_ref, keep_ref):
    half_grads(core_ref[0], keep_ref, rows, part_ref, mn_ref, qg_ref, att_ref, og_ref)


def back_body(part_ref, wkv_ref, s0, s1, s2, s3):
    cap = s0.shape[1]
    for o in range(3):
        rows = slice(o * 4 * cap, (o + 1) * 4 * cap)
        back = nt(part_ref[rows, :], wkv_ref[...]).astype(BF16)
        for k, piece in enumerate((s0, s1, s2, s3)):
            piece[o] = back[k * cap : (k + 1) * cap]


def mesh_body(att_ref, qg_ref, og_ref, wo_ref, wq_ref, mesh_ref, gain_ref, out_ref, grad_ref):
    wide = mesh_ref[...].astype(F32)
    out_ref[...] = (wide + nn(att_ref[...], wo_ref[...])).astype(BF16)
    upstream = nt(qg_ref[...], wq_ref[...])
    back = norm_back(wide, inv_rms(wide), gain_ref[...], upstream)
    grad_ref[...] = (og_ref[...].astype(F32) + back).astype(BF16)


def pack_body(core_ref, p0, p1, p2, p3, near_ref, far_ref):
    cap = p0.shape[1]
    near = core_ref[0] * 2
    for k, piece in enumerate((p0, p1, p2, p3)):
        near_ref[k * cap : (k + 1) * cap, :] = piece[near]
        far_ref[k * cap : (k + 1) * cap, :] = piece[2 - near]


def mix_body(own, near, m1, m2, m3):
    cap = m1.shape[0] // 2
    for k, mixed in enumerate((m1, m2, m3), 1):
        mixed[0:cap] = own[k * cap : (k + 1) * cap]
        mixed[cap : 2 * cap] = near[k * cap : (k + 1) * cap]


def split_body(block, f1, f2, f3):
    cap = f1.shape[0]
    for k, piece in enumerate((f1, f2, f3), 1):
        piece[...] = block[k * cap : (k + 1) * cap]


def grid_half(upper, sub_ref, outer, s0, s1, s2, s3, rows_ref, gain_ref, x_ref, out_hbm, got, done_ref,
              sems, ready):
    half = x_ref.shape[0]
    base = pl.multiple_of(upper * half, half)
    cap = rows_ref.shape[3]
    block = 4 * cap
    me = sub_ref[0]
    got[0:block] = outer[...]
    for k, piece in enumerate((s0, s1, s2, s3)):
        got[block + k * cap : block + (k + 1) * cap] = piece[1]
    gain = gain_ref[...]
    idx = []
    for o in (2 * upper, 1):
        for k in range(4):
            idx.append(rows_ref[0, o, pl.ds(lax.rem(me + k, 4), 1), :])
    idx = jnp.concatenate(idx, axis=1) - base
    tile = 256
    stores = []
    for t in range(half // tile):
        part = slice(t * tile, (t + 1) * tile)
        ids = lax.broadcasted_iota(jnp.int32, (tile, 2 * block), 0) + t * tile
        onehot = jnp.where(ids == idx, 1.0, 0.0).astype(BF16)
        upstream = nn(onehot, got[...])
        if t == 0:
            ready()
        wide = x_ref[part, :].astype(F32)
        done_ref[part, :] = norm_back(wide, inv_rms(wide), gain, upstream).astype(BF16)
        stores.append(
            pltpu.make_async_copy(
                done_ref.at[part], out_hbm.at[pl.ds(base + t * tile, tile)], sems.at[t]
            )
        )
        stores[-1].start()
    for store in stores:
        store.wait()


def grid_near_body(sub_ref, core_ref, near, s0, s1, s2, s3, rows_ref, gain_ref, x_hbm, out_hbm,
                   got, done_ref, done_sems, x_ref, sems):
    half = x_ref.shape[0]
    upper = 1 - core_ref[0]
    (copy,) = fetch([x_hbm.at[pl.ds(pl.multiple_of(upper * half, half), half)]], [x_ref], sems)
    grid_half(upper, sub_ref, near, s0, s1, s2, s3, rows_ref, gain_ref, x_ref, out_hbm, got, done_ref,
              done_sems, copy.wait)


def grid_far_body(sub_ref, core_ref, far, s0, s1, s2, s3, rows_ref, gain_ref, mine_ref, x_hbm, prior_hbm,
                  out_hbm, weights_hbm, got, done_ref, done_sems, x_ref, sems, wide, wide_sems):
    half = x_ref.shape[0]
    upper = core_ref[0]
    (copy,) = fetch([x_hbm.at[pl.ds(pl.multiple_of(upper * half, half), half)]], [x_ref], sems)
    copies = widen(upper, mine_ref, weights_hbm, wide, wide_sems)
    grid_half(upper, sub_ref, far, s0, s1, s2, s3, rows_ref, gain_ref, x_ref, out_hbm, got, done_ref,
              done_sems, copy.wait)
    for copy in copies:
        copy.wait()


def widen(half, half_ref, out_hbm, wide, sems):
    count, width, _ = wide.shape
    part = width // 4
    copies = []
    for i in range(4 * count):
        m, rows = i // 4, pl.ds((i % 4) * part, part)
        wide[m, rows, :] = half_ref[i * part : (i + 1) * part, :].astype(F32)
        copies.append(
            pltpu.make_async_copy(
                wide.at[m, rows], out_hbm.at[lax.select(half == 0, m, 3 - m), rows], sems.at[i]
            )
        )
        copies[-1].start()
    return copies


def widen_body(core_ref, half_ref, prior_hbm, out_hbm, wide, sems):
    for copy in widen(1 - core_ref[0], half_ref, out_hbm, wide, sems):
        copy.wait()


def pair_body(keep_ref, other_ref, out_hbm, sums, sems):
    part = sums.shape[0] // 4
    copies = []
    for i in range(4):
        at = slice(i * part, (i + 1) * part)
        sums[at, :] = (keep_ref[at, :].astype(F32) + other_ref[at, :].astype(F32)).astype(BF16)
        copies.append(pltpu.make_async_copy(sums.at[at], out_hbm.at[at], sems.at[i]))
        copies[-1].start()
    for copy in copies:
        copy.wait()


def plane_body(parts_ref, out_ref):
    total = parts_ref[0].astype(F32)
    for i in range(1, parts_ref.shape[0]):
        total = total + parts_ref[i].astype(F32)
    out_ref[...] = total.astype(BF16)


def spread_body(p0, p1, p2, p3, out_hbm, total, sems):
    even = p0[...].astype(F32) + p2[...].astype(F32)
    odd = p1[...].astype(F32) + p3[...].astype(F32)
    total[...] = (even + odd).astype(BF16)
    copies = []
    for i in range(out_hbm.shape[0]):
        copies.append(pltpu.make_async_copy(total, out_hbm.at[i], sems.at[i]))
        copies[-1].start()
    for copy in copies:
        copy.wait()


def shifted(block, axis, k):
    n = lax.axis_size(axis)
    return lax.ppermute(block, axis, [(i, (i + k) % n) for i in range(n)])


def swapped_far(block):
    n = lax.axis_size(SLAB)
    pairs = [(i, i + 1) for i in range(1, n - 1, 2)]
    return lax.ppermute(block, SLAB, pairs + [(j, i) for i, j in pairs])


def sds(shape, dtype=BF16):
    return jax.ShapeDtypeStruct(shape, dtype)


def shards(grid_x, mesh_h, gain_grid, gain_mesh, w_query, w_key, w_value, w_out, edge_bias,
           neighbours, valid, send_rows, out_grad):
    points, width = grid_x.shape
    nodes, fan = neighbours.shape
    cap = send_rows.shape[3]
    block = 4 * cap
    slots = 3 * block
    heads = edge_bias.shape[1] // fan
    sub1 = lax.axis_index("z").astype(jnp.int32).reshape(1)
    core1 = lax.axis_index("gc").astype(jnp.int32).reshape(1)
    gain_g, gain_m = gain_grid.reshape(1, width), gain_mesh.reshape(1, width)
    (grid_x, mesh_h, out_grad, send_rows, w_key, w_value, w_query, w_out, gain_g, gain_m, edge_bias,
     neighbours, valid) = (
        pltpu.with_memory_space_constraint(a, pltpu.HBM)
        for a in (grid_x, mesh_h, out_grad, send_rows, w_key, w_value, w_query, w_out, gain_g, gain_m,
                  edge_bias, neighbours, valid)
    )

    one, two, four = sds((cap, width)), sds((2 * cap, width)), sds((block, width))
    later = (mesh_h, gain_m, w_query, w_out, out_grad, neighbours, valid, edge_bias)
    near, far, own, rows_near, gain_g_near, *later = call(
        gather_body,
        [four] * 3 + [sds(a.shape, a.dtype) for a in (send_rows, gain_g, *later)],
        [SM, SM] + [HB] * (3 + len(later)),
        (sub1, core1, send_rows, gain_g, grid_x, *later), 1 << 30, 5 << 20, "gather_rows",
        [pltpu.VMEM((points, width), BF16), pltpu.SemaphoreType.DMA((4,)),
         pltpu.SemaphoreType.DMA((len(later),))],
    )
    mesh_near, gain_near, wq_near, wo_near, og_near, nbr_near, valid_near, bias_near = later
    far = swapped_far(far)
    near = shifted(near, "gc", 1)
    mixed = call(mix_body, [two] * 3, [VM] * 2, (own, near), 0, 1 << 20, "mix")
    mixed = [shifted(m, "z", k) for k, m in enumerate(mixed, 1)]
    mesh_normed, queries, att_grad = call(
        mesh_in_body, [sds((nodes, width))] * 3, [VM] * 5,
        (mesh_near, gain_near, wq_near, wo_near, og_near), 1 << 28, 2 << 20, "mesh_in",
    )
    far, mixed[0], queries = lax.optimization_barrier((far, mixed[0], queries))
    outer = call(split_body, [one] * 3, [VM], (far,), 0, 1 << 19, "split")
    outer = [shifted(f, "z", k) for k, f in enumerate(outer, 1)]
    received = near, far, own, *mixed, *outer
    sub2, far = lax.optimization_barrier((sub1, far))
    dense, weights_near = call(
        slots_body, [sds((heads, nodes, slots), F32), sds((width, 2 * width))],
        [SM] + [VM] * 3 + [HB] * 2,
        (sub2, nbr_near, valid_near, bias_near, w_key, w_value), 1 << 30, 8 << 20, "slots",
        [pltpu.VMEM((nodes * 8, 128), F32), pltpu.VMEM((heads, nodes, 128), F32),
         pltpu.SemaphoreType.DMA((2,))],
    )
    send, part_grads, attended, query_grad, rows = call(
        middle_body,
        [sds((2 * width, width)), sds((slots, 2 * width))] + [sds((nodes, width))] * 2
        + [sds((slots, width))],
        [SM] + [VM] * 15,
        (core1, *received, queries, att_grad, mesh_normed, og_near, dense, weights_near),
        3 << 30, 8 << 20, "middle", [pltpu.VMEM((slots, width), BF16)] * 2,
    )

    other = shifted(send, "gc", 1)
    (keep,) = call(
        keep_body, [sds((2 * width, width))], [SM] + [VM] * 6,
        (core1, rows, part_grads, mesh_normed, query_grad, attended, og_near), 1 << 29, 3 << 20, "keep",
    )
    s0, s1, s2, s3 = call(
        back_body, [sds((3, cap, width))] * 4, [VM] * 2, (part_grads, weights_near),
        1 << 30, 3 << 20, "back",
    )
    other, s1, keep = lax.optimization_barrier((other, s1, keep))
    (own,) = call(
        pair_body, [sds((2 * width, width))], [VM] * 2, (keep, other), 1 << 20, 3 << 20, "pair",
        [pltpu.VMEM((2 * width, width), BF16), pltpu.SemaphoreType.DMA((4,))], [HB],
    )
    plane = lax.axis_size(PLANE)
    share = 2 * width // plane
    parts = lax.all_to_all(own.reshape(plane, share, width), PLANE, 0, 0, tiled=True)

    attended, own = lax.optimization_barrier((attended, own))
    mesh_out, mesh_grad = call(
        mesh_body, [sds((nodes, width))] * 2, [VM] * 7,
        (attended, query_grad, og_near, wo_near, wq_near, mesh_near, gain_near), 1 << 28, 2 << 20, "mesh",
    )
    s1, s2, s3 = (shifted(s, "z", -k) for k, s in ((1, s1), (2, s2), (3, s3)))
    s1, s2, s3, parts, mesh_out = lax.optimization_barrier((s1, s2, s3, parts, mesh_out))
    (part,) = call(plane_body, [sds((share, width))], [VM], (parts,), 1 << 20, 1 << 20, "plane")
    part, s0 = lax.optimization_barrier((part, s0))
    near, far = call(
        pack_body, [four] * 2, [SM] + [VM] * 4, (core1, s0, s1, s2, s3), 0, 1 << 20, "pack"
    )
    far = swapped_far(far)
    near = shifted(near, "gc", 1)
    p1, p2, p3 = (shifted(part, "z", k) for k in (1, 2, 3))
    (spread,) = call(
        spread_body, [sds((plane, share, width))], [VM] * 4, (part, p1, p2, p3), 1 << 18, 1 << 20,
        "spread", [pltpu.VMEM((share, width), BF16), pltpu.SemaphoreType.DMA((plane,))], [HB],
    )
    mine = lax.all_to_all(spread, PLANE, 0, 0, tiled=True).reshape(2 * width, width)
    half = points // 2
    grid_scratch = [
        pltpu.VMEM((2 * block, width), BF16), pltpu.VMEM((half, width), BF16),
        pltpu.SemaphoreType.DMA((half // 256,)), pltpu.VMEM((half, width), BF16),
        pltpu.SemaphoreType.DMA((1,)),
    ]
    (grid_grad,) = call(
        grid_near_body, [sds((points, width))], [SM] * 2 + [VM] * 7 + [HB],
        (sub1, core1, near, s0, s1, s2, s3, rows_near, gain_g_near, grid_x),
        1 << 29, 3 << 20, "grid_near", grid_scratch, [HB],
    )
    mine, far, grid_grad = lax.optimization_barrier((mine, far, grid_grad))
    theirs = shifted(mine, "gc", 1)
    whole = sds((4, width, width), F32)
    wide = [pltpu.VMEM((2, width, width), F32), pltpu.SemaphoreType.DMA((8,))]
    grid_grad, weight_grads = call(
        grid_far_body, [sds((points, width)), whole], [SM] * 2 + [VM] * 8 + [HB] * 2,
        (sub1, core1, far, s0, s1, s2, s3, rows_near, gain_g_near, mine, grid_x, grid_grad),
        1 << 29, 5 << 20, "grid_far", grid_scratch + wide, [HB, HB], {11: 0},
    )
    (weight_grads,) = call(
        widen_body, [whole], [SM, VM, HB], (core1, theirs, weight_grads), 1 << 20, 3 << 20, "widen", wide,
        [HB], {2: 0},
    )
    return mesh_out, mesh_grad, grid_grad, weight_grads


def solution(mesh):
    split = Mesh(mesh.devices.reshape(4, 4, 2, mesh.shape["sub"]), ALL)
    rows = P(ALL, None)
    return jax.shard_map(
        shards,
        mesh=split,
        in_specs=(rows, rows, P(), P(), P(), P(), P(), P(), rows, rows, rows,
                  P(ALL, None, None, None), rows),
        out_specs=(rows, rows, rows, P()),
        check_vma=False,
    )
```

```python
import functools

import jax
import jax.numpy as jnp
from jax import lax
from jax.experimental import pallas as pl
from jax.experimental.pallas import tpu as pltpu
from jax.sharding import Mesh
from jax.sharding import PartitionSpec as P

SLAB = ("gx", "gy", "gc")
PLANE = ("gx", "gy")
ALL = ("gx", "gy", "gc", "z")

EPSILON = 1e-06
ABSENT = -1e30
F32 = jnp.float32
BF16 = jnp.bfloat16

VM = pl.BlockSpec(memory_space=pltpu.VMEM)
SM = pl.BlockSpec(memory_space=pltpu.SMEM)
HB = pl.BlockSpec(memory_space=pltpu.HBM)


def nn(a, b):
    return lax.dot_general(a, b, (((1,), (0,)), ((), ())), preferred_element_type=F32)


def nt(a, b):
    return lax.dot_general(a, b, (((1,), (1,)), ((), ())), preferred_element_type=F32)


def tn(a, b):
    return lax.dot_general(a, b, (((0,), (0,)), ((), ())), preferred_element_type=F32)


def inv_rms(wide):
    return lax.rsqrt(jnp.mean(wide * wide, axis=-1, keepdims=True) + EPSILON)


def norm_back(wide, factor, gain_row, upstream):
    scaled = gain_row * upstream
    inner = jnp.mean(wide * scaled, axis=-1, keepdims=True)
    return factor * scaled - wide * (factor * factor * factor * inner)


def call(body, outs, in_specs, args, flops, nbytes, name, scratch=(), out_specs=None, aliases=None):
    return pl.pallas_call(
        body,
        out_shape=outs,
        in_specs=in_specs,
        out_specs=out_specs or [VM] * len(outs),
        scratch_shapes=list(scratch),
        input_output_aliases=aliases or {},
        compiler_params=pltpu.CompilerParams(vmem_limit_bytes=16 << 20),
        cost_estimate=pl.CostEstimate(flops=flops, bytes_accessed=nbytes, transcendentals=0),
        name=name,
    )(*args)


def fetch(sources, targets, sems):
    copies = []
    for i, (source, target) in enumerate(zip(sources, targets)):
        copies.append(pltpu.make_async_copy(source, target, sems.at[i]))
        copies[-1].start()
    return copies


def held(*args):
    return [pltpu.VMEM(a.shape, a.dtype) for a in args] + [pltpu.SemaphoreType.DMA((len(args),))]


def early_body(core_ref, near, own, m1, m2, m3, wkv_ref, rows, keys, vals):
    block = near.shape[0]
    cap = block // 4
    width = rows.shape[1]
    near_at = pl.multiple_of(core_ref[0] * (2 * block), block)
    rows[block : block + cap] = own[0:cap]
    rows[pl.ds(near_at, cap), :] = near[0:cap]
    for k, mixed in enumerate((m1, m2, m3), 1):
        rows[block + k * cap : block + (k + 1) * cap] = mixed[0:cap]
        rows[pl.ds(near_at + k * cap, cap), :] = mixed[cap : 2 * cap]
    for first in (block, near_at):
        at = pl.ds(first, block)
        keys[at, :] = nn(rows[at, :], wkv_ref[:, :width]).astype(BF16)
        vals[at, :] = nn(rows[at, :], wkv_ref[:, width:]).astype(BF16)


def gather_body(sub_ref, core_ref, rows_hbm, gain_hbm, x_hbm, *refs):
    later = (len(refs) - 8) // 2
    later_hbm, refs = refs[:later], refs[later:]
    near_ref, far_ref, own_ref, rows_ref, gain_ref = refs[:5]
    later_refs = refs[5 : 5 + later]
    x_ref, sems, later_sems = refs[-3:]
    half = x_ref.shape[0] // 2
    cap = rows_ref.shape[3]
    core = core_ref[0]
    firsts = [pl.multiple_of((1 - core) * half, half), pl.multiple_of(core * half, half)]
    parts = [pl.ds(first, half) for first in firsts]
    copies = fetch(
        [rows_hbm, gain_hbm] + [x_hbm.at[p] for p in parts],
        [rows_ref, gain_ref] + [x_ref.at[p] for p in parts],
        sems,
    )
    copies[0].wait()
    copies[1].wait()
    me = sub_ref[0]
    eye = lax.broadcasted_iota(jnp.int32, (cap, cap), 0) == lax.broadcasted_iota(
        jnp.int32, (cap, cap), 1
    )
    gain = gain_ref[...]
    steps = (
        (2 - 2 * core, firsts[0], half, near_ref),
        (2 * core, firsts[1], half, far_ref),
        (1, 0, 2 * half, own_ref),
    )
    for step, (o, first, count, out_ref) in enumerate(steps):
        cols = []
        for k in range(4):
            s = lax.rem(me + k, 4)
            row = rows_ref[0, o, pl.ds(s, 1), :].astype(F32)
            cols.append(jnp.sum(jnp.where(eye, row, 0.0), axis=1, keepdims=True))
        col = jnp.concatenate(cols, axis=0).astype(jnp.int32) - first
        lanes = lax.broadcasted_iota(jnp.int32, (4 * cap, count), 1)
        onehot = jnp.where(lanes == col, 1.0, 0.0).astype(BF16)
        if step < 2:
            copies[2 + step].wait()
        if step == 1:
            later_copies = fetch(later_hbm, later_refs, later_sems)
        wide = nn(onehot, x_ref[pl.ds(first, count), :])
        out_ref[...] = (wide * inv_rms(wide) * gain).astype(BF16)
    for copy in later_copies:
        copy.wait()


def mesh_in_body(mesh_ref, gain_ref, wq_ref, wo_ref, og_ref, normed_ref, q_ref, ag_ref):
    wide = mesh_ref[...].astype(F32)
    normed = (wide * inv_rms(wide) * gain_ref[...]).astype(BF16)
    normed_ref[...] = normed
    q_ref[...] = (nn(normed, wq_ref[...]) * (128 ** -0.5)).astype(BF16)
    ag_ref[...] = nt(og_ref[...], wo_ref[...]).astype(BF16)


def slots_body(sub_ref, nbr_ref, valid_ref, bias_ref, wk_hbm, wv_hbm, dense_ref, wkv_ref,
               inv_ref, edge_ref, sems):
    width = wk_hbm.shape[0]
    copies = fetch(
        (wk_hbm, wv_hbm), (wkv_ref.at[:, pl.ds(0, width)], wkv_ref.at[:, pl.ds(width, width)]), sems
    )
    heads, nodes, slots = dense_ref.shape
    fan = nbr_ref.shape[1]
    slot = nbr_ref[...]
    slot = (slot & ~192) | (((sub_ref[0] - (slot >> 6)) & 3) << 6)
    high, low = slot >> 7, slot & 127
    blocks = lax.broadcasted_iota(jnp.int32, (8, fan), 0)
    lanes = lax.broadcasted_iota(jnp.int32, (128, fan), 0)
    edge = lax.broadcasted_iota(jnp.int32, (8, fan), 1).astype(F32) + 1.0
    for m in range(nodes):
        named = jnp.where(high[m : m + 1, :] == blocks, edge, 0.0).astype(BF16)
        places = jnp.where(low[m : m + 1, :] == lanes, 1.0, 0.0).astype(BF16)
        inv_ref[m * 8 : (m + 1) * 8, :] = nt(named, places)
    live = valid_ref[...] == 1
    for h in range(heads):
        edge_ref[h, :, 0:fan] = jnp.where(live, bias_ref[:, h * fan : (h + 1) * fan], ABSENT)
    for b in range(slots // 128):
        at = inv_ref[pl.ds(b, nodes, stride=8), :].astype(jnp.int32) - 1
        here = at >= 0
        at = jnp.maximum(at, 0)
        for h in range(heads):
            got = jnp.take_along_axis(edge_ref[h], at, axis=1, mode="promise_in_bounds")
            dense_ref[h, :, b * 128 : (b + 1) * 128] = jnp.where(here, got, ABSENT)
    for copy in copies:
        copy.wait()


def middle_body(core_ref, far, f1, f2, f3, q_ref, ag_ref, mn_ref, og_ref, bias_ref, wkv_ref,
                rows_in, keys_in, vals_in, send_ref, part_ref, att_ref, qg_ref, rows, keys, vals):
    width = q_ref.shape[1]
    heads = bias_ref.shape[0]
    core = core_ref[0]
    block = far.shape[0]
    cap = block // 4
    far_at = pl.multiple_of((1 - core) * (2 * block), block)
    rows[pl.ds(far_at, cap), :] = far[0:cap]
    for k, piece in enumerate((f1, f2, f3), 1):
        rows[pl.ds(far_at + k * cap, cap), :] = piece[...]
    at = pl.ds(far_at, block)
    keys[at, :] = nn(rows[at, :], wkv_ref[:, :width]).astype(BF16)
    vals[at, :] = nn(rows[at, :], wkv_ref[:, width:]).astype(BF16)
    for h in range(heads):
        at = slice(h * 128, (h + 1) * 128)
        q, ag = q_ref[:, at], ag_ref[:, at]
        kh, vh = keys[:, at], vals[:, at]
        scores = nt(q, kh) + bias_ref[h]
        peak = jnp.max(scores, axis=1, keepdims=True)
        terms = jnp.exp(scores - peak)
        probs = terms * (1.0 / jnp.sum(terms, axis=1, keepdims=True))
        probs_b = probs.astype(BF16)
        att_ref[:, at] = nn(probs_b, vh).astype(BF16)
        pg = nt(ag, vh)
        sg = (probs * (pg - jnp.sum(probs * pg, axis=1, keepdims=True))).astype(BF16)
        qg_ref[:, at] = (nn(sg, kh) * (128 ** -0.5)).astype(BF16)
        part_ref[:, at] = tn(sg, q).astype(BF16)
        part_ref[:, width + h * 128 : width + (h + 1) * 128] = tn(probs_b, ag).astype(BF16)
    half_grads(1 - core, send_ref, rows, part_ref, mn_ref, qg_ref, att_ref, og_ref)


def half_grads(half, out_ref, rows, part_ref, mn_ref, qg_ref, att_ref, og_ref):
    width = mn_ref.shape[1]
    first = half == 0
    left = jnp.where(first, mn_ref[...].astype(F32), att_ref[...].astype(F32)).astype(BF16)
    right = jnp.where(first, qg_ref[...].astype(F32), og_ref[...].astype(F32)).astype(BF16)
    columns = pl.ds(pl.multiple_of(half * width, width), width)
    out_ref[0:width] = tn(left, right).astype(BF16)
    out_ref[width : 2 * width] = tn(rows[...], part_ref[:, columns]).astype(BF16)


def keep_body(core_ref, rows, part_ref, mn_ref, qg_ref, att_ref, og_ref, keep_ref):
    half_grads(core_ref[0], keep_ref, rows, part_ref, mn_ref, qg_ref, att_ref, og_ref)


def back_body(part_ref, wkv_ref, s0, s1, s2, s3):
    cap = s0.shape[1]
    for o in range(3):
        rows = slice(o * 4 * cap, (o + 1) * 4 * cap)
        back = nt(part_ref[rows, :], wkv_ref[...]).astype(BF16)
        for k, piece in enumerate((s0, s1, s2, s3)):
            piece[o] = back[k * cap : (k + 1) * cap]


def mesh_body(att_ref, qg_ref, og_ref, wo_ref, wq_ref, mesh_ref, gain_ref, out_ref, grad_ref):
    wide = mesh_ref[...].astype(F32)
    out_ref[...] = (wide + nn(att_ref[...], wo_ref[...])).astype(BF16)
    upstream = nt(qg_ref[...], wq_ref[...])
    back = norm_back(wide, inv_rms(wide), gain_ref[...], upstream)
    grad_ref[...] = (og_ref[...].astype(F32) + back).astype(BF16)


def pack_body(core_ref, p0, p1, p2, p3, near_ref, far_ref):
    cap = p0.shape[1]
    near = core_ref[0] * 2
    for k, piece in enumerate((p0, p1, p2, p3)):
        near_ref[k * cap : (k + 1) * cap, :] = piece[near]
        far_ref[k * cap : (k + 1) * cap, :] = piece[2 - near]


def mix_body(own, near, m1, m2, m3):
    cap = m1.shape[0] // 2
    for k, mixed in enumerate((m1, m2, m3), 1):
        mixed[0:cap] = own[k * cap : (k + 1) * cap]
        mixed[cap : 2 * cap] = near[k * cap : (k + 1) * cap]


def split_body(block, f1, f2, f3):
    cap = f1.shape[0]
    for k, piece in enumerate((f1, f2, f3), 1):
        piece[...] = block[k * cap : (k + 1) * cap]


def grid_half(upper, sub_ref, outer, s0, s1, s2, s3, rows_ref, gain_ref, x_ref, out_hbm, got, done_ref,
              sems, ready):
    half = x_ref.shape[0]
    base = pl.multiple_of(upper * half, half)
    cap = rows_ref.shape[3]
    block = 4 * cap
    me = sub_ref[0]
    got[0:block] = outer[...]
    for k, piece in enumerate((s0, s1, s2, s3)):
        got[block + k * cap : block + (k + 1) * cap] = piece[1]
    gain = gain_ref[...]
    idx = []
    for o in (2 * upper, 1):
        for k in range(4):
            idx.append(rows_ref[0, o, pl.ds(lax.rem(me + k, 4), 1), :])
    idx = jnp.concatenate(idx, axis=1) - base
    tile = 256
    stores = []
    for t in range(half // tile):
        part = slice(t * tile, (t + 1) * tile)
        ids = lax.broadcasted_iota(jnp.int32, (tile, 2 * block), 0) + t * tile
        onehot = jnp.where(ids == idx, 1.0, 0.0).astype(BF16)
        upstream = nn(onehot, got[...])
        if t == 0:
            ready()
        wide = x_ref[part, :].astype(F32)
        done_ref[part, :] = norm_back(wide, inv_rms(wide), gain, upstream).astype(BF16)
        stores.append(
            pltpu.make_async_copy(
                done_ref.at[part], out_hbm.at[pl.ds(base + t * tile, tile)], sems.at[t]
            )
        )
        stores[-1].start()
    for store in stores:
        store.wait()


def grid_near_body(sub_ref, core_ref, near, s0, s1, s2, s3, rows_ref, gain_ref, x_hbm, out_hbm,
                   got, done_ref, done_sems, x_ref, sems):
    half = x_ref.shape[0]
    upper = 1 - core_ref[0]
    (copy,) = fetch([x_hbm.at[pl.ds(pl.multiple_of(upper * half, half), half)]], [x_ref], sems)
    grid_half(upper, sub_ref, near, s0, s1, s2, s3, rows_ref, gain_ref, x_ref, out_hbm, got, done_ref,
              done_sems, copy.wait)


def grid_far_body(sub_ref, core_ref, far, s0, s1, s2, s3, rows_ref, gain_ref, mine_ref, x_hbm, prior_hbm,
                  out_hbm, weights_hbm, got, done_ref, done_sems, x_ref, sems, wide, wide_sems):
    half = x_ref.shape[0]
    upper = core_ref[0]
    (copy,) = fetch([x_hbm.at[pl.ds(pl.multiple_of(upper * half, half), half)]], [x_ref], sems)
    copies = widen(upper, mine_ref, weights_hbm, wide, wide_sems)
    grid_half(upper, sub_ref, far, s0, s1, s2, s3, rows_ref, gain_ref, x_ref, out_hbm, got, done_ref,
              done_sems, copy.wait)
    for copy in copies:
        copy.wait()


def widen(half, half_ref, out_hbm, wide, sems):
    count, width, _ = wide.shape
    part = width // 4
    copies = []
    for i in range(4 * count):
        m, rows = i // 4, pl.ds((i % 4) * part, part)
        wide[m, rows, :] = half_ref[i * part : (i + 1) * part, :].astype(F32)
        copies.append(
            pltpu.make_async_copy(
                wide.at[m, rows], out_hbm.at[lax.select(half == 0, m, 3 - m), rows], sems.at[i]
            )
        )
        copies[-1].start()
    return copies


def widen_body(core_ref, half_ref, prior_hbm, out_hbm, wide, sems):
    for copy in widen(1 - core_ref[0], half_ref, out_hbm, wide, sems):
        copy.wait()


def pair_body(keep_ref, other_ref, out_hbm, sums, sems):
    part = sums.shape[0] // 4
    copies = []
    for i in range(4):
        at = slice(i * part, (i + 1) * part)
        sums[at, :] = (keep_ref[at, :].astype(F32) + other_ref[at, :].astype(F32)).astype(BF16)
        copies.append(pltpu.make_async_copy(sums.at[at], out_hbm.at[at], sems.at[i]))
        copies[-1].start()
    for copy in copies:
        copy.wait()


def plane_body(parts_ref, out_ref):
    total = parts_ref[0].astype(F32)
    for i in range(1, parts_ref.shape[0]):
        total = total + parts_ref[i].astype(F32)
    out_ref[...] = total.astype(BF16)


def spread_body(p0, p1, p2, p3, out_hbm, total, sems):
    even = p0[...].astype(F32) + p2[...].astype(F32)
    odd = p1[...].astype(F32) + p3[...].astype(F32)
    total[...] = (even + odd).astype(BF16)
    copies = []
    for i in range(out_hbm.shape[0]):
        copies.append(pltpu.make_async_copy(total, out_hbm.at[i], sems.at[i]))
        copies[-1].start()
    for copy in copies:
        copy.wait()


def shifted(block, axis, k):
    n = lax.axis_size(axis)
    return lax.ppermute(block, axis, [(i, (i + k) % n) for i in range(n)])


def swapped_far(block):
    n = lax.axis_size(SLAB)
    pairs = [(i, i + 1) for i in range(1, n - 1, 2)]
    return lax.ppermute(block, SLAB, pairs + [(j, i) for i, j in pairs])


def sds(shape, dtype=BF16):
    return jax.ShapeDtypeStruct(shape, dtype)


def shards(grid_x, mesh_h, gain_grid, gain_mesh, w_query, w_key, w_value, w_out, edge_bias,
           neighbours, valid, send_rows, out_grad):
    points, width = grid_x.shape
    nodes, fan = neighbours.shape
    cap = send_rows.shape[3]
    block = 4 * cap
    slots = 3 * block
    heads = edge_bias.shape[1] // fan
    sub1 = lax.axis_index("z").astype(jnp.int32).reshape(1)
    core1 = lax.axis_index("gc").astype(jnp.int32).reshape(1)
    gain_g, gain_m = gain_grid.reshape(1, width), gain_mesh.reshape(1, width)
    (grid_x, mesh_h, out_grad, send_rows, w_key, w_value, w_query, w_out, gain_g, gain_m, edge_bias,
     neighbours, valid) = (
        pltpu.with_memory_space_constraint(a, pltpu.HBM)
        for a in (grid_x, mesh_h, out_grad, send_rows, w_key, w_value, w_query, w_out, gain_g, gain_m,
                  edge_bias, neighbours, valid)
    )

    one, two, four = sds((cap, width)), sds((2 * cap, width)), sds((block, width))
    later = (mesh_h, gain_m, w_query, w_out, out_grad, neighbours, valid, edge_bias)
    near, far, own, rows_near, gain_g_near, *later = call(
        gather_body,
        [four] * 3 + [sds(a.shape, a.dtype) for a in (send_rows, gain_g, *later)],
        [SM, SM] + [HB] * (3 + len(later)),
        (sub1, core1, send_rows, gain_g, grid_x, *later), 1 << 30, 5 << 20, "gather_rows",
        [pltpu.VMEM((points, width), BF16), pltpu.SemaphoreType.DMA((4,)),
         pltpu.SemaphoreType.DMA((len(later),))],
    )
    mesh_near, gain_near, wq_near, wo_near, og_near, nbr_near, valid_near, bias_near = later
    far = swapped_far(far)
    near = shifted(near, "gc", 1)
    mixed = call(mix_body, [two] * 3, [VM] * 2, (own, near), 0, 1 << 20, "mix")
    mixed = [shifted(m, "z", k) for k, m in enumerate(mixed, 1)]
    mesh_normed, queries, att_grad = call(
        mesh_in_body, [sds((nodes, width))] * 3, [VM] * 5,
        (mesh_near, gain_near, wq_near, wo_near, og_near), 1 << 28, 2 << 20, "mesh_in",
    )
    far, mixed[0], queries = lax.optimization_barrier((far, mixed[0], queries))
    outer = call(split_body, [one] * 3, [VM], (far,), 0, 1 << 19, "split")
    outer = [shifted(f, "z", k) for k, f in enumerate(outer, 1)]
    sub2, far = lax.optimization_barrier((sub1, far))
    dense, weights_near = call(
        slots_body, [sds((heads, nodes, slots), F32), sds((width, 2 * width))],
        [SM] + [VM] * 3 + [HB] * 2,
        (sub2, nbr_near, valid_near, bias_near, w_key, w_value), 1 << 30, 8 << 20, "slots",
        [pltpu.VMEM((nodes * 8, 128), F32), pltpu.VMEM((heads, nodes, 128), F32),
         pltpu.SemaphoreType.DMA((2,))],
    )
    table = sds((slots, width))
    rows, keys, vals = call(
        early_body, [table] * 3, [SM] + [VM] * 6, (core1, near, own, *mixed, weights_near),
        1 << 29, 3 << 20, "early",
    )
    send, part_grads, attended, query_grad, rows, *_ = call(
        middle_body,
        [sds((2 * width, width)), sds((slots, 2 * width))] + [sds((nodes, width))] * 2 + [table] * 3,
        [SM] + [VM] * 13,
        (core1, far, *outer, queries, att_grad, mesh_normed, og_near, dense, weights_near, rows, keys, vals),
        3 << 30, 8 << 20, "middle", (), None, {11: 4, 12: 5, 13: 6},
    )

    other = shifted(send, "gc", 1)
    (keep,) = call(
        keep_body, [sds((2 * width, width))], [SM] + [VM] * 6,
        (core1, rows, part_grads, mesh_normed, query_grad, attended, og_near), 1 << 29, 3 << 20, "keep",
    )
    s0, s1, s2, s3 = call(
        back_body, [sds((3, cap, width))] * 4, [VM] * 2, (part_grads, weights_near),
        1 << 30, 3 << 20, "back",
    )
    other, s1, keep = lax.optimization_barrier((other, s1, keep))
    (own,) = call(
        pair_body, [sds((2 * width, width))], [VM] * 2, (keep, other), 1 << 20, 3 << 20, "pair",
        [pltpu.VMEM((2 * width, width), BF16), pltpu.SemaphoreType.DMA((4,))], [HB],
    )
    plane = lax.axis_size(PLANE)
    share = 2 * width // plane
    parts = lax.all_to_all(own.reshape(plane, share, width), PLANE, 0, 0, tiled=True)

    attended, own = lax.optimization_barrier((attended, own))
    mesh_out, mesh_grad = call(
        mesh_body, [sds((nodes, width))] * 2, [VM] * 7,
        (attended, query_grad, og_near, wo_near, wq_near, mesh_near, gain_near), 1 << 28, 2 << 20, "mesh",
    )
    s1, s2, s3 = (shifted(s, "z", -k) for k, s in ((1, s1), (2, s2), (3, s3)))
    s1, s2, s3, parts, mesh_out = lax.optimization_barrier((s1, s2, s3, parts, mesh_out))
    (part,) = call(plane_body, [sds((share, width))], [VM], (parts,), 1 << 20, 1 << 20, "plane")
    part, s0 = lax.optimization_barrier((part, s0))
    near, far = call(
        pack_body, [four] * 2, [SM] + [VM] * 4, (core1, s0, s1, s2, s3), 0, 1 << 20, "pack"
    )
    far = swapped_far(far)
    near = shifted(near, "gc", 1)
    p1, p2, p3 = (shifted(part, "z", k) for k in (1, 2, 3))
    (spread,) = call(
        spread_body, [sds((plane, share, width))], [VM] * 4, (part, p1, p2, p3), 1 << 18, 1 << 20,
        "spread", [pltpu.VMEM((share, width), BF16), pltpu.SemaphoreType.DMA((plane,))], [HB],
    )
    mine = lax.all_to_all(spread, PLANE, 0, 0, tiled=True).reshape(2 * width, width)
    half = points // 2
    grid_scratch = [
        pltpu.VMEM((2 * block, width), BF16), pltpu.VMEM((half, width), BF16),
        pltpu.SemaphoreType.DMA((half // 256,)), pltpu.VMEM((half, width), BF16),
        pltpu.SemaphoreType.DMA((1,)),
    ]
    (grid_grad,) = call(
        grid_near_body, [sds((points, width))], [SM] * 2 + [VM] * 7 + [HB],
        (sub1, core1, near, s0, s1, s2, s3, rows_near, gain_g_near, grid_x),
        1 << 29, 3 << 20, "grid_near", grid_scratch, [HB],
    )
    mine, far, grid_grad = lax.optimization_barrier((mine, far, grid_grad))
    theirs = shifted(mine, "gc", 1)
    whole = sds((4, width, width), F32)
    wide = [pltpu.VMEM((2, width, width), F32), pltpu.SemaphoreType.DMA((8,))]
    grid_grad, weight_grads = call(
        grid_far_body, [sds((points, width)), whole], [SM] * 2 + [VM] * 8 + [HB] * 2,
        (sub1, core1, far, s0, s1, s2, s3, rows_near, gain_g_near, mine, grid_x, grid_grad),
        1 << 29, 5 << 20, "grid_far", grid_scratch + wide, [HB, HB], {11: 0},
    )
    (weight_grads,) = call(
        widen_body, [whole], [SM, VM, HB], (core1, theirs, weight_grads), 1 << 20, 3 << 20, "widen", wide,
        [HB], {2: 0},
    )
    return mesh_out, mesh_grad, grid_grad, weight_grads


def solution(mesh):
    split = Mesh(mesh.devices.reshape(4, 4, 2, mesh.shape["sub"]), ALL)
    rows = P(ALL, None)
    return jax.shard_map(
        shards,
        mesh=split,
        in_specs=(rows, rows, P(), P(), P(), P(), P(), P(), rows, rows, rows,
                  P(ALL, None, None, None), rows),
        out_specs=(rows, rows, rows, P()),
        check_vma=False,
    )
```

```python
import functools

import jax
import jax.numpy as jnp
from jax import lax
from jax.experimental import pallas as pl
from jax.experimental.pallas import tpu as pltpu
from jax.sharding import Mesh
from jax.sharding import PartitionSpec as P

SLAB = ("gx", "gy", "gc")
PLANE = ("gx", "gy")
ALL = ("gx", "gy", "gc", "z")

EPSILON = 1e-06
ABSENT = -1e30
F32 = jnp.float32
BF16 = jnp.bfloat16

VM = pl.BlockSpec(memory_space=pltpu.VMEM)
SM = pl.BlockSpec(memory_space=pltpu.SMEM)
HB = pl.BlockSpec(memory_space=pltpu.HBM)


def nn(a, b):
    return lax.dot_general(a, b, (((1,), (0,)), ((), ())), preferred_element_type=F32)


def nt(a, b):
    return lax.dot_general(a, b, (((1,), (1,)), ((), ())), preferred_element_type=F32)


def tn(a, b):
    return lax.dot_general(a, b, (((0,), (0,)), ((), ())), preferred_element_type=F32)


def inv_rms(wide):
    return lax.rsqrt(jnp.mean(wide * wide, axis=-1, keepdims=True) + EPSILON)


def norm_back(wide, factor, gain_row, upstream):
    scaled = gain_row * upstream
    inner = jnp.mean(wide * scaled, axis=-1, keepdims=True)
    return factor * scaled - wide * (factor * factor * factor * inner)


def call(body, outs, in_specs, args, flops, nbytes, name, scratch=(), out_specs=None, aliases=None):
    return pl.pallas_call(
        body,
        out_shape=outs,
        in_specs=in_specs,
        out_specs=out_specs or [VM] * len(outs),
        scratch_shapes=list(scratch),
        input_output_aliases=aliases or {},
        compiler_params=pltpu.CompilerParams(vmem_limit_bytes=16 << 20),
        cost_estimate=pl.CostEstimate(flops=flops, bytes_accessed=nbytes, transcendentals=0),
        name=name,
    )(*args)


def fetch(sources, targets, sems):
    copies = []
    for i, (source, target) in enumerate(zip(sources, targets)):
        copies.append(pltpu.make_async_copy(source, target, sems.at[i]))
        copies[-1].start()
    return copies


def held(*args):
    return [pltpu.VMEM(a.shape, a.dtype) for a in args] + [pltpu.SemaphoreType.DMA((len(args),))]


def early_body(core_ref, near, own, m1, m2, m3, wkv_ref, q_ref, ag_ref, bias_ref, rows, keys, vals,
               scores_ref, pg_ref):
    block = near.shape[0]
    cap = block // 4
    width = rows.shape[1]
    near_at = pl.multiple_of(core_ref[0] * (2 * block), block)
    rows[block : block + cap] = own[0:cap]
    rows[pl.ds(near_at, cap), :] = near[0:cap]
    for k, mixed in enumerate((m1, m2, m3), 1):
        rows[block + k * cap : block + (k + 1) * cap] = mixed[0:cap]
        rows[pl.ds(near_at + k * cap, cap), :] = mixed[cap : 2 * cap]
    for first in (block, near_at):
        columns(pl.ds(first, block), wkv_ref, q_ref, ag_ref, bias_ref, rows, keys, vals, scores_ref, pg_ref)


def columns(at, wkv_ref, q_ref, ag_ref, bias_ref, rows, keys, vals, scores_ref, pg_ref):
    width = rows.shape[1]
    keys_at = nn(rows[at, :], wkv_ref[:, :width]).astype(BF16)
    vals_at = nn(rows[at, :], wkv_ref[:, width:]).astype(BF16)
    keys[at, :] = keys_at
    vals[at, :] = vals_at
    for h in range(bias_ref.shape[0]):
        head = slice(h * 128, (h + 1) * 128)
        scores_ref[h, :, at] = nt(q_ref[:, head], keys_at[:, head]) + bias_ref[h, :, at]
        pg_ref[h, :, at] = nt(ag_ref[:, head], vals_at[:, head])


def gather_body(sub_ref, core_ref, rows_hbm, gain_hbm, x_hbm, *refs):
    later = (len(refs) - 8) // 2
    later_hbm, refs = refs[:later], refs[later:]
    near_ref, far_ref, own_ref, rows_ref, gain_ref = refs[:5]
    later_refs = refs[5 : 5 + later]
    x_ref, sems, later_sems = refs[-3:]
    half = x_ref.shape[0] // 2
    cap = rows_ref.shape[3]
    core = core_ref[0]
    firsts = [pl.multiple_of((1 - core) * half, half), pl.multiple_of(core * half, half)]
    parts = [pl.ds(first, half) for first in firsts]
    copies = fetch(
        [rows_hbm, gain_hbm] + [x_hbm.at[p] for p in parts],
        [rows_ref, gain_ref] + [x_ref.at[p] for p in parts],
        sems,
    )
    copies[0].wait()
    copies[1].wait()
    me = sub_ref[0]
    eye = lax.broadcasted_iota(jnp.int32, (cap, cap), 0) == lax.broadcasted_iota(
        jnp.int32, (cap, cap), 1
    )
    gain = gain_ref[...]
    steps = (
        (2 - 2 * core, firsts[0], half, near_ref),
        (2 * core, firsts[1], half, far_ref),
        (1, 0, 2 * half, own_ref),
    )
    for step, (o, first, count, out_ref) in enumerate(steps):
        cols = []
        for k in range(4):
            s = lax.rem(me + k, 4)
            row = rows_ref[0, o, pl.ds(s, 1), :].astype(F32)
            cols.append(jnp.sum(jnp.where(eye, row, 0.0), axis=1, keepdims=True))
        col = jnp.concatenate(cols, axis=0).astype(jnp.int32) - first
        lanes = lax.broadcasted_iota(jnp.int32, (4 * cap, count), 1)
        onehot = jnp.where(lanes == col, 1.0, 0.0).astype(BF16)
        if step < 2:
            copies[2 + step].wait()
        if step == 1:
            later_copies = fetch(later_hbm, later_refs, later_sems)
        wide = nn(onehot, x_ref[pl.ds(first, count), :])
        out_ref[...] = (wide * inv_rms(wide) * gain).astype(BF16)
    for copy in later_copies:
        copy.wait()


def mesh_in_body(mesh_ref, gain_ref, wq_ref, wo_ref, og_ref, normed_ref, q_ref, ag_ref):
    wide = mesh_ref[...].astype(F32)
    normed = (wide * inv_rms(wide) * gain_ref[...]).astype(BF16)
    normed_ref[...] = normed
    q_ref[...] = (nn(normed, wq_ref[...]) * (128 ** -0.5)).astype(BF16)
    ag_ref[...] = nt(og_ref[...], wo_ref[...]).astype(BF16)


def slots_body(sub_ref, nbr_ref, valid_ref, bias_ref, wk_hbm, wv_hbm, dense_ref, wkv_ref,
               inv_ref, edge_ref, sems):
    width = wk_hbm.shape[0]
    copies = fetch(
        (wk_hbm, wv_hbm), (wkv_ref.at[:, pl.ds(0, width)], wkv_ref.at[:, pl.ds(width, width)]), sems
    )
    heads, nodes, slots = dense_ref.shape
    fan = nbr_ref.shape[1]
    slot = nbr_ref[...]
    slot = (slot & ~192) | (((sub_ref[0] - (slot >> 6)) & 3) << 6)
    high, low = slot >> 7, slot & 127
    blocks = lax.broadcasted_iota(jnp.int32, (8, fan), 0)
    lanes = lax.broadcasted_iota(jnp.int32, (128, fan), 0)
    edge = lax.broadcasted_iota(jnp.int32, (8, fan), 1).astype(F32) + 1.0
    for m in range(nodes):
        named = jnp.where(high[m : m + 1, :] == blocks, edge, 0.0).astype(BF16)
        places = jnp.where(low[m : m + 1, :] == lanes, 1.0, 0.0).astype(BF16)
        inv_ref[m * 8 : (m + 1) * 8, :] = nt(named, places)
    live = valid_ref[...] == 1
    for h in range(heads):
        edge_ref[h, :, 0:fan] = jnp.where(live, bias_ref[:, h * fan : (h + 1) * fan], ABSENT)
    for b in range(slots // 128):
        at = inv_ref[pl.ds(b, nodes, stride=8), :].astype(jnp.int32) - 1
        here = at >= 0
        at = jnp.maximum(at, 0)
        for h in range(heads):
            got = jnp.take_along_axis(edge_ref[h], at, axis=1, mode="promise_in_bounds")
            dense_ref[h, :, b * 128 : (b + 1) * 128] = jnp.where(here, got, ABSENT)
    for copy in copies:
        copy.wait()


def middle_body(core_ref, far, f1, f2, f3, q_ref, ag_ref, mn_ref, og_ref, bias_ref, wkv_ref,
                rows_in, keys_in, vals_in, scores_in, pg_in,
                send_ref, part_ref, att_ref, qg_ref, rows, keys, vals, scores_ref, pg_ref):
    width = q_ref.shape[1]
    heads = bias_ref.shape[0]
    core = core_ref[0]
    block = far.shape[0]
    cap = block // 4
    far_at = pl.multiple_of((1 - core) * (2 * block), block)
    rows[pl.ds(far_at, cap), :] = far[0:cap]
    for k, piece in enumerate((f1, f2, f3), 1):
        rows[pl.ds(far_at + k * cap, cap), :] = piece[...]
    columns(
        pl.ds(far_at, block), wkv_ref, q_ref, ag_ref, bias_ref, rows, keys, vals, scores_ref, pg_ref
    )
    for h in range(heads):
        at = slice(h * 128, (h + 1) * 128)
        q, ag = q_ref[:, at], ag_ref[:, at]
        kh, vh = keys[:, at], vals[:, at]
        scores = scores_ref[h]
        peak = jnp.max(scores, axis=1, keepdims=True)
        terms = jnp.exp(scores - peak)
        probs = terms * (1.0 / jnp.sum(terms, axis=1, keepdims=True))
        probs_b = probs.astype(BF16)
        att_ref[:, at] = nn(probs_b, vh).astype(BF16)
        pg = pg_ref[h]
        sg = (probs * (pg - jnp.sum(probs * pg, axis=1, keepdims=True))).astype(BF16)
        qg_ref[:, at] = (nn(sg, kh) * (128 ** -0.5)).astype(BF16)
        part_ref[:, at] = tn(sg, q).astype(BF16)
        part_ref[:, width + h * 128 : width + (h + 1) * 128] = tn(probs_b, ag).astype(BF16)
    half_grads(1 - core, send_ref, rows, part_ref, mn_ref, qg_ref, att_ref, og_ref)


def half_grads(half, out_ref, rows, part_ref, mn_ref, qg_ref, att_ref, og_ref):
    width = mn_ref.shape[1]
    first = half == 0
    left = jnp.where(first, mn_ref[...].astype(F32), att_ref[...].astype(F32)).astype(BF16)
    right = jnp.where(first, qg_ref[...].astype(F32), og_ref[...].astype(F32)).astype(BF16)
    columns = pl.ds(pl.multiple_of(half * width, width), width)
    out_ref[0:width] = tn(left, right).astype(BF16)
    out_ref[width : 2 * width] = tn(rows[...], part_ref[:, columns]).astype(BF16)


def keep_body(core_ref, rows, part_ref, mn_ref, qg_ref, att_ref, og_ref, keep_ref):
    half_grads(core_ref[0], keep_ref, rows, part_ref, mn_ref, qg_ref, att_ref, og_ref)


def back_body(part_ref, wkv_ref, s0, s1, s2, s3):
    cap = s0.shape[1]
    for o in range(3):
        rows = slice(o * 4 * cap, (o + 1) * 4 * cap)
        back = nt(part_ref[rows, :], wkv_ref[...]).astype(BF16)
        for k, piece in enumerate((s0, s1, s2, s3)):
            piece[o] = back[k * cap : (k + 1) * cap]


def mesh_body(att_ref, qg_ref, og_ref, wo_ref, wq_ref, mesh_ref, gain_ref, out_ref, grad_ref):
    wide = mesh_ref[...].astype(F32)
    out_ref[...] = (wide + nn(att_ref[...], wo_ref[...])).astype(BF16)
    upstream = nt(qg_ref[...], wq_ref[...])
    back = norm_back(wide, inv_rms(wide), gain_ref[...], upstream)
    grad_ref[...] = (og_ref[...].astype(F32) + back).astype(BF16)


def pack_body(core_ref, p0, p1, p2, p3, near_ref, far_ref):
    cap = p0.shape[1]
    near = core_ref[0] * 2
    for k, piece in enumerate((p0, p1, p2, p3)):
        near_ref[k * cap : (k + 1) * cap, :] = piece[near]
        far_ref[k * cap : (k + 1) * cap, :] = piece[2 - near]


def mix_body(own, near, m1, m2, m3):
    cap = m1.shape[0] // 2
    for k, mixed in enumerate((m1, m2, m3), 1):
        mixed[0:cap] = own[k * cap : (k + 1) * cap]
        mixed[cap : 2 * cap] = near[k * cap : (k + 1) * cap]


def split_body(block, f1, f2, f3):
    cap = f1.shape[0]
    for k, piece in enumerate((f1, f2, f3), 1):
        piece[...] = block[k * cap : (k + 1) * cap]


def grid_half(upper, sub_ref, outer, s0, s1, s2, s3, rows_ref, gain_ref, x_ref, out_hbm, got, done_ref,
              sems, ready):
    half = x_ref.shape[0]
    base = pl.multiple_of(upper * half, half)
    cap = rows_ref.shape[3]
    block = 4 * cap
    me = sub_ref[0]
    got[0:block] = outer[...]
    for k, piece in enumerate((s0, s1, s2, s3)):
        got[block + k * cap : block + (k + 1) * cap] = piece[1]
    gain = gain_ref[...]
    idx = []
    for o in (2 * upper, 1):
        for k in range(4):
            idx.append(rows_ref[0, o, pl.ds(lax.rem(me + k, 4), 1), :])
    idx = jnp.concatenate(idx, axis=1) - base
    tile = 256
    stores = []
    for t in range(half // tile):
        part = slice(t * tile, (t + 1) * tile)
        ids = lax.broadcasted_iota(jnp.int32, (tile, 2 * block), 0) + t * tile
        onehot = jnp.where(ids == idx, 1.0, 0.0).astype(BF16)
        upstream = nn(onehot, got[...])
        if t == 0:
            ready()
        wide = x_ref[part, :].astype(F32)
        done_ref[part, :] = norm_back(wide, inv_rms(wide), gain, upstream).astype(BF16)
        stores.append(
            pltpu.make_async_copy(
                done_ref.at[part], out_hbm.at[pl.ds(base + t * tile, tile)], sems.at[t]
            )
        )
        stores[-1].start()
    for store in stores:
        store.wait()


def grid_near_body(sub_ref, core_ref, near, s0, s1, s2, s3, rows_ref, gain_ref, x_hbm, out_hbm,
                   got, done_ref, done_sems, x_ref, sems):
    half = x_ref.shape[0]
    upper = 1 - core_ref[0]
    (copy,) = fetch([x_hbm.at[pl.ds(pl.multiple_of(upper * half, half), half)]], [x_ref], sems)
    grid_half(upper, sub_ref, near, s0, s1, s2, s3, rows_ref, gain_ref, x_ref, out_hbm, got, done_ref,
              done_sems, copy.wait)


def grid_far_body(sub_ref, core_ref, far, s0, s1, s2, s3, rows_ref, gain_ref, mine_ref, x_hbm, prior_hbm,
                  out_hbm, weights_hbm, got, done_ref, done_sems, x_ref, sems, wide, wide_sems):
    half = x_ref.shape[0]
    upper = core_ref[0]
    (copy,) = fetch([x_hbm.at[pl.ds(pl.multiple_of(upper * half, half), half)]], [x_ref], sems)
    copies = widen(upper, mine_ref, weights_hbm, wide, wide_sems)
    grid_half(upper, sub_ref, far, s0, s1, s2, s3, rows_ref, gain_ref, x_ref, out_hbm, got, done_ref,
              done_sems, copy.wait)
    for copy in copies:
        copy.wait()


def widen(half, half_ref, out_hbm, wide, sems):
    count, width, _ = wide.shape
    part = width // 4
    copies = []
    for i in range(4 * count):
        m, rows = i // 4, pl.ds((i % 4) * part, part)
        wide[m, rows, :] = half_ref[i * part : (i + 1) * part, :].astype(F32)
        copies.append(
            pltpu.make_async_copy(
                wide.at[m, rows], out_hbm.at[lax.select(half == 0, m, 3 - m), rows], sems.at[i]
            )
        )
        copies[-1].start()
    return copies


def widen_body(core_ref, half_ref, prior_hbm, out_hbm, wide, sems):
    for copy in widen(1 - core_ref[0], half_ref, out_hbm, wide, sems):
        copy.wait()


def pair_body(keep_ref, other_ref, out_hbm, sums, sems):
    part = sums.shape[0] // 4
    copies = []
    for i in range(4):
        at = slice(i * part, (i + 1) * part)
        sums[at, :] = (keep_ref[at, :].astype(F32) + other_ref[at, :].astype(F32)).astype(BF16)
        copies.append(pltpu.make_async_copy(sums.at[at], out_hbm.at[at], sems.at[i]))
        copies[-1].start()
    for copy in copies:
        copy.wait()


def plane_body(parts_ref, out_ref):
    total = parts_ref[0].astype(F32)
    for i in range(1, parts_ref.shape[0]):
        total = total + parts_ref[i].astype(F32)
    out_ref[...] = total.astype(BF16)


def spread_body(p0, p1, p2, p3, out_hbm, total, sems):
    even = p0[...].astype(F32) + p2[...].astype(F32)
    odd = p1[...].astype(F32) + p3[...].astype(F32)
    total[...] = (even + odd).astype(BF16)
    copies = []
    for i in range(out_hbm.shape[0]):
        copies.append(pltpu.make_async_copy(total, out_hbm.at[i], sems.at[i]))
        copies[-1].start()
    for copy in copies:
        copy.wait()


def shifted(block, axis, k):
    n = lax.axis_size(axis)
    return lax.ppermute(block, axis, [(i, (i + k) % n) for i in range(n)])


def swapped_far(block):
    n = lax.axis_size(SLAB)
    pairs = [(i, i + 1) for i in range(1, n - 1, 2)]
    return lax.ppermute(block, SLAB, pairs + [(j, i) for i, j in pairs])


def sds(shape, dtype=BF16):
    return jax.ShapeDtypeStruct(shape, dtype)


def shards(grid_x, mesh_h, gain_grid, gain_mesh, w_query, w_key, w_value, w_out, edge_bias,
           neighbours, valid, send_rows, out_grad):
    points, width = grid_x.shape
    nodes, fan = neighbours.shape
    cap = send_rows.shape[3]
    block = 4 * cap
    slots = 3 * block
    heads = edge_bias.shape[1] // fan
    sub1 = lax.axis_index("z").astype(jnp.int32).reshape(1)
    core1 = lax.axis_index("gc").astype(jnp.int32).reshape(1)
    gain_g, gain_m = gain_grid.reshape(1, width), gain_mesh.reshape(1, width)
    (grid_x, mesh_h, out_grad, send_rows, w_key, w_value, w_query, w_out, gain_g, gain_m, edge_bias,
     neighbours, valid) = (
        pltpu.with_memory_space_constraint(a, pltpu.HBM)
        for a in (grid_x, mesh_h, out_grad, send_rows, w_key, w_value, w_query, w_out, gain_g, gain_m,
                  edge_bias, neighbours, valid)
    )

    one, two, four = sds((cap, width)), sds((2 * cap, width)), sds((block, width))
    later = (mesh_h, gain_m, w_query, w_out, out_grad, neighbours, valid, edge_bias)
    near, far, own, rows_near, gain_g_near, *later = call(
        gather_body,
        [four] * 3 + [sds(a.shape, a.dtype) for a in (send_rows, gain_g, *later)],
        [SM, SM] + [HB] * (3 + len(later)),
        (sub1, core1, send_rows, gain_g, grid_x, *later), 1 << 30, 5 << 20, "gather_rows",
        [pltpu.VMEM((points, width), BF16), pltpu.SemaphoreType.DMA((4,)),
         pltpu.SemaphoreType.DMA((len(later),))],
    )
    mesh_near, gain_near, wq_near, wo_near, og_near, nbr_near, valid_near, bias_near = later
    far = swapped_far(far)
    near = shifted(near, "gc", 1)
    mixed = call(mix_body, [two] * 3, [VM] * 2, (own, near), 0, 1 << 20, "mix")
    mixed = [shifted(m, "z", k) for k, m in enumerate(mixed, 1)]
    mesh_normed, queries, att_grad = call(
        mesh_in_body, [sds((nodes, width))] * 3, [VM] * 5,
        (mesh_near, gain_near, wq_near, wo_near, og_near), 1 << 28, 2 << 20, "mesh_in",
    )
    far, mixed[0], queries = lax.optimization_barrier((far, mixed[0], queries))
    outer = call(split_body, [one] * 3, [VM], (far,), 0, 1 << 19, "split")
    outer = [shifted(f, "z", k) for k, f in enumerate(outer, 1)]
    sub2, far = lax.optimization_barrier((sub1, far))
    dense, weights_near = call(
        slots_body, [sds((heads, nodes, slots), F32), sds((width, 2 * width))],
        [SM] + [VM] * 3 + [HB] * 2,
        (sub2, nbr_near, valid_near, bias_near, w_key, w_value), 1 << 30, 8 << 20, "slots",
        [pltpu.VMEM((nodes * 8, 128), F32), pltpu.VMEM((heads, nodes, 128), F32),
         pltpu.SemaphoreType.DMA((2,))],
    )
    table = sds((slots, width))
    map_of = sds((heads, nodes, slots), F32)
    rows, keys, vals, scores, prob_grads = call(
        early_body, [table] * 3 + [map_of] * 2, [SM] + [VM] * 9,
        (core1, near, own, *mixed, weights_near, queries, att_grad, dense),
        1 << 29, 3 << 20, "early",
    )
    send, part_grads, attended, query_grad, rows, *_ = call(
        middle_body,
        [sds((2 * width, width)), sds((slots, 2 * width))] + [sds((nodes, width))] * 2 + [table] * 3
        + [map_of] * 2,
        [SM] + [VM] * 15,
        (core1, far, *outer, queries, att_grad, mesh_normed, og_near, dense, weights_near, rows, keys, vals,
         scores, prob_grads),
        3 << 30, 8 << 20, "middle", (), None, {11: 4, 12: 5, 13: 6, 14: 7, 15: 8},
    )

    other = shifted(send, "gc", 1)
    (keep,) = call(
        keep_body, [sds((2 * width, width))], [SM] + [VM] * 6,
        (core1, rows, part_grads, mesh_normed, query_grad, attended, og_near), 1 << 29, 3 << 20, "keep",
    )
    s0, s1, s2, s3 = call(
        back_body, [sds((3, cap, width))] * 4, [VM] * 2, (part_grads, weights_near),
        1 << 30, 3 << 20, "back",
    )
    other, s1, keep = lax.optimization_barrier((other, s1, keep))
    (own,) = call(
        pair_body, [sds((2 * width, width))], [VM] * 2, (keep, other), 1 << 20, 3 << 20, "pair",
        [pltpu.VMEM((2 * width, width), BF16), pltpu.SemaphoreType.DMA((4,))], [HB],
    )
    plane = lax.axis_size(PLANE)
    share = 2 * width // plane
    parts = lax.all_to_all(own.reshape(plane, share, width), PLANE, 0, 0, tiled=True)

    attended, own = lax.optimization_barrier((attended, own))
    mesh_out, mesh_grad = call(
        mesh_body, [sds((nodes, width))] * 2, [VM] * 7,
        (attended, query_grad, og_near, wo_near, wq_near, mesh_near, gain_near), 1 << 28, 2 << 20, "mesh",
    )
    s1, s2, s3 = (shifted(s, "z", -k) for k, s in ((1, s1), (2, s2), (3, s3)))
    s1, s2, s3, parts, mesh_out = lax.optimization_barrier((s1, s2, s3, parts, mesh_out))
    (part,) = call(plane_body, [sds((share, width))], [VM], (parts,), 1 << 20, 1 << 20, "plane")
    part, s0 = lax.optimization_barrier((part, s0))
    near, far = call(
        pack_body, [four] * 2, [SM] + [VM] * 4, (core1, s0, s1, s2, s3), 0, 1 << 20, "pack"
    )
    far = swapped_far(far)
    near = shifted(near, "gc", 1)
    p1, p2, p3 = (shifted(part, "z", k) for k in (1, 2, 3))
    (spread,) = call(
        spread_body, [sds((plane, share, width))], [VM] * 4, (part, p1, p2, p3), 1 << 18, 1 << 20,
        "spread", [pltpu.VMEM((share, width), BF16), pltpu.SemaphoreType.DMA((plane,))], [HB],
    )
    mine = lax.all_to_all(spread, PLANE, 0, 0, tiled=True).reshape(2 * width, width)
    half = points // 2
    grid_scratch = [
        pltpu.VMEM((2 * block, width), BF16), pltpu.VMEM((half, width), BF16),
        pltpu.SemaphoreType.DMA((half // 256,)), pltpu.VMEM((half, width), BF16),
        pltpu.SemaphoreType.DMA((1,)),
    ]
    (grid_grad,) = call(
        grid_near_body, [sds((points, width))], [SM] * 2 + [VM] * 7 + [HB],
        (sub1, core1, near, s0, s1, s2, s3, rows_near, gain_g_near, grid_x),
        1 << 29, 3 << 20, "grid_near", grid_scratch, [HB],
    )
    mine, far, grid_grad = lax.optimization_barrier((mine, far, grid_grad))
    theirs = shifted(mine, "gc", 1)
    whole = sds((4, width, width), F32)
    wide = [pltpu.VMEM((2, width, width), F32), pltpu.SemaphoreType.DMA((8,))]
    grid_grad, weight_grads = call(
        grid_far_body, [sds((points, width)), whole], [SM] * 2 + [VM] * 8 + [HB] * 2,
        (sub1, core1, far, s0, s1, s2, s3, rows_near, gain_g_near, mine, grid_x, grid_grad),
        1 << 29, 5 << 20, "grid_far", grid_scratch + wide, [HB, HB], {11: 0},
    )
    (weight_grads,) = call(
        widen_body, [whole], [SM, VM, HB], (core1, theirs, weight_grads), 1 << 20, 3 << 20, "widen", wide,
        [HB], {2: 0},
    )
    return mesh_out, mesh_grad, grid_grad, weight_grads


def solution(mesh):
    split = Mesh(mesh.devices.reshape(4, 4, 2, mesh.shape["sub"]), ALL)
    rows = P(ALL, None)
    return jax.shard_map(
        shards,
        mesh=split,
        in_specs=(rows, rows, P(), P(), P(), P(), P(), P(), rows, rows, rows,
                  P(ALL, None, None, None), rows),
        out_specs=(rows, rows, rows, P()),
        check_vma=False,
    )
```
